256 devices in a mesh: seq: 32 (over z, x_hi, core), tp: 8 (over x_lo, y).
Axes of the slice: x: 4 (x_hi: 2, x_lo: 2; x = x_hi * 2 + x_lo), y: 4, z: 8, core: 2. Of those that a mesh axis runs over, the one named last changes fastest.
Arguments:
- hidden_in: bfloat16 [8192, 2560], P('seq'), may hold values from -6 to 6
- norm_gain: float32 [2560], replicated, may hold values from 0.25 to 1.75
- w_query: bfloat16 [2560, 2560], P(None, 'tp'), may hold values from -0.3131453 to 0.3131453
- w_key: bfloat16 [2560, 640], P(None, 'tp'), may hold values from -0.125 to 0.125
- w_value: bfloat16 [2560, 640], P(None, 'tp'), may hold values from -0.125 to 0.125
- w_out: bfloat16 [2560, 2560], P('tp'), may hold values from -0.625 to 0.625
- prefix_keys: bfloat16 [8192, 640], P('seq', 'tp'), may hold values from -6 to 6
- prefix_values: bfloat16 [8192, 640], P('seq', 'tp'), may hold values from -6 to 6
- lengths: int32 [4], replicated, may hold values from 1 to 6144, 8192 in all
- groups: int32 [4], replicated, may hold values from 0 to 1
Outputs:
- hidden_out: bfloat16 [8192, 2560], P('seq', 'tp')
- suffix_keys: bfloat16 [8192, 640], P('seq', 'tp')
- suffix_values: bfloat16 [8192, 640], P('seq', 'tp')
The draws below stay inside these ranges and needn't reach their ends.
Inputs may be any that keep to these rules, and one draw needn't show every extreme that they name: The 4 lengths sum to 8192, and the largest is exactly 6144.
All inputs are finite; a program needn't handle non-finite values.
Results may differ from the reference program's by a relative error of at most 0.02.
The reference program's roundings to bfloat16 on the way count: a program that leaves them out, or rounds other values in their place, can miss the bound.
Values may be sent and summed in bfloat16 or wider, within the bound.
No kernel may reach another device: no remote copies, remote signals or barrier semaphores. Data moves between devices by JAX's collectives and lax.ppermute only.
A program may use at most 192 MiB of HBM per device.

```python
import math
import jax
import jax.numpy as jnp
import numpy as np
from jax import lax

D = 2560
HEADS = 32
KV_HEADS = 8
HEAD_DIM = 80
GROUPS = 2
REQS = 4
SUFFIX = 8192
PREFIX = 8192
PRE_LEN = 4096
N_TP = 8


stream_scale = 0.1


def draw_hidden_in(key, part):
    noise_key = jax.random.fold_in(key, 101)
    values = jnp.clip(jax.random.normal(noise_key, (SUFFIX, D), jnp.float32), -6.0, 6.0)
    return (values * stream_scale).astype(jnp.bfloat16)


def draw_w_query(key, part):
    columns = HEADS * HEAD_DIM
    noise_key = jax.random.fold_in(key, 201)
    spread = D ** (-0.5)
    values = jnp.clip(jax.random.normal(noise_key, (D, columns), jnp.float32), -4.0, 4.0) * spread
    return values.astype(jnp.bfloat16)


def draw_prefix_keys(key, part):
    columns = KV_HEADS * HEAD_DIM
    noise_key = jax.random.fold_in(key, 301)
    values = jnp.clip(jax.random.normal(noise_key, (PREFIX, columns), jnp.float32), -6.0, 6.0)
    return values.astype(jnp.bfloat16)


def place_ends(values, rng, smallest, high):
    shape = values.shape
    index_at = [jax.random.randint(jax.random.fold_in(rng, axis), (), 0, shape[axis]) for axis in range(len(shape))]
    values = values.at[tuple(index_at)].set(smallest)
    longest = shape.index(max(shape))
    index_at[longest] = (index_at[longest] + 1) % shape[longest]
    return values.at[tuple(index_at)].set(high)


def shard_levels(key, dims, shards, low, largest):
    factor_of, own = 1.0, jax.random.fold_in(key, 6)
    for axis_at, shards_of in shards:
        steps = jnp.exp(jax.random.uniform(jax.random.fold_in(own, axis_at), (shards_of,), jnp.float32, low / len(shards), largest / len(shards)))
        factor_of = factor_of * jnp.repeat(steps, dims[axis_at] // shards_of).reshape([-1 if axis == axis_at else 1 for axis in range(len(dims))])
    return factor_of


def split_up(amount, total, most, skew):
    portions = [(1 << 20) // math.isqrt(standing ** skew) + 1 for standing in range(2, amount + 1)]
    rest, counts = total - most - (amount - 1), [1] * (amount - 1)
    while rest > 0:
        movable = [i for i in range(amount - 1) if counts[i] < most]
        whole, remaining = sum([portions[i] for i in movable]), rest
        for i in movable:
            more = min(most - counts[i], max(1, remaining * portions[i] // whole), rest)
            counts[i] = counts[i] + more
            rest = rest - more
    return np.array([most] + counts)


def uneven_parts(stream_key, amount, total, reach, skew):
    if amount == 2:
        one = jax.random.randint(stream_key, (), max(1, total - reach), min(reach, total - 1) + 1)
        return jnp.stack([one, total - one])
    tallies = jnp.asarray(split_up(amount, total, reach, skew), jnp.int32)
    pairs = (amount - 1) // 2
    giver, taker = tallies[1:1 + 2 * pairs:2], tallies[2:2 + 2 * pairs:2]
    room = jnp.minimum(giver - 1, reach - taker)
    passed = jax.random.randint(jax.random.fold_in(stream_key, 1), (pairs,), 0, 1 << 20) % (room + 1)
    tallies = tallies.at[1:1 + 2 * pairs:2].set(giver - passed).at[2:2 + 2 * pairs:2].set(taker + passed)
    return tallies[jax.random.permutation(jax.random.fold_in(stream_key, 2), amount)]


def bell_draw(own_key, dims, width, most, pieces=(), kind=jnp.bfloat16):
    level = shard_levels(own_key, dims, pieces, -0.22, 0.18) if pieces else 1.0
    array = jax.random.normal(own_key, dims, jnp.float32) * width * level
    return jnp.minimum(jnp.maximum(array, -most), most).astype(kind)


def setup_inputs(seed: int = 0) -> dict:
    splits = jax.random.split(jax.random.key(seed), 11)
    return {
        "hidden_in": draw_hidden_in(jax.random.fold_in(splits[10], 71), 0),
        "norm_gain": jnp.clip(1.0 + 0.15 * jax.random.normal(splits[1], (D,), jnp.float32), 0.25, 1.75),
        "w_query": draw_w_query(jax.random.fold_in(splits[10], 71), 0),
        "w_key": bell_draw(splits[3], (D, KV_HEADS * HEAD_DIM), D ** -0.5, 0.125, ((1, 8),)),
        "w_value": bell_draw(splits[4], (D, KV_HEADS * HEAD_DIM), D ** -0.5, 0.125, ((1, 8),)),
        "w_out": bell_draw(splits[5], (HEADS * HEAD_DIM, D), HEAD_DIM ** -0.5, 0.625, ((0, 8),)),
        "prefix_keys": draw_prefix_keys(jax.random.fold_in(splits[10], 71), 0),
        "prefix_values": bell_draw(splits[7], (PREFIX, KV_HEADS * HEAD_DIM), 1.0, 6.0, ((0, 32), (1, 8))),
        "lengths": uneven_parts(splits[8], REQS, SUFFIX, SUFFIX * 3 // 4, 2).astype(jnp.int32),
        "groups": place_ends(jax.random.randint(splits[9], (REQS,), 0, GROUPS), jax.random.fold_in(splits[9], 1), 0, GROUPS - 1).astype(jnp.int32),
    }


def rotate_pairs(vectors, positions):
    half_dim = vectors.shape[-1] // 2
    exponent = jnp.arange(half_dim, dtype=jnp.float32) / half_dim
    frequency = jnp.power(jnp.float32(1000000.0), -exponent)
    angles = positions.astype(jnp.float32)[:, None] * frequency[None, :]
    cosine = jnp.cos(angles)[:, None, :]
    sinusoid = jnp.sin(angles)[:, None, :]
    first_half = vectors[..., :half_dim]
    second_half = vectors[..., half_dim:]
    return jnp.concatenate([first_half * cosine - second_half * sinusoid, second_half * cosine + first_half * sinusoid], axis=-1)

def token_facts(lengths, groups, token_index):
    request_ends = jnp.cumsum(lengths).astype(jnp.int32)
    request = lax.optimization_barrier(jnp.sum((token_index[:, None] >= request_ends[None, :]).astype(jnp.int32), axis=1)).astype(jnp.int32)
    onehot = (request[:, None] == jnp.arange(lengths.shape[0], dtype=jnp.int32)[None, :]).astype(jnp.int32)
    request_start = lax.optimization_barrier(jnp.sum(onehot * (request_ends - lengths)[None, :], axis=1)).astype(jnp.int32)
    group_of = lax.optimization_barrier(jnp.sum(onehot * groups[None, :], axis=1)).astype(jnp.int32)
    return (request, request_start, group_of)

def project_tokens(hidden_in, norm_gain, w_query, w_key, w_value, positions):
    wide_values = hidden_in.astype(jnp.float32)
    mean_square = lax.optimization_barrier(jnp.mean(wide_values * wide_values, axis=-1, keepdims=True))
    normed = (wide_values * lax.rsqrt(mean_square + 1e-05) * norm_gain.astype(jnp.float32)).astype(jnp.bfloat16)
    row_count = hidden_in.shape[0]
    queries = jnp.dot(normed, w_query, preferred_element_type=jnp.float32).reshape(row_count, -1, HEAD_DIM)
    key_rows = jnp.dot(normed, w_key, preferred_element_type=jnp.float32).reshape(row_count, -1, HEAD_DIM)
    value_rows = jnp.dot(normed, w_value, preferred_element_type=jnp.float32).reshape(row_count, -1, HEAD_DIM)
    queries = (rotate_pairs(queries, positions) * HEAD_DIM ** (-0.5)).astype(jnp.bfloat16)
    key_rows = rotate_pairs(key_rows, positions).astype(jnp.bfloat16)
    return (queries, key_rows, value_rows.astype(jnp.bfloat16))

def reference(hidden_in, norm_gain, w_query, w_key, w_value, w_out, prefix_keys, prefix_values, lengths, groups):
    token_index = jnp.arange(SUFFIX, dtype=jnp.int32)
    request, request_start, group_of = token_facts(lengths, groups, token_index)
    positions = PRE_LEN + token_index - request_start
    queries, key_rows, value_rows = project_tokens(hidden_in, norm_gain, w_query, w_key, w_value, positions)
    group_ratio = HEADS // KV_HEADS
    all_keys = jnp.concatenate([prefix_keys.reshape(PREFIX, KV_HEADS, HEAD_DIM), key_rows], axis=0).astype(jnp.float32)
    all_values = jnp.concatenate([prefix_values.reshape(PREFIX, KV_HEADS, HEAD_DIM), value_rows], axis=0).astype(jnp.float32)
    prefix_group = (jnp.arange(PREFIX, dtype=jnp.int32) // PRE_LEN).astype(jnp.int32)
    block_rows = 128

    def one_block(block_id):
        first_row = (block_id * block_rows).astype(jnp.int32)
        rows_here = lax.dynamic_slice_in_dim(token_index, first_row, block_rows)
        request_here = lax.dynamic_slice_in_dim(request, first_row, block_rows)
        group_here = lax.dynamic_slice_in_dim(group_of, first_row, block_rows)
        q_block = lax.dynamic_slice_in_dim(queries, first_row, block_rows, 0)
        q_block = q_block.reshape(block_rows, KV_HEADS, group_ratio, HEAD_DIM).astype(jnp.float32)
        prefix_ok = group_here[:, None] == prefix_group[None, :]
        suffix_ok = (request_here[:, None] == request[None, :]) & (token_index[None, :] <= rows_here[:, None])
        allowed = jnp.concatenate([prefix_ok, suffix_ok], axis=1)[:, None, None, :]
        scores = jnp.einsum('bkrd,nkd->bkrn', q_block, all_keys)
        scores = jnp.where(allowed, scores, -1e+30)
        row_max = lax.optimization_barrier(jnp.max(scores, axis=-1, keepdims=True))
        weights = jnp.where(allowed, jnp.exp(scores - row_max), 0.0)
        row_sum = lax.optimization_barrier(jnp.sum(weights, axis=-1))
        rounded = lax.optimization_barrier(weights.astype(jnp.bfloat16))
        weighted = jnp.einsum('bkrn,nkd->bkrd', rounded.astype(jnp.float32), all_values)
        return (weighted / row_sum[..., None]).reshape(block_rows, HEADS * HEAD_DIM).astype(jnp.bfloat16)
    attended = lax.map(one_block, jnp.arange(SUFFIX // block_rows, dtype=jnp.int32)).reshape(SUFFIX, HEADS * HEAD_DIM)
    head_block = HEADS * HEAD_DIM // N_TP
    projected = jnp.zeros((SUFFIX, D), jnp.float32)
    for group_index in range(N_TP):
        partial_term = jnp.dot(attended[:, group_index * head_block:(group_index + 1) * head_block], w_out[group_index * head_block:(group_index + 1) * head_block, :], preferred_element_type=jnp.float32)
        rounded_term = lax.optimization_barrier(partial_term.astype(jnp.bfloat16))
        projected = projected + rounded_term.astype(jnp.float32)
    hidden_out = (projected + hidden_in.astype(jnp.float32)).astype(jnp.bfloat16)
    return (hidden_out, key_rows.reshape(SUFFIX, KV_HEADS * HEAD_DIM), value_rows.reshape(SUFFIX, KV_HEADS * HEAD_DIM))
```

```python
import jax
import jax.numpy as jnp
from jax import lax
from jax.experimental import pallas as pl
from jax.experimental.pallas import tpu as pltpu
from jax.sharding import PartitionSpec as P

HEAD_DIM = 80
GROUPS = 2
REQS = 4
BLK = 256
COLS = 4
ZDIM = 8
HPD = 4
QROWS = HPD * HEAD_DIM
PROWS = QROWS + 16
NEG = -1e30
SHIFTS = (1, -1, 2, -2, 3, -3, 4)


def rotate_t(vectors, cosine, sinusoid):
    half = HEAD_DIM // 2
    first = vectors[:, :half]
    second = vectors[:, half:]
    return jnp.concatenate(
        [first * cosine - second * sinusoid, second * cosine + first * sinusoid], axis=1
    )


def attention_body(lens, grps, sidx, *refs):
    pre = refs[:ZDIM]
    suf = refs[ZDIM : 2 * ZDIM]
    q_own, q_x, q_c, keep, send, kscr, vscr, qscr, acc, mscr = refs[2 * ZDIM :]
    s = sidx[0]
    z = s // COLS
    r = s % COLS
    half = ZDIM * PRE_BLOCKS_PER_Z // GROUPS

    def place(ref, pos):
        kt = jnp.concatenate(
            [ref[0:HEAD_DIM, :], jnp.zeros((128 - HEAD_DIM, BLK), jnp.bfloat16)], axis=0
        )
        kscr[pl.ds(pl.multiple_of(pos * BLK, BLK), BLK), :] = kt.T
        vscr[pos, 0:HEAD_DIM, :] = ref[HEAD_DIM : 2 * HEAD_DIM, :]
        vscr[pos, HEAD_DIM:96, :] = jnp.ones((96 - HEAD_DIM, BLK), jnp.bfloat16)

    for n, d in enumerate((0,) + SHIFTS):
        source = (z - d + ZDIM) % ZDIM
        place(pre[n], source)
        place(suf[n], ZDIM + source)
    for k, (ref, off) in enumerate(((q_own, 0), (q_c, 0), (q_x, 0), (q_c, QROWS))):
        for h in range(HPD):
            lo = off + h * HEAD_DIM
            qscr[k, 0:HEAD_DIM, h * BLK : (h + 1) * BLK] = ref[lo : lo + HEAD_DIM, :]
        qscr[k, HEAD_DIM:128, :] = jnp.zeros((128 - HEAD_DIM, HPD * BLK), jnp.bfloat16)

    ends = []
    total = 0
    for i in range(REQS):
        total = total + lens[i]
        ends.append(total)

    def start_of(p):
        st = jnp.int32(0)
        for i in range(REQS - 1):
            st = jnp.where(p >= ends[i], ends[i], st)
        return st

    def process(k, row0, blk0, nblk, mask):
        for h in range(HPD):
            cols = slice(h * BLK, (h + 1) * BLK)
            sc = jnp.dot(
                kscr[pl.ds(pl.multiple_of(row0, BLK), nblk * BLK), :],
                qscr[k, :, cols],
                preferred_element_type=jnp.float32,
            )
            if mask is not None:
                sc = jnp.where(mask, sc, NEG)
            m_old = mscr[h]
            m_new = jnp.maximum(m_old, jnp.max(sc, axis=0, keepdims=True))
            w = jnp.exp(sc - m_new).astype(jnp.bfloat16)
            pv = jnp.dot(vscr[blk0], w[0:BLK], preferred_element_type=jnp.float32)
            for j in range(1, nblk):
                pv = pv + jnp.dot(
                    vscr[blk0 + j],
                    w[j * BLK : (j + 1) * BLK],
                    preferred_element_type=jnp.float32,
                )
            acc[h] = acc[h] * jnp.exp(m_old - m_new) + pv
            mscr[h] = m_new

    def one_tokens(k, carry):
        b = r ^ k
        tok0 = (z * COLS + b) * BLK
        tvec = tok0 + lax.broadcasted_iota(jnp.int32, (1, BLK), 1)
        svec = jnp.zeros((1, BLK), jnp.int32)
        gvec = jnp.zeros((1, BLK), jnp.int32) + grps[0]
        for i in range(REQS - 1):
            svec = jnp.where(tvec >= ends[i], ends[i], svec)
            gvec = jnp.where(tvec >= ends[i], grps[i + 1], gvec)
        acc[...] = jnp.zeros_like(acc)
        mscr[...] = jnp.full(mscr.shape, NEG, jnp.float32)
        for g in range(GROUPS):
            seen = jnp.bool_(False)
            pure = jnp.bool_(True)
            begin = jnp.int32(0)
            for i in range(REQS):
                inside = (begin < tok0 + BLK) & (ends[i] > tok0)
                same = grps[i] == g
                seen = seen | (inside & same)
                pure = pure & (jnp.logical_not(inside) | same)
                begin = ends[i]

            @pl.when(seen & pure)
            def _():
                @pl.loop(0, 2)
                def _(c):
                    blk = g * half + c * (half // 2)
                    process(k, blk * BLK, blk, half // 2, None)

            @pl.when(seen & jnp.logical_not(pure))
            def _():
                @pl.loop(0, half)
                def _(c):
                    blk = g * half + c
                    process(k, blk * BLK, blk, 1, jnp.broadcast_to(gvec == g, (BLK, BLK)))

        first = start_of(tok0)
        last = start_of(tok0 + BLK - 1)
        gap = jnp.maximum(first - (BLK - 1) - r * BLK, 0)
        low = (gap + COLS * BLK - 1) // (COLS * BLK)
        high = z + (b >= r).astype(jnp.int32)

        def suffix_step(jz, c):
            key0 = (jz * COLS + r) * BLK
            full = (key0 < tok0) & (last <= key0)

            @pl.when(full)
            def _():
                process(k, (ZDIM + jz) * BLK, ZDIM + jz, 1, None)

            @pl.when(jnp.logical_not(full))
            def _():
                kvec = key0 + lax.broadcasted_iota(jnp.int32, (BLK, BLK), 0)
                process(k, (ZDIM + jz) * BLK, ZDIM + jz, 1, (kvec <= tvec) & (kvec >= svec))

            return c

        lax.fori_loop(low, high, suffix_step, 0)

        extra = jnp.zeros((16, BLK), jnp.float32)
        rows = lax.broadcasted_iota(jnp.int32, (16, BLK), 0)
        outs = []
        for h in range(HPD):
            total_w = acc[h, HEAD_DIM : HEAD_DIM + 1, :]
            outs.append((acc[h, 0:HEAD_DIM, :] / total_w).astype(jnp.bfloat16))
            lse = mscr[h] + jnp.log(total_w)
            for j in range(3):
                part = lse.astype(jnp.bfloat16).astype(jnp.float32)
                extra = jnp.where(rows == 3 * h + j, part, extra)
                lse = lse - part
        whole = jnp.concatenate(outs + [extra.astype(jnp.bfloat16)], axis=0)

        @pl.when(k % 2 == 0)
        def _():
            keep[k // 2] = whole

        @pl.when(k % 2 == 1)
        def _():
            send[k // 2] = whole

        return carry

    lax.fori_loop(0, COLS, one_tokens, 0)


PRE_BLOCKS_PER_Z = 1


def merged(one, two):
    e1 = one[QROWS:PROWS, :].astype(jnp.float32)
    e2 = two[QROWS:PROWS, :].astype(jnp.float32)
    outs = []
    lses = []
    for h in range(HPD):
        l1 = e1[3 * h : 3 * h + 1] + e1[3 * h + 1 : 3 * h + 2] + e1[3 * h + 2 : 3 * h + 3]
        l2 = e2[3 * h : 3 * h + 1] + e2[3 * h + 1 : 3 * h + 2] + e2[3 * h + 2 : 3 * h + 3]
        top = jnp.maximum(l1, l2)
        w1 = jnp.exp(l1 - top)
        w2 = jnp.exp(l2 - top)
        tot = w1 + w2
        rows = slice(h * HEAD_DIM, (h + 1) * HEAD_DIM)
        o1 = one[rows, :].astype(jnp.float32)
        o2 = two[rows, :].astype(jnp.float32)
        outs.append((o1 * (w1 / tot) + o2 * (w2 / tot)).astype(jnp.bfloat16))
        lses.append(top + jnp.log(tot))
    return outs, lses


def merge_core_body(keep, recv, own, far):
    for k, dst in ((0, own), (1, far)):
        outs, lses = merged(keep[k], recv[k])
        extra = jnp.zeros((16, BLK), jnp.float32)
        rows = lax.broadcasted_iota(jnp.int32, (16, BLK), 0)
        for h in range(HPD):
            lse = lses[h]
            for j in range(3):
                part = lse.astype(jnp.bfloat16).astype(jnp.float32)
                extra = jnp.where(rows == 3 * h + j, part, extra)
                lse = lse - part
        dst[...] = jnp.concatenate(outs + [extra.astype(jnp.bfloat16)], axis=0)


def project_out_body(own, recv, w_t, out):
    outs, unused = merged(own[...], recv[...])
    attended = jnp.concatenate(outs, axis=0)
    out[...] = jnp.dot(w_t[...], attended, preferred_element_type=jnp.float32).astype(
        jnp.bfloat16
    )


def final_body(parts, residual, out):
    total = residual[...].astype(jnp.float32)
    acc = parts[0].astype(jnp.float32)
    for i in range(1, parts.shape[0]):
        acc = acc + parts[i].astype(jnp.float32)
    out[...] = (acc + total).astype(jnp.bfloat16)


def shape_of(*dims):
    return jax.ShapeDtypeStruct(dims, jnp.bfloat16)


VMEM_SPEC = pl.BlockSpec(memory_space=pltpu.VMEM)
SMEM_SPEC = pl.BlockSpec(memory_space=pltpu.SMEM)
PARAMS = pltpu.CompilerParams(vmem_limit_bytes=48 * 1024 * 1024)


def per_device(
    hidden_in,
    norm_gain,
    w_query,
    w_key,
    w_value,
    w_out,
    prefix_keys,
    prefix_values,
    lengths,
    groups,
):
    seq = lax.axis_index("seq")
    zperm = [[(i, (i + COLS * d) % 32) for i in range(32)] for d in SHIFTS]
    pre_own = jnp.concatenate([prefix_keys.T, prefix_values.T], axis=0)
    pre = [pre_own] + [lax.ppermute(pre_own, "seq", p) for p in zperm]

    tok_rows = hidden_in.shape[0]
    token_index = seq * tok_rows + jnp.arange(tok_rows, dtype=jnp.int32)
    ends = jnp.cumsum(lengths)
    start = jnp.zeros((tok_rows,), jnp.int32)
    for i in range(REQS - 1):
        start = jnp.where(token_index >= ends[i], ends[i], start)
    positions = 4096 + token_index - start
    half_dim = HEAD_DIM // 2
    frequency = jnp.power(
        jnp.float32(1000000.0), -jnp.arange(half_dim, dtype=jnp.float32) / half_dim
    )
    angles = frequency[:, None] * positions.astype(jnp.float32)[None, :]
    cosine = jnp.cos(angles)[None]
    sinusoid = jnp.sin(angles)[None]
    wide = hidden_in.astype(jnp.float32)
    mean_square = jnp.mean(wide * wide, axis=-1, keepdims=True)
    normed = (wide * lax.rsqrt(mean_square + 1e-05) * norm_gain).astype(jnp.bfloat16)

    def proj(w):
        return lax.dot_general(
            w, normed, (((0,), (1,)), ((), ())), preferred_element_type=jnp.float32
        )

    key_t = rotate_t(proj(w_key)[None], cosine, sinusoid)[0].astype(jnp.bfloat16)
    value_t = proj(w_value).astype(jnp.bfloat16)
    q_t = rotate_t(proj(w_query).reshape(HPD, HEAD_DIM, tok_rows), cosine, sinusoid)
    q_t = (q_t * HEAD_DIM ** (-0.5)).astype(jnp.bfloat16).reshape(QROWS, tok_rows)

    suf_own = jnp.concatenate([key_t, value_t], axis=0)
    q_x = lax.ppermute(q_t, "seq", [(i, i ^ 2) for i in range(32)])
    q_c = lax.ppermute(
        jnp.concatenate([q_t, q_x], axis=0), "seq", [(i, i ^ 1) for i in range(32)]
    )
    suf = [suf_own] + [lax.ppermute(suf_own, "seq", p) for p in zperm]

    keep, send = pl.pallas_call(
        attention_body,
        out_shape=(shape_of(2, PROWS, BLK), shape_of(2, PROWS, BLK)),
        in_specs=[SMEM_SPEC] * 3 + [VMEM_SPEC] * (2 * ZDIM + 3),
        out_specs=(VMEM_SPEC, VMEM_SPEC),
        scratch_shapes=[
            pltpu.VMEM((2 * ZDIM * BLK, 128), jnp.bfloat16),
            pltpu.VMEM((2 * ZDIM, 96, BLK), jnp.bfloat16),
            pltpu.VMEM((COLS, 128, HPD * BLK), jnp.bfloat16),
            pltpu.VMEM((HPD, 96, BLK), jnp.float32),
            pltpu.VMEM((HPD, 1, BLK), jnp.float32),
        ],
        compiler_params=PARAMS,
        name="attention",
    )(lengths, groups, seq.astype(jnp.int32).reshape(1), *pre, *suf, q_t, q_x, q_c)

    core_recv = lax.ppermute(send, "seq", [(i, i ^ 1) for i in range(32)])
    own, far = pl.pallas_call(
        merge_core_body,
        out_shape=(shape_of(PROWS, BLK), shape_of(PROWS, BLK)),
        in_specs=[VMEM_SPEC] * 2,
        out_specs=(VMEM_SPEC, VMEM_SPEC),
        compiler_params=PARAMS,
        name="merge_core",
    )(keep, core_recv)
    x_recv = lax.ppermute(far, "seq", [(i, i ^ 2) for i in range(32)])
    width = w_out.shape[1]
    projected = pl.pallas_call(
        project_out_body,
        out_shape=shape_of(width, BLK),
        in_specs=[VMEM_SPEC] * 3,
        out_specs=VMEM_SPEC,
        compiler_params=PARAMS,
        name="project_out",
    )(own, x_recv, w_out.T)
    tp = lax.axis_size("tp")
    columns = width // tp
    parts = lax.all_to_all(
        projected.reshape(tp, columns, BLK), "tp", split_axis=0, concat_axis=0, tiled=True
    )
    residual = lax.dynamic_slice_in_dim(
        hidden_in, lax.axis_index("tp") * columns, columns, 1
    ).T
    hidden_t = pl.pallas_call(
        final_body,
        out_shape=shape_of(columns, BLK),
        in_specs=[VMEM_SPEC] * 2,
        out_specs=VMEM_SPEC,
        compiler_params=PARAMS,
        name="final_sum",
    )(parts, residual)
    return (hidden_t.T, key_t.T, value_t.T)


def solution(mesh):
    return jax.shard_map(
        per_device,
        mesh=mesh,
        in_specs=(
            P("seq", None),
            P(),
            P(None, "tp"),
            P(None, "tp"),
            P(None, "tp"),
            P("tp", None),
            P("seq", "tp"),
            P("seq", "tp"),
            P(),
            P(),
        ),
        out_specs=(P("seq", "tp"), P("seq", "tp"), P("seq", "tp")),
        check_vma=False,
    )
```

```python
import jax
import jax.numpy as jnp
from jax import lax
from jax.experimental import pallas as pl
from jax.experimental.pallas import tpu as pltpu
from jax.sharding import PartitionSpec as P

HEAD_DIM = 80
GROUPS = 2
REQS = 4
BLK = 256
COLS = 4
ZDIM = 8
HPD = 4
QROWS = HPD * HEAD_DIM
PROWS = QROWS + 16
NEG = -1e30
LIMIT = 1e30
AHEAD = 4
TILES = COLS * HPD


def request_ends(lens):
    ends = []
    total = 0
    for i in range(REQS):
        total = total + lens[i]
        ends.append(total)
    return ends


def start_of(p, ends):
    st = jnp.int32(0)
    for i in range(REQS - 1):
        st = jnp.where(p >= ends[i], ends[i], st)
    return st


def token_vectors(z, r, ends, grps):
    tvecs, svecs, gvecs = [], [], []
    for k in range(COLS):
        tok0 = (z * COLS + (r ^ k)) * BLK
        tvec = tok0 + lax.broadcasted_iota(jnp.int32, (1, BLK), 1)
        svec = jnp.zeros((1, BLK), jnp.int32)
        gvec = jnp.zeros((1, BLK), jnp.int32) + grps[0]
        for i in range(REQS - 1):
            svec = jnp.where(tvec >= ends[i], ends[i], svec)
            gvec = jnp.where(tvec >= ends[i], grps[i + 1], gvec)
        tvecs.append(tvec)
        svecs.append(svec)
        gvecs.append(gvec)
    return tvecs, svecs, gvecs


def place(src, kscr, vscr):
    for n in range(ZDIM):
        kt = jnp.concatenate(
            [src[n, 0:HEAD_DIM, :], jnp.zeros((128 - HEAD_DIM, BLK), jnp.bfloat16)], axis=0
        )
        kscr[n * BLK : (n + 1) * BLK, :] = kt.T
        vscr[n, 0:HEAD_DIM, :] = src[n, HEAD_DIM : 2 * HEAD_DIM, :]
        vscr[n, HEAD_DIM:96, :] = jnp.ones((96 - HEAD_DIM, BLK), jnp.bfloat16)


def key_rows(kscr, blk):
    return kscr[pl.ds(pl.multiple_of(blk * BLK, BLK), BLK), :]


def add_block(blk, masks, kscr, vscr, qs, acc, m):
    scores, weights = {}, {}
    for i in range(TILES + AHEAD + 1):
        if i < TILES:
            scores[i] = jnp.dot(key_rows(kscr, blk), qs[i], preferred_element_type=jnp.float32)
        j = i - AHEAD
        if 0 <= j < TILES:
            sc = scores.pop(j)
            if masks is not None:
                sc = jnp.where(masks[j // HPD], sc, NEG)
            weights[j] = jnp.exp(sc - m[j]).astype(jnp.bfloat16)
        n = j - 1
        if 0 <= n < TILES:
            acc[n] = acc[n] + jnp.dot(
                vscr[blk], weights.pop(n), preferred_element_type=jnp.float32
            )


def add_block_exact(tile, blk, mask, kscr, vscr, qs, acc, m):
    sc = jnp.dot(key_rows(kscr, blk), qs[tile], preferred_element_type=jnp.float32)
    sc = jnp.where(mask, sc, NEG)
    m_old = m[tile]
    m_new = jnp.maximum(m_old, jnp.max(sc, axis=0, keepdims=True))
    w = jnp.exp(sc - m_new).astype(jnp.bfloat16)
    acc[tile] = acc[tile] * jnp.exp(m_old - m_new) + jnp.dot(
        vscr[blk], w, preferred_element_type=jnp.float32
    )
    m[tile] = m_new


def overflowed(acc):
    top = acc[0, HEAD_DIM : HEAD_DIM + 1, :]
    for t in range(1, TILES):
        top = jnp.maximum(top, acc[t, HEAD_DIM : HEAD_DIM + 1, :])
    return jnp.logical_not(jnp.max(top) < LIMIT)


def prefix_body(lens, grps, sidx, pre, q_own, q_x, q_c, qs, acc, m, kscr, vscr):
    s = sidx[0]
    z = s // COLS
    r = s % COLS
    half = ZDIM // GROUPS
    place(pre, kscr, vscr)
    for k, (ref, off) in enumerate(((q_own, 0), (q_c, 0), (q_x, 0), (q_c, QROWS))):
        for h in range(HPD):
            lo = off + h * HEAD_DIM
            qs[k * HPD + h, 0:HEAD_DIM, :] = ref[lo : lo + HEAD_DIM, :]
            qs[k * HPD + h, HEAD_DIM:128, :] = jnp.zeros((128 - HEAD_DIM, BLK), jnp.bfloat16)
    ends = request_ends(lens)
    gvecs = token_vectors(z, r, ends, grps)[2]
    tok0 = z * COLS * BLK
    seen = [jnp.bool_(False) for g in range(GROUPS)]
    begin = jnp.int32(0)
    for i in range(REQS):
        inside = (begin < tok0 + COLS * BLK) & (ends[i] > tok0)
        for g in range(GROUPS):
            seen[g] = seen[g] | (inside & (grps[i] == g))
        begin = ends[i]
    mixed = seen[0] & seen[1]
    acc[...] = jnp.zeros_like(acc)
    m[...] = jnp.full(m.shape, NEG, jnp.float32)

    for g in range(GROUPS):

        @pl.when(seen[g])
        def _():
            tops = []
            for t in range(TILES):
                sc = jnp.dot(
                    key_rows(kscr, g * half), qs[t], preferred_element_type=jnp.float32
                )
                tops.append(jnp.max(sc, axis=0, keepdims=True))
            for t in range(TILES):
                m[t] = jnp.where(gvecs[t // HPD] == g, tops[t], m[t])

    @pl.when(jnp.logical_not(mixed))
    def _():
        first = jnp.where(seen[0], 0, half)

        @pl.loop(0, half)
        def _(c):
            add_block(first + c, None, kscr, vscr, qs, acc, m)

    @pl.when(mixed)
    def _():
        @pl.loop(0, ZDIM)
        def _(c):
            masks = [jnp.broadcast_to(gv == c // half, (BLK, BLK)) for gv in gvecs]
            add_block(c, masks, kscr, vscr, qs, acc, m)

    @pl.when(overflowed(acc))
    def _():
        acc[...] = jnp.zeros_like(acc)
        m[...] = jnp.full(m.shape, NEG, jnp.float32)
        for k in range(COLS):

            @pl.loop(0, ZDIM)
            def _(c):
                mask = jnp.broadcast_to(gvecs[k] == c // half, (BLK, BLK))

                @pl.loop(0, HPD)
                def _(h):
                    add_block_exact(k * HPD + h, c, mask, kscr, vscr, qs, acc, m)


def suffix_body(lens, grps, sidx, suf, qs, acc_in, m_in, keep, send, kscr, vscr, acc, m):
    s = sidx[0]
    z = s // COLS
    r = s % COLS
    place(suf, kscr, vscr)
    ends = request_ends(lens)
    tvecs, svecs, unused = token_vectors(z, r, ends, grps)
    tok0 = z * COLS * BLK
    first = start_of(tok0, ends)
    last = start_of(tok0 + COLS * BLK - 1, ends)
    gap = jnp.maximum(first - (BLK - 1) - r * BLK, 0)
    low = jnp.minimum((gap + COLS * BLK - 1) // (COLS * BLK), z)
    acc[...] = acc_in[...]
    m[...] = m_in[...]

    def allowed(k, jz):
        kvec = (jz * COLS + r) * BLK + lax.broadcasted_iota(jnp.int32, (BLK, BLK), 0)
        return (kvec <= tvecs[k]) & (kvec >= svecs[k])

    def step(jz, c):
        full = (jz < z) & (last <= (jz * COLS + r) * BLK)

        @pl.when(full)
        def _():
            add_block(jz, None, kscr, vscr, qs, acc, m)

        @pl.when(jnp.logical_not(full))
        def _():
            add_block(jz, [allowed(k, jz) for k in range(COLS)], kscr, vscr, qs, acc, m)

        return c

    lax.fori_loop(low, z + 1, step, 0)

    @pl.when(overflowed(acc))
    def _():
        acc[...] = acc_in[...]
        m[...] = m_in[...]
        for k in range(COLS):

            def exact_step(jz, c):
                mask = allowed(k, jz)

                @pl.loop(0, HPD)
                def _(h):
                    add_block_exact(k * HPD + h, jz, mask, kscr, vscr, qs, acc, m)

                return c

            lax.fori_loop(low, z + 1, exact_step, 0)

    rows = lax.broadcasted_iota(jnp.int32, (16, BLK), 0)
    for k in range(COLS):
        extra = jnp.zeros((16, BLK), jnp.float32)
        dst = send if k % 2 else keep
        for h in range(HPD):
            t = k * HPD + h
            total_w = acc[t, HEAD_DIM : HEAD_DIM + 1, :]
            dst[k // 2, h * HEAD_DIM : (h + 1) * HEAD_DIM, :] = (
                acc[t, 0:HEAD_DIM, :] * (1.0 / total_w)
            ).astype(jnp.bfloat16)
            lse = m[t] + jnp.log(total_w)
            for j in range(3):
                part = lse.astype(jnp.bfloat16).astype(jnp.float32)
                extra = jnp.where(rows == 3 * h + j, part, extra)
                lse = lse - part
        dst[k // 2, QROWS:PROWS, :] = extra.astype(jnp.bfloat16)


def project_body(hidden, gain, wq, wk, wv, cosine, sinusoid, q_out, kv_out, k_out, v_out):
    wide = hidden[...].astype(jnp.float32)
    mean_square = jnp.mean(wide * wide, axis=-1, keepdims=True)
    normed = (wide * lax.rsqrt(mean_square + 1e-05) * gain[...]).astype(jnp.bfloat16)

    def proj(w):
        return lax.dot_general(
            w[...], normed, (((1,), (1,)), ((), ())), preferred_element_type=jnp.float32
        )

    c = cosine[...]
    sn = sinusoid[...]
    hf = HEAD_DIM // 2

    def rotate(a, b):
        return a * c - b * sn, b * c + a * sn

    kf = proj(wk)
    ka, kb = rotate(kf[0:hf], kf[hf:HEAD_DIM])
    kt = jnp.concatenate([ka, kb], axis=0).astype(jnp.bfloat16)
    vt = proj(wv).astype(jnp.bfloat16)
    k_out[...] = kt
    v_out[...] = vt
    for n in range(ZDIM):
        kv_out[n, 0:HEAD_DIM, :] = kt
        kv_out[n, HEAD_DIM : 2 * HEAD_DIM, :] = vt
    qf = proj(wq)
    for h in range(HPD):
        lo = h * HEAD_DIM
        qa, qb = rotate(qf[lo : lo + hf], qf[lo + hf : lo + HEAD_DIM])
        q_out[lo : lo + HEAD_DIM, :] = (
            jnp.concatenate([qa, qb], axis=0) * HEAD_DIM ** (-0.5)
        ).astype(jnp.bfloat16)


def merged(one, two):
    e1 = one[QROWS:PROWS, :].astype(jnp.float32)
    e2 = two[QROWS:PROWS, :].astype(jnp.float32)
    outs = []
    lses = []
    for h in range(HPD):
        l1 = e1[3 * h : 3 * h + 1] + e1[3 * h + 1 : 3 * h + 2] + e1[3 * h + 2 : 3 * h + 3]
        l2 = e2[3 * h : 3 * h + 1] + e2[3 * h + 1 : 3 * h + 2] + e2[3 * h + 2 : 3 * h + 3]
        top = jnp.maximum(l1, l2)
        w1 = jnp.exp(l1 - top)
        w2 = jnp.exp(l2 - top)
        tot = w1 + w2
        rows = slice(h * HEAD_DIM, (h + 1) * HEAD_DIM)
        o1 = one[rows, :].astype(jnp.float32)
        o2 = two[rows, :].astype(jnp.float32)
        outs.append((o1 * (w1 / tot) + o2 * (w2 / tot)).astype(jnp.bfloat16))
        lses.append(top + jnp.log(tot))
    return outs, lses


def merge_core_body(keep, recv, own, far):
    for k, dst in ((0, own), (1, far)):
        outs, lses = merged(keep[k], recv[k])
        extra = jnp.zeros((16, BLK), jnp.float32)
        rows = lax.broadcasted_iota(jnp.int32, (16, BLK), 0)
        for h in range(HPD):
            lse = lses[h]
            for j in range(3):
                part = lse.astype(jnp.bfloat16).astype(jnp.float32)
                extra = jnp.where(rows == 3 * h + j, part, extra)
                lse = lse - part
        dst[...] = jnp.concatenate(outs + [extra.astype(jnp.bfloat16)], axis=0)


def project_out_body(own, recv, w_t, out):
    outs, unused = merged(own[...], recv[...])
    attended = jnp.concatenate(outs, axis=0)
    out[...] = jnp.dot(w_t[...], attended, preferred_element_type=jnp.float32).astype(
        jnp.bfloat16
    )


def final_body(parts, residual, out):
    total = residual[...].astype(jnp.float32)
    acc = parts[0].astype(jnp.float32)
    for i in range(1, parts.shape[0]):
        acc = acc + parts[i].astype(jnp.float32)
    out[...] = (acc + total).astype(jnp.bfloat16)


def shape_of(*dims):
    return jax.ShapeDtypeStruct(dims, jnp.bfloat16)


VMEM_SPEC = pl.BlockSpec(memory_space=pltpu.VMEM)
SMEM_SPEC = pl.BlockSpec(memory_space=pltpu.SMEM)
PARAMS = pltpu.CompilerParams(vmem_limit_bytes=48 * 1024 * 1024)


def per_device(
    hidden_in,
    norm_gain,
    w_query,
    w_key,
    w_value,
    w_out,
    prefix_keys,
    prefix_values,
    lengths,
    groups,
):
    seq = lax.axis_index("seq")
    columns_of_z = [list(range(c, ZDIM * COLS, COLS)) for c in range(COLS)]

    def along_z(x):
        return lax.all_to_all(
            x, "seq", split_axis=0, concat_axis=0, tiled=True, axis_index_groups=columns_of_z
        )

    pre_own = jnp.concatenate([prefix_keys.T, prefix_values.T], axis=0)
    pre = along_z(jnp.broadcast_to(pre_own[None], (ZDIM,) + pre_own.shape))

    tok_rows = hidden_in.shape[0]
    token_index = seq * tok_rows + jnp.arange(tok_rows, dtype=jnp.int32)
    start = jnp.zeros((tok_rows,), jnp.int32)
    end = lengths[0]
    for i in range(1, REQS):
        start = jnp.where(token_index >= end, end, start)
        end = end + lengths[i]
    positions = 4096 + token_index - start
    half_dim = HEAD_DIM // 2
    frequency = jnp.power(
        jnp.float32(1000000.0), -jnp.arange(half_dim, dtype=jnp.float32) / half_dim
    )
    angles = frequency[:, None] * positions.astype(jnp.float32)[None, :]
    q_t, suf_own, key_t, value_t = pl.pallas_call(
        project_body,
        out_shape=(
            shape_of(QROWS, BLK),
            shape_of(ZDIM, 2 * HEAD_DIM, BLK),
            shape_of(HEAD_DIM, BLK),
            shape_of(HEAD_DIM, BLK),
        ),
        in_specs=[VMEM_SPEC] * 7,
        out_specs=(VMEM_SPEC,) * 4,
        compiler_params=PARAMS,
        name="project_in",
    )(
        hidden_in,
        norm_gain.reshape(1, -1),
        w_query.T,
        w_key.T,
        w_value.T,
        jnp.cos(angles),
        jnp.sin(angles),
    )
    q_x = lax.ppermute(q_t, "seq", [(i, i ^ 2) for i in range(32)])
    q_c = lax.ppermute(
        jnp.concatenate([q_t, q_x], axis=0), "seq", [(i, i ^ 1) for i in range(32)]
    )
    suf = along_z(suf_own)
    scalars = (lengths, groups, seq.astype(jnp.int32).reshape(1))
    kv_scratch = [
        pltpu.VMEM((ZDIM * BLK, 128), jnp.bfloat16),
        pltpu.VMEM((ZDIM, 96, BLK), jnp.bfloat16),
    ]
    qs, acc, top = pl.pallas_call(
        prefix_body,
        out_shape=(
            shape_of(TILES, 128, BLK),
            jax.ShapeDtypeStruct((TILES, 96, BLK), jnp.float32),
            jax.ShapeDtypeStruct((TILES, 1, BLK), jnp.float32),
        ),
        in_specs=[SMEM_SPEC] * 3 + [VMEM_SPEC] * 4,
        out_specs=(VMEM_SPEC,) * 3,
        scratch_shapes=kv_scratch,
        compiler_params=PARAMS,
        name="attend_prefix",
    )(*scalars, pre, q_t, q_x, q_c)
    top, w_out_t = lax.optimization_barrier((top, w_out.T))
    keep, send = pl.pallas_call(
        suffix_body,
        out_shape=(shape_of(2, PROWS, BLK), shape_of(2, PROWS, BLK)),
        in_specs=[SMEM_SPEC] * 3 + [VMEM_SPEC] * 4,
        out_specs=(VMEM_SPEC, VMEM_SPEC),
        scratch_shapes=kv_scratch
        + [
            pltpu.VMEM((TILES, 96, BLK), jnp.float32),
            pltpu.VMEM((TILES, 1, BLK), jnp.float32),
        ],
        compiler_params=PARAMS,
        name="attend_suffix",
    )(*scalars, suf, qs, acc, top)

    core_recv = lax.ppermute(send, "seq", [(i, i ^ 1) for i in range(32)])
    own, far = pl.pallas_call(
        merge_core_body,
        out_shape=(shape_of(PROWS, BLK), shape_of(PROWS, BLK)),
        in_specs=[VMEM_SPEC] * 2,
        out_specs=(VMEM_SPEC, VMEM_SPEC),
        compiler_params=PARAMS,
        name="merge_core",
    )(keep, core_recv)
    x_recv = lax.ppermute(far, "seq", [(i, i ^ 2) for i in range(32)])
    width = w_out.shape[1]
    projected = pl.pallas_call(
        project_out_body,
        out_shape=shape_of(width, BLK),
        in_specs=[VMEM_SPEC] * 3,
        out_specs=VMEM_SPEC,
        compiler_params=PARAMS,
        name="project_out",
    )(own, x_recv, w_out_t)
    tp = lax.axis_size("tp")
    columns = width // tp
    parts = lax.all_to_all(
        projected.reshape(tp, columns, BLK), "tp", split_axis=0, concat_axis=0, tiled=True
    )
    residual = lax.dynamic_slice_in_dim(
        hidden_in, lax.axis_index("tp") * columns, columns, 1
    ).T
    hidden_t = pl.pallas_call(
        final_body,
        out_shape=shape_of(columns, BLK),
        in_specs=[VMEM_SPEC] * 2,
        out_specs=VMEM_SPEC,
        compiler_params=PARAMS,
        name="final_sum",
    )(parts, residual)
    return (hidden_t.T, key_t.T, value_t.T)


def solution(mesh):
    return jax.shard_map(
        per_device,
        mesh=mesh,
        in_specs=(
            P("seq", None),
            P(),
            P(None, "tp"),
            P(None, "tp"),
            P(None, "tp"),
            P("tp", None),
            P("seq", "tp"),
            P("seq", "tp"),
            P(),
            P(),
        ),
        out_specs=(P("seq", "tp"), P("seq", "tp"), P("seq", "tp")),
        check_vma=False,
    )
```

```python
import jax
import jax.numpy as jnp
from jax import lax
from jax.experimental import pallas as pl
from jax.experimental.pallas import tpu as pltpu
from jax.sharding import PartitionSpec as P

HEAD_DIM = 80
GROUPS = 2
REQS = 4
BLK = 256
COLS = 4
ZDIM = 8
HPD = 4
QROWS = HPD * HEAD_DIM
PROWS = QROWS + 16
NEG = -1e30
LIMIT = 1e30
AHEAD = 4
TILES = COLS * HPD


def request_ends(lens):
    ends = []
    total = 0
    for i in range(REQS):
        total = total + lens[i]
        ends.append(total)
    return ends


def start_of(p, ends):
    st = jnp.int32(0)
    for i in range(REQS - 1):
        st = jnp.where(p >= ends[i], ends[i], st)
    return st


def token_vectors(z, r, ends, grps):
    tvecs, svecs, gvecs = [], [], []
    for k in range(COLS):
        tok0 = (z * COLS + (r ^ k)) * BLK
        tvec = tok0 + lax.broadcasted_iota(jnp.int32, (1, BLK), 1)
        svec = jnp.zeros((1, BLK), jnp.int32)
        gvec = jnp.zeros((1, BLK), jnp.int32) + grps[0]
        for i in range(REQS - 1):
            svec = jnp.where(tvec >= ends[i], ends[i], svec)
            gvec = jnp.where(tvec >= ends[i], grps[i + 1], gvec)
        tvecs.append(tvec)
        svecs.append(svec)
        gvecs.append(gvec)
    return tvecs, svecs, gvecs


def place(kv, n, kscr, vscr):
    kt = jnp.concatenate(
        [kv[0:HEAD_DIM, :], jnp.zeros((128 - HEAD_DIM, BLK), jnp.bfloat16)], axis=0
    )
    kscr[pl.ds(pl.multiple_of(n * BLK, BLK), BLK), :] = kt.T
    vscr[n, 0:HEAD_DIM, :] = kv[HEAD_DIM : 2 * HEAD_DIM, :]
    vscr[n, HEAD_DIM:96, :] = jnp.ones((96 - HEAD_DIM, BLK), jnp.bfloat16)


def key_rows(kscr, blk):
    return kscr[pl.ds(pl.multiple_of(blk * BLK, BLK), BLK), :]


def add_block(blk, masks, kscr, vscr, qs, acc, m):
    scores, weights = {}, {}
    for i in range(TILES + AHEAD + 1):
        if i < TILES:
            scores[i] = jnp.dot(key_rows(kscr, blk), qs[i], preferred_element_type=jnp.float32)
        j = i - AHEAD
        if 0 <= j < TILES:
            sc = scores.pop(j)
            if masks is not None:
                sc = jnp.where(masks[j // HPD], sc, NEG)
            weights[j] = jnp.exp(sc - m[j]).astype(jnp.bfloat16)
        n = j - 1
        if 0 <= n < TILES:
            acc[n] = acc[n] + jnp.dot(
                vscr[blk], weights.pop(n), preferred_element_type=jnp.float32
            )


def add_block_exact(tile, blk, mask, kscr, vscr, qs, acc, m):
    sc = jnp.dot(key_rows(kscr, blk), qs[tile], preferred_element_type=jnp.float32)
    sc = jnp.where(mask, sc, NEG)
    m_old = m[tile]
    m_new = jnp.maximum(m_old, jnp.max(sc, axis=0, keepdims=True))
    w = jnp.exp(sc - m_new).astype(jnp.bfloat16)
    acc[tile] = acc[tile] * jnp.exp(m_old - m_new) + jnp.dot(
        vscr[blk], w, preferred_element_type=jnp.float32
    )
    m[tile] = m_new


def overflowed(acc):
    top = acc[0, HEAD_DIM : HEAD_DIM + 1, :]
    for t in range(1, TILES):
        top = jnp.maximum(top, acc[t, HEAD_DIM : HEAD_DIM + 1, :])
    return jnp.logical_not(jnp.max(top) < LIMIT)


def prefix_body(lens, grps, sidx, pre, q_own, q_x, q_c, qs, acc, m, kscr, vscr):
    s = sidx[0]
    z = s // COLS
    r = s % COLS
    half = ZDIM // GROUPS
    for n in range(ZDIM):
        place(pre.at[n], n, kscr, vscr)
    for k, (ref, off) in enumerate(((q_own, 0), (q_c, 0), (q_x, 0), (q_c, QROWS))):
        for h in range(HPD):
            lo = off + h * HEAD_DIM
            qs[k * HPD + h, 0:HEAD_DIM, :] = ref[lo : lo + HEAD_DIM, :]
            qs[k * HPD + h, HEAD_DIM:128, :] = jnp.zeros((128 - HEAD_DIM, BLK), jnp.bfloat16)
    ends = request_ends(lens)
    gvecs = token_vectors(z, r, ends, grps)[2]
    tok0 = z * COLS * BLK
    seen = [jnp.bool_(False) for g in range(GROUPS)]
    begin = jnp.int32(0)
    for i in range(REQS):
        inside = (begin < tok0 + COLS * BLK) & (ends[i] > tok0)
        for g in range(GROUPS):
            seen[g] = seen[g] | (inside & (grps[i] == g))
        begin = ends[i]
    mixed = seen[0] & seen[1]
    acc[...] = jnp.zeros_like(acc)
    m[...] = jnp.full(m.shape, NEG, jnp.float32)

    for g in range(GROUPS):

        @pl.when(seen[g])
        def _():
            tops = []
            for t in range(TILES):
                sc = jnp.dot(
                    key_rows(kscr, g * half), qs[t], preferred_element_type=jnp.float32
                )
                tops.append(jnp.max(sc, axis=0, keepdims=True))
            for t in range(TILES):
                m[t] = jnp.where(gvecs[t // HPD] == g, tops[t], m[t])

    @pl.when(jnp.logical_not(mixed))
    def _():
        first = jnp.where(seen[0], 0, half)

        @pl.loop(0, half)
        def _(c):
            add_block(first + c, None, kscr, vscr, qs, acc, m)

    @pl.when(mixed)
    def _():
        @pl.loop(0, ZDIM)
        def _(c):
            masks = [jnp.broadcast_to(gv == c // half, (BLK, BLK)) for gv in gvecs]
            add_block(c, masks, kscr, vscr, qs, acc, m)

    @pl.when(overflowed(acc))
    def _():
        acc[...] = jnp.zeros_like(acc)
        m[...] = jnp.full(m.shape, NEG, jnp.float32)
        for k in range(COLS):

            @pl.loop(0, ZDIM)
            def _(c):
                mask = jnp.broadcast_to(gvecs[k] == c // half, (BLK, BLK))

                @pl.loop(0, HPD)
                def _(h):
                    add_block_exact(k * HPD + h, c, mask, kscr, vscr, qs, acc, m)


def suffix_body(lens, grps, sidx, *refs):
    suf = refs[:ZDIM]
    qs, acc_in, m_in, keep, send, kscr, vscr, acc, m = refs[ZDIM:]
    s = sidx[0]
    z = s // COLS
    r = s % COLS
    for d in range(ZDIM):
        place(suf[d], (z - d + ZDIM) % ZDIM, kscr, vscr)
    ends = request_ends(lens)
    tvecs, svecs, unused = token_vectors(z, r, ends, grps)
    tok0 = z * COLS * BLK
    first = start_of(tok0, ends)
    last = start_of(tok0 + COLS * BLK - 1, ends)
    gap = jnp.maximum(first - (BLK - 1) - r * BLK, 0)
    low = jnp.minimum((gap + COLS * BLK - 1) // (COLS * BLK), z)
    acc[...] = acc_in[...]
    m[...] = m_in[...]

    def allowed(k, jz):
        kvec = (jz * COLS + r) * BLK + lax.broadcasted_iota(jnp.int32, (BLK, BLK), 0)
        return (kvec <= tvecs[k]) & (kvec >= svecs[k])

    def step(jz, c):
        full = (jz < z) & (last <= (jz * COLS + r) * BLK)

        @pl.when(full)
        def _():
            add_block(jz, None, kscr, vscr, qs, acc, m)

        @pl.when(jnp.logical_not(full))
        def _():
            add_block(jz, [allowed(k, jz) for k in range(COLS)], kscr, vscr, qs, acc, m)

        return c

    lax.fori_loop(low, z + 1, step, 0)

    @pl.when(overflowed(acc))
    def _():
        acc[...] = acc_in[...]
        m[...] = m_in[...]
        for k in range(COLS):

            def exact_step(jz, c):
                mask = allowed(k, jz)

                @pl.loop(0, HPD)
                def _(h):
                    add_block_exact(k * HPD + h, jz, mask, kscr, vscr, qs, acc, m)

                return c

            lax.fori_loop(low, z + 1, exact_step, 0)

    rows = lax.broadcasted_iota(jnp.int32, (16, BLK), 0)
    for k in range(COLS):
        extra = jnp.zeros((16, BLK), jnp.float32)
        dst = send if k % 2 else keep
        for h in range(HPD):
            t = k * HPD + h
            total_w = acc[t, HEAD_DIM : HEAD_DIM + 1, :]
            dst[k // 2, h * HEAD_DIM : (h + 1) * HEAD_DIM, :] = (
                acc[t, 0:HEAD_DIM, :] * (1.0 / total_w)
            ).astype(jnp.bfloat16)
            lse = m[t] + jnp.log(total_w)
            for j in range(3):
                part = lse.astype(jnp.bfloat16).astype(jnp.float32)
                extra = jnp.where(rows == 3 * h + j, part, extra)
                lse = lse - part
        dst[k // 2, QROWS:PROWS, :] = extra.astype(jnp.bfloat16)


def project_body(hidden, gain, wq, wk, wv, cosine, sinusoid, q_out, kv_out, k_out, v_out):
    wide = hidden[...].astype(jnp.float32)
    mean_square = jnp.mean(wide * wide, axis=-1, keepdims=True)
    normed = (wide * lax.rsqrt(mean_square + 1e-05) * gain[...]).astype(jnp.bfloat16)

    def proj(w):
        return lax.dot_general(
            w[...], normed, (((1,), (1,)), ((), ())), preferred_element_type=jnp.float32
        )

    c = cosine[...]
    sn = sinusoid[...]
    hf = HEAD_DIM // 2

    def rotate(a, b):
        return a * c - b * sn, b * c + a * sn

    kf = proj(wk)
    ka, kb = rotate(kf[0:hf], kf[hf:HEAD_DIM])
    kt = jnp.concatenate([ka, kb], axis=0).astype(jnp.bfloat16)
    vt = proj(wv).astype(jnp.bfloat16)
    k_out[...] = kt
    v_out[...] = vt
    kv_out[0:HEAD_DIM, :] = kt
    kv_out[HEAD_DIM : 2 * HEAD_DIM, :] = vt
    qf = proj(wq)
    for h in range(HPD):
        lo = h * HEAD_DIM
        qa, qb = rotate(qf[lo : lo + hf], qf[lo + hf : lo + HEAD_DIM])
        q_out[lo : lo + HEAD_DIM, :] = (
            jnp.concatenate([qa, qb], axis=0) * HEAD_DIM ** (-0.5)
        ).astype(jnp.bfloat16)


def merged(one, two):
    e1 = one[QROWS:PROWS, :].astype(jnp.float32)
    e2 = two[QROWS:PROWS, :].astype(jnp.float32)
    outs = []
    lses = []
    for h in range(HPD):
        l1 = e1[3 * h : 3 * h + 1] + e1[3 * h + 1 : 3 * h + 2] + e1[3 * h + 2 : 3 * h + 3]
        l2 = e2[3 * h : 3 * h + 1] + e2[3 * h + 1 : 3 * h + 2] + e2[3 * h + 2 : 3 * h + 3]
        top = jnp.maximum(l1, l2)
        w1 = jnp.exp(l1 - top)
        w2 = jnp.exp(l2 - top)
        tot = w1 + w2
        rows = slice(h * HEAD_DIM, (h + 1) * HEAD_DIM)
        o1 = one[rows, :].astype(jnp.float32)
        o2 = two[rows, :].astype(jnp.float32)
        outs.append((o1 * (w1 / tot) + o2 * (w2 / tot)).astype(jnp.bfloat16))
        lses.append(top + jnp.log(tot))
    return outs, lses


def merge_core_body(keep, recv, own, far):
    for k, dst in ((0, own), (1, far)):
        outs, lses = merged(keep[k], recv[k])
        extra = jnp.zeros((16, BLK), jnp.float32)
        rows = lax.broadcasted_iota(jnp.int32, (16, BLK), 0)
        for h in range(HPD):
            lse = lses[h]
            for j in range(3):
                part = lse.astype(jnp.bfloat16).astype(jnp.float32)
                extra = jnp.where(rows == 3 * h + j, part, extra)
                lse = lse - part
        dst[...] = jnp.concatenate(outs + [extra.astype(jnp.bfloat16)], axis=0)


def project_out_body(own, recv, w_t, out):
    outs, unused = merged(own[...], recv[...])
    attended = jnp.concatenate(outs, axis=0)
    out[...] = jnp.dot(w_t[...], attended, preferred_element_type=jnp.float32).astype(
        jnp.bfloat16
    )


def final_body(parts, residual, out):
    total = residual[...].astype(jnp.float32)
    acc = parts[0].astype(jnp.float32)
    for i in range(1, parts.shape[0]):
        acc = acc + parts[i].astype(jnp.float32)
    out[...] = (acc + total).astype(jnp.bfloat16)


def shape_of(*dims):
    return jax.ShapeDtypeStruct(dims, jnp.bfloat16)


VMEM_SPEC = pl.BlockSpec(memory_space=pltpu.VMEM)
SMEM_SPEC = pl.BlockSpec(memory_space=pltpu.SMEM)
PARAMS = pltpu.CompilerParams(vmem_limit_bytes=20 * 1024 * 1024)


def per_device(
    hidden_in,
    norm_gain,
    w_query,
    w_key,
    w_value,
    w_out,
    prefix_keys,
    prefix_values,
    lengths,
    groups,
):
    seq = lax.axis_index("seq")
    columns_of_z = [list(range(c, ZDIM * COLS, COLS)) for c in range(COLS)]

    def along_z(x):
        return lax.all_to_all(
            x, "seq", split_axis=0, concat_axis=0, tiled=True, axis_index_groups=columns_of_z
        )

    pre_own = jnp.concatenate([prefix_keys.T, prefix_values.T], axis=0)
    pre = along_z(jnp.broadcast_to(pre_own[None], (ZDIM,) + pre_own.shape))

    tok_rows = hidden_in.shape[0]
    token_index = seq * tok_rows + jnp.arange(tok_rows, dtype=jnp.int32)
    start = jnp.zeros((tok_rows,), jnp.int32)
    end = lengths[0]
    for i in range(1, REQS):
        start = jnp.where(token_index >= end, end, start)
        end = end + lengths[i]
    positions = 4096 + token_index - start
    half_dim = HEAD_DIM // 2
    frequency = jnp.power(
        jnp.float32(1000000.0), -jnp.arange(half_dim, dtype=jnp.float32) / half_dim
    )
    angles = frequency[:, None] * positions.astype(jnp.float32)[None, :]
    q_t, suf_own, key_t, value_t = pl.pallas_call(
        project_body,
        out_shape=(
            shape_of(QROWS, BLK),
            shape_of(2 * HEAD_DIM, BLK),
            shape_of(HEAD_DIM, BLK),
            shape_of(HEAD_DIM, BLK),
        ),
        in_specs=[VMEM_SPEC] * 7,
        out_specs=(VMEM_SPEC,) * 4,
        compiler_params=PARAMS,
        name="project_in",
    )(
        hidden_in,
        norm_gain.reshape(1, -1),
        w_query.T,
        w_key.T,
        w_value.T,
        jnp.cos(angles),
        jnp.sin(angles),
    )
    q_x = lax.ppermute(q_t, "seq", [(i, i ^ 2) for i in range(32)])
    q_c = lax.ppermute(
        jnp.concatenate([q_t, q_x], axis=0), "seq", [(i, i ^ 1) for i in range(32)]
    )
    suf = [suf_own] + [
        lax.ppermute(
            suf_own, "seq", [(i, i + COLS * d) for i in range(COLS * (ZDIM - d))]
        )
        for d in range(1, ZDIM)
    ]
    scalars = (lengths, groups, seq.astype(jnp.int32).reshape(1))
    kv_scratch = [
        pltpu.VMEM((ZDIM * BLK, 128), jnp.bfloat16),
        pltpu.VMEM((ZDIM, 96, BLK), jnp.bfloat16),
    ]
    qs, acc, top = pl.pallas_call(
        prefix_body,
        out_shape=(
            shape_of(TILES, 128, BLK),
            jax.ShapeDtypeStruct((TILES, 96, BLK), jnp.float32),
            jax.ShapeDtypeStruct((TILES, 1, BLK), jnp.float32),
        ),
        in_specs=[SMEM_SPEC] * 3 + [VMEM_SPEC] * 4,
        out_specs=(VMEM_SPEC,) * 3,
        scratch_shapes=kv_scratch,
        compiler_params=PARAMS,
        name="attend_prefix",
    )(*scalars, pre, q_t, q_x, q_c)
    top, w_out_t = lax.optimization_barrier((top, w_out.T))
    keep, send = pl.pallas_call(
        suffix_body,
        out_shape=(shape_of(2, PROWS, BLK), shape_of(2, PROWS, BLK)),
        in_specs=[SMEM_SPEC] * 3 + [VMEM_SPEC] * (ZDIM + 3),
        out_specs=(VMEM_SPEC, VMEM_SPEC),
        scratch_shapes=kv_scratch
        + [
            pltpu.VMEM((TILES, 96, BLK), jnp.float32),
            pltpu.VMEM((TILES, 1, BLK), jnp.float32),
        ],
        compiler_params=PARAMS,
        name="attend_suffix",
    )(*scalars, *suf, qs, acc, top)

    core_recv = lax.ppermute(send, "seq", [(i, i ^ 1) for i in range(32)])
    own, far = pl.pallas_call(
        merge_core_body,
        out_shape=(shape_of(PROWS, BLK), shape_of(PROWS, BLK)),
        in_specs=[VMEM_SPEC] * 2,
        out_specs=(VMEM_SPEC, VMEM_SPEC),
        compiler_params=PARAMS,
        name="merge_core",
    )(keep, core_recv)
    x_recv = lax.ppermute(far, "seq", [(i, i ^ 2) for i in range(32)])
    width = w_out.shape[1]
    projected = pl.pallas_call(
        project_out_body,
        out_shape=shape_of(width, BLK),
        in_specs=[VMEM_SPEC] * 3,
        out_specs=VMEM_SPEC,
        compiler_params=PARAMS,
        name="project_out",
    )(own, x_recv, w_out_t)
    tp = lax.axis_size("tp")
    columns = width // tp
    parts = lax.all_to_all(
        projected.reshape(tp, columns, BLK), "tp", split_axis=0, concat_axis=0, tiled=True
    )
    residual = lax.dynamic_slice_in_dim(
        hidden_in, lax.axis_index("tp") * columns, columns, 1
    ).T
    hidden_t = pl.pallas_call(
        final_body,
        out_shape=shape_of(columns, BLK),
        in_specs=[VMEM_SPEC] * 2,
        out_specs=VMEM_SPEC,
        compiler_params=PARAMS,
        name="final_sum",
    )(parts, residual)
    return (hidden_t.T, key_t.T, value_t.T)


def solution(mesh):
    return jax.shard_map(
        per_device,
        mesh=mesh,
        in_specs=(
            P("seq", None),
            P(),
            P(None, "tp"),
            P(None, "tp"),
            P(None, "tp"),
            P("tp", None),
            P("seq", "tp"),
            P("seq", "tp"),
            P(),
            P(),
        ),
        out_specs=(P("seq", "tp"), P("seq", "tp"), P("seq", "tp")),
        check_vma=False,
    )
```

```python
import jax
import jax.numpy as jnp
from jax import lax
from jax.experimental import pallas as pl
from jax.experimental.pallas import tpu as pltpu
from jax.sharding import PartitionSpec as P

HEAD_DIM = 80
GROUPS = 2
REQS = 4
BLK = 256
COLS = 4
ZDIM = 8
HPD = 4
QROWS = HPD * HEAD_DIM
PROWS = QROWS + 16
NEG = -1e30
LIMIT = 1e30
AHEAD = 4
TILES = COLS * HPD


def request_ends(lens):
    ends = []
    total = 0
    for i in range(REQS):
        total = total + lens[i]
        ends.append(total)
    return ends


def start_of(p, ends):
    st = jnp.int32(0)
    for i in range(REQS - 1):
        st = jnp.where(p >= ends[i], ends[i], st)
    return st


def token_vectors(z, r, ends, grps):
    tvecs, svecs, gvecs = [], [], []
    for k in range(COLS):
        tok0 = (z * COLS + (r ^ k)) * BLK
        tvec = tok0 + lax.broadcasted_iota(jnp.int32, (1, BLK), 1)
        svec = jnp.zeros((1, BLK), jnp.int32)
        gvec = jnp.zeros((1, BLK), jnp.int32) + grps[0]
        for i in range(REQS - 1):
            svec = jnp.where(tvec >= ends[i], ends[i], svec)
            gvec = jnp.where(tvec >= ends[i], grps[i + 1], gvec)
        tvecs.append(tvec)
        svecs.append(svec)
        gvecs.append(gvec)
    return tvecs, svecs, gvecs


def place(kv, n, kscr, vscr):
    kt = jnp.concatenate(
        [kv[0:HEAD_DIM, :], jnp.zeros((128 - HEAD_DIM, BLK), jnp.bfloat16)], axis=0
    )
    kscr[pl.ds(pl.multiple_of(n * BLK, BLK), BLK), :] = kt.T
    vscr[n, 0:HEAD_DIM, :] = kv[HEAD_DIM : 2 * HEAD_DIM, :]
    vscr[n, HEAD_DIM:96, :] = jnp.ones((96 - HEAD_DIM, BLK), jnp.bfloat16)


def key_rows(kscr, blk):
    return kscr[pl.ds(pl.multiple_of(blk * BLK, BLK), BLK), :]


def add_block(blk, masks, kscr, vscr, qs, acc, m):
    tiles = qs.shape[0]
    scores, weights = {}, {}
    for i in range(tiles + AHEAD + 1):
        if i < tiles:
            scores[i] = jnp.dot(key_rows(kscr, blk), qs[i], preferred_element_type=jnp.float32)
        j = i - AHEAD
        if 0 <= j < tiles:
            sc = scores.pop(j)
            if masks is not None:
                sc = jnp.where(masks[j // HPD], sc, NEG)
            weights[j] = jnp.exp(sc - m[j]).astype(jnp.bfloat16)
        n = j - 1
        if 0 <= n < tiles:
            acc[n] = acc[n] + jnp.dot(
                vscr[blk], weights.pop(n), preferred_element_type=jnp.float32
            )


def add_block_exact(tile, blk, mask, kscr, vscr, qs, acc, m):
    sc = jnp.dot(key_rows(kscr, blk), qs[tile], preferred_element_type=jnp.float32)
    sc = jnp.where(mask, sc, NEG)
    m_old = m[tile]
    m_new = jnp.maximum(m_old, jnp.max(sc, axis=0, keepdims=True))
    w = jnp.exp(sc - m_new).astype(jnp.bfloat16)
    acc[tile] = acc[tile] * jnp.exp(m_old - m_new) + jnp.dot(
        vscr[blk], w, preferred_element_type=jnp.float32
    )
    m[tile] = m_new


def overflowed(acc):
    top = acc[0, HEAD_DIM : HEAD_DIM + 1, :]
    for t in range(1, acc.shape[0]):
        top = jnp.maximum(top, acc[t, HEAD_DIM : HEAD_DIM + 1, :])
    return jnp.logical_not(jnp.max(top) < LIMIT)


def prefix_body(lens, grps, sidx, pre, q_0, q_1, q_2, q_3, qs, acc, m, kscr, vscr):
    s = sidx[0]
    z = s // COLS
    r = s % COLS
    half = ZDIM // GROUPS
    for n in range(ZDIM):
        place(pre.at[n], n, kscr, vscr)
    for k, ref in enumerate((q_0, q_1, q_2, q_3)):
        for h in range(HPD):
            lo = h * HEAD_DIM
            qs[k * HPD + h, 0:HEAD_DIM, :] = ref[lo : lo + HEAD_DIM, :]
            qs[k * HPD + h, HEAD_DIM:128, :] = jnp.zeros((128 - HEAD_DIM, BLK), jnp.bfloat16)
    ends = request_ends(lens)
    gvecs = token_vectors(z, r, ends, grps)[2]
    tok0 = z * COLS * BLK
    seen = [jnp.bool_(False) for g in range(GROUPS)]
    begin = jnp.int32(0)
    for i in range(REQS):
        inside = (begin < tok0 + COLS * BLK) & (ends[i] > tok0)
        for g in range(GROUPS):
            seen[g] = seen[g] | (inside & (grps[i] == g))
        begin = ends[i]
    mixed = seen[0] & seen[1]
    acc[...] = jnp.zeros_like(acc)
    m[...] = jnp.full(m.shape, NEG, jnp.float32)

    for g in range(GROUPS):

        @pl.when(seen[g])
        def _():
            tops = []
            for t in range(TILES):
                sc = jnp.dot(
                    key_rows(kscr, g * half), qs[t], preferred_element_type=jnp.float32
                )
                tops.append(jnp.max(sc, axis=0, keepdims=True))
            for t in range(TILES):
                m[t] = jnp.where(gvecs[t // HPD] == g, tops[t], m[t])

    @pl.when(jnp.logical_not(mixed))
    def _():
        first = jnp.where(seen[0], 0, half)

        @pl.loop(0, half)
        def _(c):
            add_block(first + c, None, kscr, vscr, qs, acc, m)

    @pl.when(mixed)
    def _():
        @pl.loop(0, ZDIM)
        def _(c):
            masks = [jnp.broadcast_to(gv == c // half, (BLK, BLK)) for gv in gvecs]
            add_block(c, masks, kscr, vscr, qs, acc, m)

    @pl.when(overflowed(acc))
    def _():
        acc[...] = jnp.zeros_like(acc)
        m[...] = jnp.full(m.shape, NEG, jnp.float32)
        for k in range(COLS):

            @pl.loop(0, ZDIM)
            def _(c):
                mask = jnp.broadcast_to(gvecs[k] == c // half, (BLK, BLK))

                @pl.loop(0, HPD)
                def _(h):
                    add_block_exact(k * HPD + h, c, mask, kscr, vscr, qs, acc, m)


def write_partial(dst, acc, m, k):
    rows = lax.broadcasted_iota(jnp.int32, (16, BLK), 0)
    extra = jnp.zeros((16, BLK), jnp.float32)
    for h in range(HPD):
        t = k * HPD + h
        total_w = acc[t, HEAD_DIM : HEAD_DIM + 1, :]
        dst[h * HEAD_DIM : (h + 1) * HEAD_DIM, :] = (
            acc[t, 0:HEAD_DIM, :] * (1.0 / total_w)
        ).astype(jnp.bfloat16)
        lse = m[t] + jnp.log(total_w)
        for j in range(3):
            part = lse.astype(jnp.bfloat16).astype(jnp.float32)
            extra = jnp.where(rows == 3 * h + j, part, extra)
            lse = lse - part
    dst[QROWS:PROWS, :] = extra.astype(jnp.bfloat16)


def suffix_tiles(k0, lens, grps, sidx, qs, acc_in, m_in, keep, send, kscr, vscr, acc, m):
    s = sidx[0]
    z = s // COLS
    r = s % COLS
    ends = request_ends(lens)
    tvecs, svecs, unused = token_vectors(z, r, ends, grps)
    tok0 = z * COLS * BLK
    first = start_of(tok0, ends)
    last = start_of(tok0 + COLS * BLK - 1, ends)
    gap = jnp.maximum(first - (BLK - 1) - r * BLK, 0)
    low = jnp.minimum((gap + COLS * BLK - 1) // (COLS * BLK), z)
    acc[...] = acc_in[...]
    m[...] = m_in[...]

    def allowed(k, jz):
        kvec = (jz * COLS + r) * BLK + lax.broadcasted_iota(jnp.int32, (BLK, BLK), 0)
        return (kvec <= tvecs[k0 + k]) & (kvec >= svecs[k0 + k])

    def step(jz, c):
        full = (jz < z) & (last <= (jz * COLS + r) * BLK)

        @pl.when(full)
        def _():
            add_block(jz, None, kscr, vscr, qs, acc, m)

        @pl.when(jnp.logical_not(full))
        def _():
            add_block(jz, [allowed(k, jz) for k in range(2)], kscr, vscr, qs, acc, m)

        return c

    lax.fori_loop(low, z + 1, step, 0)

    @pl.when(overflowed(acc))
    def _():
        acc[...] = acc_in[...]
        m[...] = m_in[...]
        for k in range(2):

            def exact_step(jz, c):
                mask = allowed(k, jz)

                @pl.loop(0, HPD)
                def _(h):
                    add_block_exact(k * HPD + h, jz, mask, kscr, vscr, qs, acc, m)

                return c

            lax.fori_loop(low, z + 1, exact_step, 0)

    write_partial(keep, acc, m, 0)
    write_partial(send, acc, m, 1)


def far_body(lens, grps, sidx, *refs):
    suf = refs[: ZDIM - 1]
    qs, acc_in, m_in, keep, send, kscr, vscr, acc, m = refs[ZDIM - 1 :]
    z = sidx[0] // COLS
    for d in range(ZDIM - 1):
        place(suf[d], (z - d + ZDIM) % ZDIM, kscr, vscr)
    suffix_tiles(2, lens, grps, sidx, qs, acc_in, m_in, keep, send, kscr, vscr, acc, m)


def near_body(lens, grps, sidx, kscr, vscr, qs, acc_in, m_in, keep, send, acc, m):
    suffix_tiles(0, lens, grps, sidx, qs, acc_in, m_in, keep, send, kscr, vscr, acc, m)


def spread_body(keys, values, out):
    for n in range(ZDIM):
        out[n, 0:HEAD_DIM, :] = keys[...]
        out[n, HEAD_DIM : 2 * HEAD_DIM, :] = values[...]


def project_body(
    hidden, gain, wq_far, wk, wv, cosine, sinusoid, q_out, kv_out, k_out, v_out, wq, sem
):
    fetch = pltpu.make_async_copy(wq_far, wq, sem)
    fetch.start()
    wide = hidden[...].astype(jnp.float32)
    mean_square = jnp.mean(wide * wide, axis=-1, keepdims=True)
    normed = (wide * lax.rsqrt(mean_square + 1e-05) * gain[...]).astype(jnp.bfloat16)

    def proj(w):
        return lax.dot_general(
            w[...], normed, (((1,), (1,)), ((), ())), preferred_element_type=jnp.float32
        )

    c = cosine[...]
    sn = sinusoid[...]
    hf = HEAD_DIM // 2

    def rotate(a, b):
        return a * c - b * sn, b * c + a * sn

    kf = proj(wk)
    ka, kb = rotate(kf[0:hf], kf[hf:HEAD_DIM])
    kt = jnp.concatenate([ka, kb], axis=0).astype(jnp.bfloat16)
    vt = proj(wv).astype(jnp.bfloat16)
    k_out[...] = kt
    v_out[...] = vt
    kv_out[0:HEAD_DIM, :] = kt
    kv_out[HEAD_DIM : 2 * HEAD_DIM, :] = vt
    fetch.wait()
    qf = proj(wq)
    for h in range(HPD):
        lo = h * HEAD_DIM
        qa, qb = rotate(qf[lo : lo + hf], qf[lo + hf : lo + HEAD_DIM])
        q_out[lo : lo + HEAD_DIM, :] = (
            jnp.concatenate([qa, qb], axis=0) * HEAD_DIM ** (-0.5)
        ).astype(jnp.bfloat16)


def merged(*parts):
    tails = [p[QROWS:PROWS, :].astype(jnp.float32) for p in parts]
    outs, lses = [], []
    for h in range(HPD):
        ls = [
            t[3 * h : 3 * h + 1] + t[3 * h + 1 : 3 * h + 2] + t[3 * h + 2 : 3 * h + 3]
            for t in tails
        ]
        top = ls[0]
        for x in ls[1:]:
            top = jnp.maximum(top, x)
        ws = [jnp.exp(x - top) for x in ls]
        tot = ws[0]
        for x in ws[1:]:
            tot = tot + x
        rows = slice(h * HEAD_DIM, (h + 1) * HEAD_DIM)
        out = parts[0][rows, :].astype(jnp.float32) * (ws[0] / tot)
        for p, w in zip(parts[1:], ws[1:]):
            out = out + p[rows, :].astype(jnp.float32) * (w / tot)
        outs.append(out.astype(jnp.bfloat16))
        lses.append(top + jnp.log(tot))
    return outs, lses


def merge_far_body(keep, recv, dst):
    outs, lses = merged(keep[...], recv[...])
    extra = jnp.zeros((16, BLK), jnp.float32)
    rows = lax.broadcasted_iota(jnp.int32, (16, BLK), 0)
    for h in range(HPD):
        lse = lses[h]
        for j in range(3):
            part = lse.astype(jnp.bfloat16).astype(jnp.float32)
            extra = jnp.where(rows == 3 * h + j, part, extra)
            lse = lse - part
    dst[...] = jnp.concatenate(outs + [extra.astype(jnp.bfloat16)], axis=0)


def project_out_body(own, near, w, out):
    outs, unused = merged(own[...], near[...])
    attended = jnp.concatenate(outs, axis=0)
    out[...] = lax.dot_general(
        w[...], attended, (((0,), (0,)), ((), ())), preferred_element_type=jnp.float32
    ).astype(jnp.bfloat16)


def final_body(parts, residual, out):
    total = residual[...].astype(jnp.float32)
    acc = parts[0].astype(jnp.float32)
    for i in range(1, parts.shape[0]):
        acc = acc + parts[i].astype(jnp.float32)
    out[...] = (acc + total).astype(jnp.bfloat16)


def shape_of(*dims):
    return jax.ShapeDtypeStruct(dims, jnp.bfloat16)


VMEM_SPEC = pl.BlockSpec(memory_space=pltpu.VMEM)
SMEM_SPEC = pl.BlockSpec(memory_space=pltpu.SMEM)
PARAMS = pltpu.CompilerParams(vmem_limit_bytes=20 * 1024 * 1024)


def per_device(
    hidden_in,
    norm_gain,
    w_query,
    w_key,
    w_value,
    w_out,
    prefix_keys,
    prefix_values,
    lengths,
    groups,
):
    seq = lax.axis_index("seq")
    columns_of_z = [list(range(c, ZDIM * COLS, COLS)) for c in range(COLS)]

    def along_z(x):
        return lax.all_to_all(
            x, "seq", split_axis=0, concat_axis=0, tiled=True, axis_index_groups=columns_of_z
        )

    pre = along_z(
        pl.pallas_call(
            spread_body,
            out_shape=shape_of(ZDIM, 2 * HEAD_DIM, BLK),
            in_specs=[VMEM_SPEC] * 2,
            out_specs=VMEM_SPEC,
            compiler_params=PARAMS,
            name="spread_prefix",
        )(prefix_keys.T, prefix_values.T)
    )

    tok_rows = hidden_in.shape[0]
    token_index = seq * tok_rows + jnp.arange(tok_rows, dtype=jnp.int32)
    start = jnp.zeros((tok_rows,), jnp.int32)
    end = lengths[0]
    for i in range(1, REQS):
        start = jnp.where(token_index >= end, end, start)
        end = end + lengths[i]
    positions = 4096 + token_index - start
    half_dim = HEAD_DIM // 2
    frequency = jnp.power(
        jnp.float32(1000000.0), -jnp.arange(half_dim, dtype=jnp.float32) / half_dim
    )
    angles = frequency[:, None] * positions.astype(jnp.float32)[None, :]
    q_t, suf_own, key_t, value_t = pl.pallas_call(
        project_body,
        out_shape=(
            shape_of(QROWS, BLK),
            shape_of(2 * HEAD_DIM, BLK),
            shape_of(HEAD_DIM, BLK),
            shape_of(HEAD_DIM, BLK),
        ),
        in_specs=[VMEM_SPEC] * 2 + [pl.BlockSpec(memory_space=pltpu.HBM)] + [VMEM_SPEC] * 4,
        out_specs=(VMEM_SPEC,) * 4,
        scratch_shapes=[
            pltpu.VMEM((QROWS, w_query.shape[0]), jnp.bfloat16),
            pltpu.SemaphoreType.DMA,
        ],
        compiler_params=PARAMS,
        name="project_in",
    )(
        hidden_in,
        norm_gain.reshape(1, -1),
        w_query.T,
        w_key.T,
        w_value.T,
        jnp.cos(angles),
        jnp.sin(angles),
    )
    q_all = [q_t] + [
        lax.ppermute(q_t, "seq", [(i, i ^ k) for i in range(32)]) for k in range(1, COLS)
    ]

    def later(x, d):
        return lax.ppermute(
            x, "seq", [(i, i + COLS * d) for i in range(COLS * (ZDIM - d))]
        )

    suf = [suf_own] + [later(suf_own, d) for d in range(1, ZDIM - 1)]
    scalars = (lengths, groups, seq.astype(jnp.int32).reshape(1))
    kv_scratch = [
        pltpu.VMEM((ZDIM * BLK, 128), jnp.bfloat16),
        pltpu.VMEM((ZDIM, 96, BLK), jnp.bfloat16),
    ]
    qs, acc, top = pl.pallas_call(
        prefix_body,
        out_shape=(
            shape_of(TILES, 128, BLK),
            jax.ShapeDtypeStruct((TILES, 96, BLK), jnp.float32),
            jax.ShapeDtypeStruct((TILES, 1, BLK), jnp.float32),
        ),
        in_specs=[SMEM_SPEC] * 3 + [VMEM_SPEC] * 5,
        out_specs=(VMEM_SPEC,) * 3,
        scratch_shapes=kv_scratch,
        compiler_params=PARAMS,
        cost_estimate=pl.CostEstimate(
            flops=6 * 10**9, transcendentals=6 * 10**6, bytes_accessed=4 * 10**6
        ),
        name="attend_prefix",
    )(*scalars, pre, *q_all)
    halves = TILES // 2
    half_scratch = [
        pltpu.VMEM((halves, 96, BLK), jnp.float32),
        pltpu.VMEM((halves, 1, BLK), jnp.float32),
    ]

    def half_specs(at):
        return [
            pl.BlockSpec((halves, 128, BLK), lambda i: (at, 0, 0)),
            pl.BlockSpec((halves, 96, BLK), lambda i: (at, 0, 0)),
            pl.BlockSpec((halves, 1, BLK), lambda i: (at, 0, 0)),
        ]

    core_pairs = [(i, i ^ 1) for i in range(32)]
    keep_far, send_far, keys, values = pl.pallas_call(
        far_body,
        grid=(1,),
        out_shape=(
            shape_of(PROWS, BLK),
            shape_of(PROWS, BLK),
            shape_of(ZDIM * BLK, 128),
            shape_of(ZDIM, 96, BLK),
        ),
        in_specs=[SMEM_SPEC] * 3 + [VMEM_SPEC] * (ZDIM - 1) + half_specs(1),
        out_specs=(VMEM_SPEC,) * 4,
        scratch_shapes=half_scratch,
        compiler_params=PARAMS,
        cost_estimate=pl.CostEstimate(
            flops=5 * 10**9, transcendentals=5 * 10**6, bytes_accessed=4 * 10**6
        ),
        name="attend_suffix_far",
    )(*scalars, *suf, qs, acc, top)

    def merge_two(one, two):
        return pl.pallas_call(
            merge_far_body,
            out_shape=shape_of(PROWS, BLK),
            in_specs=[VMEM_SPEC] * 2,
            out_specs=VMEM_SPEC,
            compiler_params=PARAMS,
            name="merge_two",
        )(one, two)

    far = merge_two(keep_far, lax.ppermute(send_far, "seq", core_pairs))
    far, values = lax.optimization_barrier((far, values))
    x_recv = lax.ppermute(far, "seq", [(i, i ^ 2) for i in range(32)])
    keep_near, send_near = pl.pallas_call(
        near_body,
        grid=(1,),
        out_shape=(shape_of(PROWS, BLK), shape_of(PROWS, BLK)),
        in_specs=[SMEM_SPEC] * 3 + [VMEM_SPEC] * 2 + half_specs(0),
        out_specs=(VMEM_SPEC, VMEM_SPEC),
        scratch_shapes=half_scratch,
        compiler_params=PARAMS,
        cost_estimate=pl.CostEstimate(
            flops=5 * 10**9, transcendentals=5 * 10**6, bytes_accessed=4 * 10**6
        ),
        name="attend_suffix_near",
    )(*scalars, keys, values, qs, acc, top)
    core_recv = lax.ppermute(send_near, "seq", core_pairs)
    width = w_out.shape[1]
    projected = pl.pallas_call(
        project_out_body,
        out_shape=shape_of(width, BLK),
        in_specs=[VMEM_SPEC] * 3,
        out_specs=VMEM_SPEC,
        compiler_params=PARAMS,
        name="project_out",
    )(merge_two(keep_near, x_recv), core_recv, w_out)
    tp = lax.axis_size("tp")
    columns = width // tp
    parts = lax.all_to_all(
        projected.reshape(tp, columns, BLK), "tp", split_axis=0, concat_axis=0, tiled=True
    )
    residual = lax.dynamic_slice_in_dim(
        hidden_in, lax.axis_index("tp") * columns, columns, 1
    ).T
    hidden_t = pl.pallas_call(
        final_body,
        out_shape=shape_of(columns, BLK),
        in_specs=[VMEM_SPEC] * 2,
        out_specs=VMEM_SPEC,
        compiler_params=PARAMS,
        name="final_sum",
    )(parts, residual)
    return (hidden_t.T, key_t.T, value_t.T)


def solution(mesh):
    return jax.shard_map(
        per_device,
        mesh=mesh,
        in_specs=(
            P("seq", None),
            P(),
            P(None, "tp"),
            P(None, "tp"),
            P(None, "tp"),
            P("tp", None),
            P("seq", "tp"),
            P("seq", "tp"),
            P(),
            P(),
        ),
        out_specs=(P("seq", "tp"), P("seq", "tp"), P("seq", "tp")),
        check_vma=False,
    )
```

```python
import jax
import jax.numpy as jnp
from jax import lax
from jax.experimental import pallas as pl
from jax.experimental.pallas import tpu as pltpu
from jax.sharding import PartitionSpec as P

HEAD_DIM = 80
GROUPS = 2
REQS = 4
BLK = 256
PRE_LEN = 4096
COLS = 4
ZDIM = 8
HPD = 4
QROWS = HPD * HEAD_DIM
PROWS = QROWS + 16
NEG = -1e30
LIMIT = 1e30
AHEAD = 4
TILES = COLS * HPD
EARLY = 3
LATE = 6 + 1 - EARLY


def request_ends(lens):
    ends = []
    total = 0
    for i in range(REQS):
        total = total + lens[i]
        ends.append(total)
    return ends


def start_of(p, ends):
    st = jnp.int32(0)
    for i in range(REQS - 1):
        st = jnp.where(p >= ends[i], ends[i], st)
    return st


def token_vectors(z, r, ends, grps):
    tvecs, svecs, gvecs = [], [], []
    for k in range(COLS):
        tok0 = (z * COLS + (r ^ k)) * BLK
        tvec = tok0 + lax.broadcasted_iota(jnp.int32, (1, BLK), 1)
        svec = jnp.zeros((1, BLK), jnp.int32)
        gvec = jnp.zeros((1, BLK), jnp.int32) + grps[0]
        for i in range(REQS - 1):
            svec = jnp.where(tvec >= ends[i], ends[i], svec)
            gvec = jnp.where(tvec >= ends[i], grps[i + 1], gvec)
        tvecs.append(tvec)
        svecs.append(svec)
        gvecs.append(gvec)
    return tvecs, svecs, gvecs


def place(kv, n, kscr, vscr):
    kt = jnp.concatenate(
        [kv[0:HEAD_DIM, :], jnp.zeros((128 - HEAD_DIM, BLK), jnp.bfloat16)], axis=0
    )
    kscr[pl.ds(pl.multiple_of(n * BLK, BLK), BLK), :] = kt.T
    vscr[n, 0:HEAD_DIM, :] = kv[HEAD_DIM : 2 * HEAD_DIM, :]
    vscr[n, HEAD_DIM:96, :] = jnp.ones((96 - HEAD_DIM, BLK), jnp.bfloat16)


def key_rows(kscr, blk):
    return kscr[pl.ds(pl.multiple_of(blk * BLK, BLK), BLK), :]


def add_block(blk, masks, kscr, vscr, qs, acc, m):
    tiles = qs.shape[0]
    scores, weights = {}, {}
    for i in range(tiles + AHEAD + 1):
        if i < tiles:
            scores[i] = jnp.dot(key_rows(kscr, blk), qs[i], preferred_element_type=jnp.float32)
        j = i - AHEAD
        if 0 <= j < tiles:
            sc = scores.pop(j)
            if masks is not None:
                sc = jnp.where(masks[j // HPD], sc, NEG)
            weights[j] = jnp.exp(sc - m[j]).astype(jnp.bfloat16)
        n = j - 1
        if 0 <= n < tiles:
            acc[n] = acc[n] + jnp.dot(
                vscr[blk], weights.pop(n), preferred_element_type=jnp.float32
            )


def add_block_exact(tile, blk, mask, kscr, vscr, qs, acc, m):
    sc = jnp.dot(key_rows(kscr, blk), qs[tile], preferred_element_type=jnp.float32)
    sc = jnp.where(mask, sc, NEG)
    m_old = m[tile]
    m_new = jnp.maximum(m_old, jnp.max(sc, axis=0, keepdims=True))
    w = jnp.exp(sc - m_new).astype(jnp.bfloat16)
    acc[tile] = acc[tile] * jnp.exp(m_old - m_new) + jnp.dot(
        vscr[blk], w, preferred_element_type=jnp.float32
    )
    m[tile] = m_new


def overflowed(acc):
    top = acc[0, HEAD_DIM : HEAD_DIM + 1, :]
    for t in range(1, acc.shape[0]):
        top = jnp.maximum(top, acc[t, HEAD_DIM : HEAD_DIM + 1, :])
    return jnp.logical_not(jnp.max(top) < LIMIT)


def suffix_low(z, r, ends):
    first = start_of(z * COLS * BLK, ends)
    gap = jnp.maximum(first - (BLK - 1) - r * BLK, 0)
    return jnp.minimum((gap + COLS * BLK - 1) // (COLS * BLK), z)


def suffix_full(jz, z, r, ends):
    last = start_of((z + 1) * COLS * BLK - 1, ends)
    return (jz < z) & (last <= (jz * COLS + r) * BLK)


def suffix_mask(jz, r, tvec, svec):
    kvec = (jz * COLS + r) * BLK + lax.broadcasted_iota(jnp.int32, (BLK, BLK), 0)
    return (kvec <= tvec) & (kvec >= svec)


def prefix_body(lens, grps, pre, s_0, s_1, s_2, q_0, q_1, q_2, q_3, qs, acc, m, kscr, vscr):
    s = lax.axis_index("seq")
    z = s // COLS
    r = s % COLS
    half = ZDIM // GROUPS
    for n in range(ZDIM):
        place(pre.at[n], n, kscr, vscr)
    for d, ref in enumerate((s_0, s_1, s_2)):
        place(ref, ZDIM + d, kscr, vscr)
    for k, ref in enumerate((q_0, q_1, q_2, q_3)):
        for h in range(HPD):
            lo = h * HEAD_DIM
            qs[k * HPD + h, 0:HEAD_DIM, :] = ref[lo : lo + HEAD_DIM, :]
            qs[k * HPD + h, HEAD_DIM:128, :] = jnp.zeros((128 - HEAD_DIM, BLK), jnp.bfloat16)
    ends = request_ends(lens)
    tvecs, svecs, gvecs = token_vectors(z, r, ends, grps)
    low = suffix_low(z, r, ends)
    tok0 = z * COLS * BLK
    seen = [jnp.bool_(False) for g in range(GROUPS)]
    begin = jnp.int32(0)
    for i in range(REQS):
        inside = (begin < tok0 + COLS * BLK) & (ends[i] > tok0)
        for g in range(GROUPS):
            seen[g] = seen[g] | (inside & (grps[i] == g))
        begin = ends[i]
    mixed = seen[0] & seen[1]
    acc[...] = jnp.zeros_like(acc)
    m[...] = jnp.full(m.shape, NEG, jnp.float32)

    for g in range(GROUPS):

        @pl.when(seen[g])
        def _():
            tops = []
            for t in range(TILES):
                sc = jnp.dot(
                    key_rows(kscr, g * half), qs[t], preferred_element_type=jnp.float32
                )
                tops.append(jnp.max(sc, axis=0, keepdims=True))
            for t in range(TILES):
                m[t] = jnp.where(gvecs[t // HPD] == g, tops[t], m[t])

    first = jnp.where(seen[0], 0, half)

    @pl.when(jnp.logical_not(mixed))
    def _():
        @pl.loop(0, half)
        def _(c):
            add_block(first + c, None, kscr, vscr, qs, acc, m)

    @pl.when(mixed)
    def _():
        @pl.loop(0, ZDIM)
        def _(c):
            masks = [jnp.broadcast_to(gv == c // half, (BLK, BLK)) for gv in gvecs]
            add_block(c, masks, kscr, vscr, qs, acc, m)

    early_end = jnp.minimum(z - low + 1, EARLY)

    @pl.loop(0, early_end)
    def _(d):
        jz = z - d
        full = suffix_full(jz, z, r, ends)

        @pl.when(full)
        def _():
            add_block(ZDIM + d, None, kscr, vscr, qs, acc, m)

        @pl.when(jnp.logical_not(full))
        def _():
            masks = [suffix_mask(jz, r, tvecs[k], svecs[k]) for k in range(COLS)]
            add_block(ZDIM + d, masks, kscr, vscr, qs, acc, m)

    @pl.when(overflowed(acc))
    def _():
        acc[...] = jnp.zeros_like(acc)
        m[...] = jnp.full(m.shape, NEG, jnp.float32)
        for k in range(COLS):

            @pl.loop(0, ZDIM)
            def _(c):
                mask = jnp.broadcast_to(gvecs[k] == c // half, (BLK, BLK))

                @pl.loop(0, HPD)
                def _(h):
                    add_block_exact(k * HPD + h, c, mask, kscr, vscr, qs, acc, m)

            @pl.loop(0, early_end)
            def _(d):
                mask = suffix_mask(z - d, r, tvecs[k], svecs[k])

                @pl.loop(0, HPD)
                def _(h):
                    add_block_exact(k * HPD + h, ZDIM + d, mask, kscr, vscr, qs, acc, m)


def write_partial(dst, acc, m, k):
    rows = lax.broadcasted_iota(jnp.int32, (16, BLK), 0)
    extra = jnp.zeros((16, BLK), jnp.float32)
    for h in range(HPD):
        t = k * HPD + h
        total_w = acc[t, HEAD_DIM : HEAD_DIM + 1, :]
        dst[h * HEAD_DIM : (h + 1) * HEAD_DIM, :] = (
            acc[t, 0:HEAD_DIM, :] * (1.0 / total_w)
        ).astype(jnp.bfloat16)
        lse = m[t] + jnp.log(total_w)
        for j in range(3):
            part = lse.astype(jnp.bfloat16).astype(jnp.float32)
            extra = jnp.where(rows == 3 * h + j, part, extra)
            lse = lse - part
    dst[QROWS:PROWS, :] = extra.astype(jnp.bfloat16)


def suffix_tiles(k0, lens, grps, qs, acc_in, m_in, keep, send, kscr, vscr, acc, m):
    s = lax.axis_index("seq")
    z = s // COLS
    r = s % COLS
    ends = request_ends(lens)
    tvecs, svecs, unused = token_vectors(z, r, ends, grps)
    end = z - suffix_low(z, r, ends) + 1
    acc[...] = acc_in[...]
    m[...] = m_in[...]

    def step(d, c):
        jz = z - d
        full = suffix_full(jz, z, r, ends)

        @pl.when(full)
        def _():
            add_block(d - EARLY, None, kscr, vscr, qs, acc, m)

        @pl.when(jnp.logical_not(full))
        def _():
            masks = [suffix_mask(jz, r, tvecs[k0 + k], svecs[k0 + k]) for k in range(2)]
            add_block(d - EARLY, masks, kscr, vscr, qs, acc, m)

        return c

    lax.fori_loop(EARLY, end, step, 0)

    @pl.when(overflowed(acc))
    def _():
        acc[...] = acc_in[...]
        m[...] = m_in[...]
        for k in range(2):

            def exact_step(d, c):
                mask = suffix_mask(z - d, r, tvecs[k0 + k], svecs[k0 + k])

                @pl.loop(0, HPD)
                def _(h):
                    add_block_exact(k * HPD + h, d - EARLY, mask, kscr, vscr, qs, acc, m)

                return c

            lax.fori_loop(EARLY, end, exact_step, 0)

    write_partial(keep, acc, m, 0)
    write_partial(send, acc, m, 1)


def far_body(lens, grps, *refs):
    late = refs[:LATE]
    qs, acc_in, m_in, keep, send, kscr, vscr, acc, m = refs[LATE:]
    for n in range(LATE):
        place(late[n], n, kscr, vscr)
    suffix_tiles(2, lens, grps, qs, acc_in, m_in, keep, send, kscr, vscr, acc, m)


def near_body(lens, grps, kscr, vscr, qs, acc_in, m_in, keep, send, acc, m):
    suffix_tiles(0, lens, grps, qs, acc_in, m_in, keep, send, kscr, vscr, acc, m)


def spread_body(keys, values, out, sem):
    copies = []
    for n in range(ZDIM):
        copies.append(
            pltpu.make_async_copy(keys, out.at[n, pl.ds(0, HEAD_DIM)], sem.at[0, n])
        )
        copies.append(
            pltpu.make_async_copy(values, out.at[n, pl.ds(HEAD_DIM, HEAD_DIM)], sem.at[1, n])
        )
    for copy in copies:
        copy.start()
    for copy in copies:
        copy.wait()


def project_body(lens, hidden, gain, wq_far, wk, wv, freq, q_out, kv_out, k_out, v_out, wq, sem):
    fetch = pltpu.make_async_copy(wq_far, wq, sem)
    fetch.start()
    ends = request_ends(lens)
    tvec = lax.axis_index("seq") * BLK + lax.broadcasted_iota(jnp.int32, (1, BLK), 1)
    svec = jnp.zeros((1, BLK), jnp.int32)
    for i in range(REQS - 1):
        svec = jnp.where(tvec >= ends[i], ends[i], svec)
    positions = (PRE_LEN + tvec - svec).astype(jnp.float32)
    angles = freq[...] * positions
    c = jnp.cos(angles)
    sn = jnp.sin(angles)
    wide = hidden[...].astype(jnp.float32)
    mean_square = jnp.mean(wide * wide, axis=-1, keepdims=True)
    normed = (
        wide * lax.rsqrt(mean_square + 1e-05) * gain[...].reshape(1, wide.shape[1])
    ).astype(jnp.bfloat16)

    def proj(w):
        return lax.dot_general(
            w[...], normed, (((1,), (1,)), ((), ())), preferred_element_type=jnp.float32
        )

    hf = HEAD_DIM // 2

    def rotate(a, b):
        return a * c - b * sn, b * c + a * sn

    kf = proj(wk)
    ka, kb = rotate(kf[0:hf], kf[hf:HEAD_DIM])
    kt = jnp.concatenate([ka, kb], axis=0).astype(jnp.bfloat16)
    vt = proj(wv).astype(jnp.bfloat16)
    k_out[...] = kt
    v_out[...] = vt
    kv_out[0:HEAD_DIM, :] = kt
    kv_out[HEAD_DIM : 2 * HEAD_DIM, :] = vt
    fetch.wait()
    qf = proj(wq)
    for h in range(HPD):
        lo = h * HEAD_DIM
        qa, qb = rotate(qf[lo : lo + hf], qf[lo + hf : lo + HEAD_DIM])
        q_out[lo : lo + HEAD_DIM, :] = (
            jnp.concatenate([qa, qb], axis=0) * HEAD_DIM ** (-0.5)
        ).astype(jnp.bfloat16)


def merged(*parts):
    tails = [p[QROWS:PROWS, :].astype(jnp.float32) for p in parts]
    outs, lses = [], []
    for h in range(HPD):
        ls = [
            t[3 * h : 3 * h + 1] + t[3 * h + 1 : 3 * h + 2] + t[3 * h + 2 : 3 * h + 3]
            for t in tails
        ]
        top = ls[0]
        for x in ls[1:]:
            top = jnp.maximum(top, x)
        ws = [jnp.exp(x - top) for x in ls]
        tot = ws[0]
        for x in ws[1:]:
            tot = tot + x
        rows = slice(h * HEAD_DIM, (h + 1) * HEAD_DIM)
        out = parts[0][rows, :].astype(jnp.float32) * (ws[0] / tot)
        for p, w in zip(parts[1:], ws[1:]):
            out = out + p[rows, :].astype(jnp.float32) * (w / tot)
        outs.append(out.astype(jnp.bfloat16))
        lses.append(top + jnp.log(tot))
    return outs, lses


def merge_far_body(keep, recv, dst):
    outs, lses = merged(keep[...], recv[...])
    extra = jnp.zeros((16, BLK), jnp.float32)
    rows = lax.broadcasted_iota(jnp.int32, (16, BLK), 0)
    for h in range(HPD):
        lse = lses[h]
        for j in range(3):
            part = lse.astype(jnp.bfloat16).astype(jnp.float32)
            extra = jnp.where(rows == 3 * h + j, part, extra)
            lse = lse - part
    dst[...] = jnp.concatenate(outs + [extra.astype(jnp.bfloat16)], axis=0)


def project_out_body(own, near, w, out):
    outs, unused = merged(own[...], near[...])
    attended = jnp.concatenate(outs, axis=0)
    out[...] = lax.dot_general(
        w[...], attended, (((0,), (0,)), ((), ())), preferred_element_type=jnp.float32
    ).astype(jnp.bfloat16)


def final_body(parts, residual, out):
    total = residual[...].astype(jnp.float32)
    acc = parts[0].astype(jnp.float32)
    for i in range(1, parts.shape[0]):
        acc = acc + parts[i].astype(jnp.float32)
    out[...] = (acc + total).astype(jnp.bfloat16)


def shape_of(*dims):
    return jax.ShapeDtypeStruct(dims, jnp.bfloat16)


VMEM_SPEC = pl.BlockSpec(memory_space=pltpu.VMEM)
HBM_SPEC = pl.BlockSpec(memory_space=pltpu.HBM)
SMEM_SPEC = pl.BlockSpec(memory_space=pltpu.SMEM)
PARAMS = pltpu.CompilerParams(vmem_limit_bytes=20 * 1024 * 1024)


def per_device(
    hidden_in,
    norm_gain,
    w_query,
    w_key,
    w_value,
    w_out,
    prefix_keys,
    prefix_values,
    lengths,
    groups,
):
    columns_of_z = [list(range(c, ZDIM * COLS, COLS)) for c in range(COLS)]

    def along_z(x):
        return lax.all_to_all(
            x, "seq", split_axis=0, concat_axis=0, tiled=True, axis_index_groups=columns_of_z
        )

    pre = along_z(
        pl.pallas_call(
            spread_body,
            out_shape=shape_of(ZDIM, 2 * HEAD_DIM, BLK),
            in_specs=[HBM_SPEC] * 2,
            out_specs=HBM_SPEC,
            scratch_shapes=[pltpu.SemaphoreType.DMA((2, ZDIM))],
            compiler_params=PARAMS,
            name="spread_prefix",
        )(prefix_keys.T, prefix_values.T)
    )

    half_dim = HEAD_DIM // 2
    frequency = jnp.power(
        jnp.float32(1000000.0), -jnp.arange(half_dim, dtype=jnp.float32) / half_dim
    )
    q_t, suf_own, key_t, value_t = pl.pallas_call(
        project_body,
        out_shape=(
            shape_of(QROWS, BLK),
            shape_of(2 * HEAD_DIM, BLK),
            shape_of(HEAD_DIM, BLK),
            shape_of(HEAD_DIM, BLK),
        ),
        in_specs=[SMEM_SPEC] + [VMEM_SPEC] * 2 + [HBM_SPEC] + [VMEM_SPEC] * 3,
        out_specs=(VMEM_SPEC,) * 4,
        scratch_shapes=[
            pltpu.VMEM((QROWS, w_query.shape[0]), jnp.bfloat16),
            pltpu.SemaphoreType.DMA,
        ],
        compiler_params=PARAMS,
        name="project_in",
    )(
        lengths,
        hidden_in,
        norm_gain,
        w_query.T,
        w_key.T,
        w_value.T,
        frequency[:, None],
    )
    q_all = [q_t] + [
        lax.ppermute(q_t, "seq", [(i, i ^ k) for i in range(32)]) for k in range(1, COLS)
    ]

    def later(x, d):
        return lax.ppermute(
            x, "seq", [(i, i + COLS * d) for i in range(COLS * (ZDIM - d))]
        )

    suf = [suf_own] + [later(suf_own, d) for d in range(1, ZDIM - 1)]
    scalars = (lengths, groups)
    qs, acc, top = pl.pallas_call(
        prefix_body,
        out_shape=(
            shape_of(TILES, 128, BLK),
            jax.ShapeDtypeStruct((TILES, 96, BLK), jnp.float32),
            jax.ShapeDtypeStruct((TILES, 1, BLK), jnp.float32),
        ),
        in_specs=[SMEM_SPEC] * 2 + [VMEM_SPEC] * (1 + EARLY + COLS),
        out_specs=(VMEM_SPEC,) * 3,
        scratch_shapes=[
            pltpu.VMEM(((ZDIM + EARLY) * BLK, 128), jnp.bfloat16),
            pltpu.VMEM((ZDIM + EARLY, 96, BLK), jnp.bfloat16),
        ],
        compiler_params=PARAMS,
        cost_estimate=pl.CostEstimate(
            flops=6 * 10**9, transcendentals=6 * 10**6, bytes_accessed=4 * 10**6
        ),
        name="attend_prefix",
    )(*scalars, pre, *suf[:EARLY], *q_all)
    halves = TILES // 2
    half_scratch = [
        pltpu.VMEM((halves, 96, BLK), jnp.float32),
        pltpu.VMEM((halves, 1, BLK), jnp.float32),
    ]

    def half_specs(at):
        return [
            pl.BlockSpec((halves, 128, BLK), lambda i: (at, 0, 0)),
            pl.BlockSpec((halves, 96, BLK), lambda i: (at, 0, 0)),
            pl.BlockSpec((halves, 1, BLK), lambda i: (at, 0, 0)),
        ]

    core_pairs = [(i, i ^ 1) for i in range(32)]
    keep_far, send_far, keys, values = pl.pallas_call(
        far_body,
        grid=(1,),
        out_shape=(
            shape_of(PROWS, BLK),
            shape_of(PROWS, BLK),
            shape_of(LATE * BLK, 128),
            shape_of(LATE, 96, BLK),
        ),
        in_specs=[SMEM_SPEC] * 2 + [VMEM_SPEC] * LATE + half_specs(1),
        out_specs=(VMEM_SPEC,) * 4,
        scratch_shapes=half_scratch,
        compiler_params=PARAMS,
        cost_estimate=pl.CostEstimate(
            flops=5 * 10**9, transcendentals=5 * 10**6, bytes_accessed=4 * 10**6
        ),
        name="attend_suffix_far",
    )(*scalars, *suf[EARLY:], qs, acc, top)

    def merge_two(one, two):
        return pl.pallas_call(
            merge_far_body,
            out_shape=shape_of(PROWS, BLK),
            in_specs=[VMEM_SPEC] * 2,
            out_specs=VMEM_SPEC,
            compiler_params=PARAMS,
            name="merge_two",
        )(one, two)

    far = merge_two(keep_far, lax.ppermute(send_far, "seq", core_pairs))
    far, values = lax.optimization_barrier((far, values))
    x_recv = lax.ppermute(far, "seq", [(i, i ^ 2) for i in range(32)])
    keep_near, send_near = pl.pallas_call(
        near_body,
        grid=(1,),
        out_shape=(shape_of(PROWS, BLK), shape_of(PROWS, BLK)),
        in_specs=[SMEM_SPEC] * 2 + [VMEM_SPEC] * 2 + half_specs(0),
        out_specs=(VMEM_SPEC, VMEM_SPEC),
        scratch_shapes=half_scratch,
        compiler_params=PARAMS,
        cost_estimate=pl.CostEstimate(
            flops=5 * 10**9, transcendentals=5 * 10**6, bytes_accessed=4 * 10**6
        ),
        name="attend_suffix_near",
    )(*scalars, keys, values, qs, acc, top)
    core_recv = lax.ppermute(send_near, "seq", core_pairs)
    width = w_out.shape[1]
    projected = pl.pallas_call(
        project_out_body,
        out_shape=shape_of(width, BLK),
        in_specs=[VMEM_SPEC] * 3,
        out_specs=VMEM_SPEC,
        compiler_params=PARAMS,
        name="project_out",
    )(merge_two(keep_near, x_recv), core_recv, w_out)
    tp = lax.axis_size("tp")
    columns = width // tp
    parts = lax.all_to_all(
        projected.reshape(tp, columns, BLK), "tp", split_axis=0, concat_axis=0, tiled=True
    )
    residual = lax.dynamic_slice_in_dim(
        hidden_in, lax.axis_index("tp") * columns, columns, 1
    ).T
    hidden_t = pl.pallas_call(
        final_body,
        out_shape=shape_of(columns, BLK),
        in_specs=[VMEM_SPEC] * 2,
        out_specs=VMEM_SPEC,
        compiler_params=PARAMS,
        name="final_sum",
    )(parts, residual)
    return (hidden_t.T, key_t.T, value_t.T)


def solution(mesh):
    return jax.shard_map(
        per_device,
        mesh=mesh,
        in_specs=(
            P("seq", None),
            P(),
            P(None, "tp"),
            P(None, "tp"),
            P(None, "tp"),
            P("tp", None),
            P("seq", "tp"),
            P("seq", "tp"),
            P(),
            P(),
        ),
        out_specs=(P("seq", "tp"), P("seq", "tp"), P("seq", "tp")),
        check_vma=False,
    )
```

```python
import jax
import jax.numpy as jnp
from jax import lax
from jax.experimental import pallas as pl
from jax.experimental.pallas import tpu as pltpu
from jax.sharding import PartitionSpec as P

HEAD_DIM = 80
GROUPS = 2
REQS = 4
BLK = 256
PRE_LEN = 4096
COLS = 4
ZDIM = 8
HPD = 4
QROWS = HPD * HEAD_DIM
PROWS = QROWS + 16
NEG = -1e30
LIMIT = 1e30
FLOOR = 1e-20
AHEAD = 4
TILES = COLS * HPD
HALF = ZDIM // GROUPS
KV_ROWS = 4 * HEAD_DIM


def request_ends(lens):
    ends = []
    total = 0
    for i in range(REQS):
        total = total + lens[i]
        ends.append(total)
    return ends


def start_of(p, ends):
    st = jnp.int32(0)
    for i in range(REQS - 1):
        st = jnp.where(p >= ends[i], ends[i], st)
    return st


def token_vectors(z, r, ends, grps):
    tvecs, svecs, gvecs = [], [], []
    for k in range(COLS):
        tok0 = (z * COLS + (r ^ k)) * BLK
        tvec = tok0 + lax.broadcasted_iota(jnp.int32, (1, BLK), 1)
        svec = jnp.zeros((1, BLK), jnp.int32)
        gvec = jnp.zeros((1, BLK), jnp.int32) + grps[0]
        for i in range(REQS - 1):
            svec = jnp.where(tvec >= ends[i], ends[i], svec)
            gvec = jnp.where(tvec >= ends[i], grps[i + 1], gvec)
        tvecs.append(tvec)
        svecs.append(svec)
        gvecs.append(gvec)
    return tvecs, svecs, gvecs


def place(keys, values, n, kscr, vscr):
    kt = jnp.concatenate([keys, jnp.zeros((128 - HEAD_DIM, BLK), jnp.bfloat16)], axis=0)
    kscr[n * BLK : (n + 1) * BLK, :] = kt.T
    vscr[n, 0:HEAD_DIM, :] = values
    vscr[n, HEAD_DIM:96, :] = jnp.ones((96 - HEAD_DIM, BLK), jnp.bfloat16)


def key_rows(kscr, blk):
    return kscr[pl.ds(pl.multiple_of(blk * BLK, BLK), BLK), :]


def add_block(blks, masks, tiles, kscr, vscr, qs, acc, m):
    count = len(tiles)
    scores, weights = {}, {}
    for i in range(count + AHEAD + 1):
        if i < count:
            t = tiles[i]
            scores[i] = jnp.dot(
                key_rows(kscr, blks[t // HPD]), qs[t], preferred_element_type=jnp.float32
            )
        j = i - AHEAD
        if 0 <= j < count:
            t = tiles[j]
            sc = scores.pop(j)
            if masks is not None:
                sc = jnp.where(masks[t // HPD], sc, NEG)
            weights[j] = jnp.exp(sc - m[t]).astype(jnp.bfloat16)
        n = j - 1
        if 0 <= n < count:
            t = tiles[n]
            acc[t] = acc[t] + jnp.dot(
                vscr[blks[t // HPD]], weights.pop(n), preferred_element_type=jnp.float32
            )


def add_block_exact(tile, blk, mask, kscr, vscr, qs, acc, m):
    sc = jnp.dot(key_rows(kscr, blk), qs[tile], preferred_element_type=jnp.float32)
    sc = jnp.where(mask, sc, NEG)
    m_old = m[tile]
    m_new = jnp.maximum(m_old, jnp.max(sc, axis=0, keepdims=True))
    w = jnp.exp(sc - m_new).astype(jnp.bfloat16)
    acc[tile] = acc[tile] * jnp.exp(m_old - m_new) + jnp.dot(
        vscr[blk], w, preferred_element_type=jnp.float32
    )
    m[tile] = m_new


def out_of_range(acc):
    top = acc[0, HEAD_DIM : HEAD_DIM + 1, :]
    least = top
    for t in range(1, acc.shape[0]):
        row = acc[t, HEAD_DIM : HEAD_DIM + 1, :]
        top = jnp.maximum(top, row)
        least = jnp.minimum(least, row)
    return jnp.logical_not((jnp.max(top) < LIMIT) & (jnp.min(least) > FLOOR))


def suffix_low(z, r, ends):
    first = start_of(z * COLS * BLK, ends)
    gap = jnp.maximum(first - (BLK - 1) - r * BLK, 0)
    return jnp.minimum((gap + COLS * BLK - 1) // (COLS * BLK), z)


def suffix_full(jz, z, r, ends):
    last = start_of((z + 1) * COLS * BLK - 1, ends)
    return (jz < z) & (last <= (jz * COLS + r) * BLK)


def suffix_mask(jz, r, tvec, svec):
    kvec = (jz * COLS + r) * BLK + lax.broadcasted_iota(jnp.int32, (BLK, BLK), 0)
    return (kvec <= tvec) & (kvec >= svec)


def own_body(lens, grps, pre_keys, keys, values, q_0, q_1, q_2, q_3, qs, acc, m, kscr, vscr):
    s = lax.axis_index("seq")
    z = s // COLS
    r = s % COLS
    for k, ref in enumerate((q_0, q_1, q_2, q_3)):
        for h in range(HPD):
            lo = h * HEAD_DIM
            qs[k * HPD + h, 0:HEAD_DIM, :] = ref[lo : lo + HEAD_DIM, :]
            qs[k * HPD + h, HEAD_DIM:128, :] = jnp.zeros((128 - HEAD_DIM, BLK), jnp.bfloat16)
    place(pre_keys[...], values[...], 0, kscr, vscr)
    place(keys[...], values[...], 1, kscr, vscr)
    ends = request_ends(lens)
    tvecs, svecs, unused = token_vectors(z, r, ends, grps)
    for t in range(TILES):
        sc = jnp.dot(key_rows(kscr, 0), qs[t], preferred_element_type=jnp.float32)
        m[t] = jnp.max(sc, axis=0, keepdims=True)
    acc[...] = jnp.zeros_like(acc)
    masks = [suffix_mask(z, r, tvecs[k], svecs[k]) for k in range(COLS)]
    add_block([1] * COLS, masks, list(range(TILES)), kscr, vscr, qs, acc, m)


def write_partial(dst, acc, m, k):
    rows = lax.broadcasted_iota(jnp.int32, (16, BLK), 0)
    extra = jnp.zeros((16, BLK), jnp.float32)
    for h in range(HPD):
        t = k * HPD + h
        total_w = acc[t, HEAD_DIM : HEAD_DIM + 1, :]
        dst[h * HEAD_DIM : (h + 1) * HEAD_DIM, :] = (
            acc[t, 0:HEAD_DIM, :] * (1.0 / total_w)
        ).astype(jnp.bfloat16)
        lse = m[t] + jnp.log(total_w)
        for j in range(3):
            part = lse.astype(jnp.bfloat16).astype(jnp.float32)
            extra = jnp.where(rows == 3 * h + j, part, extra)
            lse = lse - part
    dst[QROWS:PROWS, :] = extra.astype(jnp.bfloat16)


def attend_tiles(k0, lens, grps, qs, acc_in, m_in, keep, send, kscr, vscr, acc, m):
    s = lax.axis_index("seq")
    z = s // COLS
    r = s % COLS
    ends = request_ends(lens)
    tvecs, svecs, gvecs = [v[k0 : k0 + 2] for v in token_vectors(z, r, ends, grps)]
    low = suffix_low(z, r, ends)
    tiles = list(range(2 * HPD))
    acc[...] = acc_in[...]
    m[...] = m_in[...]
    group, both = [], []
    for k in range(2):
        tok0 = (z * COLS + (r ^ (k0 + k))) * BLK
        seen = [jnp.bool_(False) for g in range(GROUPS)]
        begin = jnp.int32(0)
        for i in range(REQS):
            inside = (begin < tok0 + BLK) & (ends[i] > tok0)
            for g in range(GROUPS):
                seen[g] = seen[g] | (inside & (grps[i] == g))
            begin = ends[i]
        group.append(jnp.where(seen[0], 0, 1))
        both.append(seen[0] & seen[1])
    any_both = both[0] | both[1]

    @pl.when(jnp.logical_not(any_both))
    def _():
        @pl.loop(0, HALF)
        def _(c):
            blks = [ZDIM + g * HALF + c for g in group]
            add_block(blks, None, tiles, kscr, vscr, qs, acc, m)

    @pl.when(any_both)
    def _():
        @pl.loop(0, HALF)
        def _(c):
            blks = [ZDIM + g * HALF + c for g in group]
            masks = [jnp.broadcast_to(gvecs[k] == group[k], (BLK, BLK)) for k in range(2)]
            add_block(blks, masks, tiles, kscr, vscr, qs, acc, m)

    for k in range(2):

        @pl.when(both[k])
        def _():
            @pl.loop(0, HALF)
            def _(c):
                blks = [ZDIM + HALF + c] * 2
                masks = [jnp.broadcast_to(gvecs[k] == 1, (BLK, BLK))] * 2
                part = tiles[k * HPD : (k + 1) * HPD]
                add_block(blks, masks, part, kscr, vscr, qs, acc, m)

    @pl.loop(low, z)
    def _(jz):
        full = suffix_full(jz, z, r, ends)

        @pl.when(full)
        def _():
            add_block([jz] * 2, None, tiles, kscr, vscr, qs, acc, m)

        @pl.when(jnp.logical_not(full))
        def _():
            masks = [suffix_mask(jz, r, tvecs[k], svecs[k]) for k in range(2)]
            add_block([jz] * 2, masks, tiles, kscr, vscr, qs, acc, m)

    @pl.when(out_of_range(acc))
    def _():
        acc[...] = jnp.zeros_like(acc)
        m[...] = jnp.full(m.shape, NEG, jnp.float32)
        for k in range(2):
            for g in range(GROUPS):

                @pl.when((group[k] == g) | both[k])
                def _():
                    mask = jnp.broadcast_to(gvecs[k] == g, (BLK, BLK))

                    @pl.loop(0, HALF)
                    def _(c):
                        blk = ZDIM + g * HALF + c

                        @pl.loop(0, HPD)
                        def _(h):
                            add_block_exact(k * HPD + h, blk, mask, kscr, vscr, qs, acc, m)

            @pl.loop(low, z + 1)
            def _(jz):
                mask = suffix_mask(jz, r, tvecs[k], svecs[k])

                @pl.loop(0, HPD)
                def _(h):
                    add_block_exact(k * HPD + h, jz, mask, kscr, vscr, qs, acc, m)

    write_partial(keep, acc, m, 0)
    write_partial(send, acc, m, 1)


def far_body(lens, grps, kv, qs, acc_in, m_in, keep, send, kscr, vscr, acc, m):
    s = lax.axis_index("seq")
    z = s // COLS
    ends = request_ends(lens)
    low = suffix_low(z, s % COLS, ends)
    tok0 = z * COLS * BLK
    for g in range(GROUPS):
        seen = jnp.bool_(False)
        begin = jnp.int32(0)
        for i in range(REQS):
            inside = (begin < tok0 + COLS * BLK) & (ends[i] > tok0)
            seen = seen | (inside & (grps[i] == g))
            begin = ends[i]

        @pl.when(seen)
        def _():
            for c in range(HALF):
                n = g * HALF + c
                place(
                    kv[n, 2 * HEAD_DIM : 3 * HEAD_DIM, :],
                    kv[n, 3 * HEAD_DIM : 4 * HEAD_DIM, :],
                    ZDIM + n,
                    kscr,
                    vscr,
                )

    for n in range(ZDIM):

        @pl.when((n >= low) & (n <= z))
        def _():
            place(kv[n, 0:HEAD_DIM, :], kv[n, HEAD_DIM : 2 * HEAD_DIM, :], n, kscr, vscr)

    attend_tiles(2, lens, grps, qs, acc_in, m_in, keep, send, kscr, vscr, acc, m)


def near_body(lens, grps, kscr, vscr, qs, acc_in, m_in, keep, send, acc, m):
    attend_tiles(0, lens, grps, qs, acc_in, m_in, keep, send, kscr, vscr, acc, m)


def project_body(
    lens,
    gain,
    freq,
    hidden_far,
    wk_far,
    wv_far,
    wq_far,
    pre_keys,
    pre_values,
    q_out,
    kv_out,
    k_out,
    v_out,
    hidden,
    wk,
    wv,
    wq,
    stage,
    sem,
    slot_sem,
):
    moves = (
        (hidden_far, hidden),
        (wk_far, wk),
        (wv_far, wv),
        (pre_keys, stage.at[pl.ds(2 * HEAD_DIM, HEAD_DIM)]),
        (pre_values, stage.at[pl.ds(3 * HEAD_DIM, HEAD_DIM)]),
        (wq_far, wq),
    )
    fetches = [
        pltpu.make_async_copy(src, dst, sem.at[n]) for n, (src, dst) in enumerate(moves)
    ]
    for fetch in fetches:
        fetch.start()
    ends = request_ends(lens)
    tvec = lax.axis_index("seq") * BLK + lax.broadcasted_iota(jnp.int32, (1, BLK), 1)
    svec = jnp.zeros((1, BLK), jnp.int32)
    for i in range(REQS - 1):
        svec = jnp.where(tvec >= ends[i], ends[i], svec)
    positions = (PRE_LEN + tvec - svec).astype(jnp.float32)
    angles = freq[...] * positions
    c = jnp.cos(angles)
    sn = jnp.sin(angles)
    fetches[0].wait()
    wide = hidden[...].astype(jnp.float32)
    mean_square = jnp.mean(wide * wide, axis=-1, keepdims=True)
    normed = (
        wide * lax.rsqrt(mean_square + 1e-05) * gain[...].reshape(1, wide.shape[1])
    ).astype(jnp.bfloat16)

    def proj(w):
        return lax.dot_general(
            w[...], normed, (((1,), (1,)), ((), ())), preferred_element_type=jnp.float32
        )

    hf = HEAD_DIM // 2

    def rotate(a, b):
        return a * c - b * sn, b * c + a * sn

    fetches[1].wait()
    kf = proj(wk)
    ka, kb = rotate(kf[0:hf], kf[hf:HEAD_DIM])
    kt = jnp.concatenate([ka, kb], axis=0).astype(jnp.bfloat16)
    fetches[2].wait()
    vt = proj(wv).astype(jnp.bfloat16)
    k_out[...] = kt
    v_out[...] = vt
    stage[0:HEAD_DIM, :] = kt
    stage[HEAD_DIM : 2 * HEAD_DIM, :] = vt
    fetches[3].wait()
    fetches[4].wait()
    slots = [
        pltpu.make_async_copy(stage, kv_out.at[n], slot_sem.at[n]) for n in range(ZDIM)
    ]
    for slot in slots:
        slot.start()
    fetches[5].wait()
    qf = proj(wq)
    for h in range(HPD):
        lo = h * HEAD_DIM
        qa, qb = rotate(qf[lo : lo + hf], qf[lo + hf : lo + HEAD_DIM])
        q_out[lo : lo + HEAD_DIM, :] = (
            jnp.concatenate([qa, qb], axis=0) * HEAD_DIM ** (-0.5)
        ).astype(jnp.bfloat16)
    for slot in slots:
        slot.wait()


def merged(*parts):
    tails = [p[QROWS:PROWS, :].astype(jnp.float32) for p in parts]
    outs, lses = [], []
    for h in range(HPD):
        ls = [
            t[3 * h : 3 * h + 1] + t[3 * h + 1 : 3 * h + 2] + t[3 * h + 2 : 3 * h + 3]
            for t in tails
        ]
        top = ls[0]
        for x in ls[1:]:
            top = jnp.maximum(top, x)
        ws = [jnp.exp(x - top) for x in ls]
        tot = ws[0]
        for x in ws[1:]:
            tot = tot + x
        rows = slice(h * HEAD_DIM, (h + 1) * HEAD_DIM)
        out = parts[0][rows, :].astype(jnp.float32) * (ws[0] / tot)
        for p, w in zip(parts[1:], ws[1:]):
            out = out + p[rows, :].astype(jnp.float32) * (w / tot)
        outs.append(out.astype(jnp.bfloat16))
        lses.append(top + jnp.log(tot))
    return outs, lses


def merge_far_body(keep, recv, dst):
    outs, lses = merged(keep[...], recv[...])
    extra = jnp.zeros((16, BLK), jnp.float32)
    rows = lax.broadcasted_iota(jnp.int32, (16, BLK), 0)
    for h in range(HPD):
        lse = lses[h]
        for j in range(3):
            part = lse.astype(jnp.bfloat16).astype(jnp.float32)
            extra = jnp.where(rows == 3 * h + j, part, extra)
            lse = lse - part
    dst[...] = jnp.concatenate(outs + [extra.astype(jnp.bfloat16)], axis=0)


def project_out_body(own, near, w, out):
    outs, unused = merged(own[...], near[...])
    attended = jnp.concatenate(outs, axis=0)
    out[...] = lax.dot_general(
        w[...], attended, (((0,), (0,)), ((), ())), preferred_element_type=jnp.float32
    ).astype(jnp.bfloat16)


def final_body(parts, residual, out):
    total = residual[...].astype(jnp.float32)
    acc = parts[0].astype(jnp.float32)
    for i in range(1, parts.shape[0]):
        acc = acc + parts[i].astype(jnp.float32)
    out[...] = (acc + total).astype(jnp.bfloat16)


def shape_of(*dims):
    return jax.ShapeDtypeStruct(dims, jnp.bfloat16)


VMEM_SPEC = pl.BlockSpec(memory_space=pltpu.VMEM)
HBM_SPEC = pl.BlockSpec(memory_space=pltpu.HBM)
SMEM_SPEC = pl.BlockSpec(memory_space=pltpu.SMEM)
PARAMS = pltpu.CompilerParams(vmem_limit_bytes=20 * 1024 * 1024)


def per_device(
    hidden_in,
    norm_gain,
    w_query,
    w_key,
    w_value,
    w_out,
    prefix_keys,
    prefix_values,
    lengths,
    groups,
):
    columns_of_z = [list(range(c, ZDIM * COLS, COLS)) for c in range(COLS)]

    def along_z(x):
        return lax.all_to_all(
            x, "seq", split_axis=0, concat_axis=0, tiled=True, axis_index_groups=columns_of_z
        )

    half_dim = HEAD_DIM // 2
    frequency = jnp.power(
        jnp.float32(1000000.0), -jnp.arange(half_dim, dtype=jnp.float32) / half_dim
    )
    q_t, slots, key_t, value_t = pl.pallas_call(
        project_body,
        out_shape=(
            shape_of(QROWS, BLK),
            shape_of(ZDIM, KV_ROWS, BLK),
            shape_of(HEAD_DIM, BLK),
            shape_of(HEAD_DIM, BLK),
        ),
        in_specs=[SMEM_SPEC] + [VMEM_SPEC] * 2 + [HBM_SPEC] * 6,
        out_specs=(VMEM_SPEC, HBM_SPEC, VMEM_SPEC, VMEM_SPEC),
        scratch_shapes=[
            pltpu.VMEM(hidden_in.shape, jnp.bfloat16),
            pltpu.VMEM((HEAD_DIM, w_query.shape[0]), jnp.bfloat16),
            pltpu.VMEM((HEAD_DIM, w_query.shape[0]), jnp.bfloat16),
            pltpu.VMEM((QROWS, w_query.shape[0]), jnp.bfloat16),
            pltpu.VMEM((KV_ROWS, BLK), jnp.bfloat16),
            pltpu.SemaphoreType.DMA((6,)),
            pltpu.SemaphoreType.DMA((ZDIM,)),
        ],
        compiler_params=PARAMS,
        name="project_in",
    )(
        lengths,
        norm_gain,
        frequency[:, None],
        *[
            pltpu.with_memory_space_constraint(x, pltpu.HBM)
            for x in (
                hidden_in,
                w_key.T,
                w_value.T,
                w_query.T,
                prefix_keys.T,
                prefix_values.T,
            )
        ],
    )
    q_all = [q_t] + [
        lax.ppermute(q_t, "seq", [(i, i ^ k) for i in range(32)]) for k in range(1, COLS)
    ]

    kv = along_z(slots)
    scalars = (lengths, groups)
    qs, acc, top = pl.pallas_call(
        own_body,
        out_shape=(
            shape_of(TILES, 128, BLK),
            jax.ShapeDtypeStruct((TILES, 96, BLK), jnp.float32),
            jax.ShapeDtypeStruct((TILES, 1, BLK), jnp.float32),
        ),
        in_specs=[SMEM_SPEC] * 2 + [VMEM_SPEC] * (3 + COLS),
        out_specs=(VMEM_SPEC,) * 3,
        scratch_shapes=[
            pltpu.VMEM((2 * BLK, 128), jnp.bfloat16),
            pltpu.VMEM((2, 96, BLK), jnp.bfloat16),
        ],
        compiler_params=PARAMS,
        cost_estimate=pl.CostEstimate(
            flops=3 * 10**9, transcendentals=3 * 10**6, bytes_accessed=4 * 10**6
        ),
        name="attend_own",
    )(*scalars, prefix_keys.T, key_t, value_t, *q_all)
    qs = pltpu.with_memory_space_constraint(qs, pltpu.HBM)
    halves = TILES // 2
    half_scratch = [
        pltpu.VMEM((halves, 96, BLK), jnp.float32),
        pltpu.VMEM((halves, 1, BLK), jnp.float32),
    ]

    def half_specs(at):
        return [
            pl.BlockSpec((halves, 128, BLK), lambda i: (at, 0, 0)),
            pl.BlockSpec((halves, 96, BLK), lambda i: (at, 0, 0)),
            pl.BlockSpec((halves, 1, BLK), lambda i: (at, 0, 0)),
        ]

    core_pairs = [(i, i ^ 1) for i in range(32)]
    keep_far, send_far, keys, values = pl.pallas_call(
        far_body,
        grid=(1,),
        out_shape=(
            shape_of(PROWS, BLK),
            shape_of(PROWS, BLK),
            shape_of(2 * ZDIM * BLK, 128),
            shape_of(2 * ZDIM, 96, BLK),
        ),
        in_specs=[SMEM_SPEC] * 2 + [VMEM_SPEC] + half_specs(1),
        out_specs=(VMEM_SPEC,) * 4,
        scratch_shapes=half_scratch,
        compiler_params=PARAMS,
        cost_estimate=pl.CostEstimate(
            flops=5 * 10**9, transcendentals=5 * 10**6, bytes_accessed=4 * 10**6
        ),
        name="attend_far",
    )(*scalars, kv, qs, acc, top)

    def merge_two(one, two):
        return pl.pallas_call(
            merge_far_body,
            out_shape=shape_of(PROWS, BLK),
            in_specs=[VMEM_SPEC] * 2,
            out_specs=VMEM_SPEC,
            compiler_params=PARAMS,
            name="merge_two",
        )(one, two)

    far = merge_two(keep_far, lax.ppermute(send_far, "seq", core_pairs))
    far, values = lax.optimization_barrier((far, values))
    x_recv = lax.ppermute(far, "seq", [(i, i ^ 2) for i in range(32)])
    keep_near, send_near = pl.pallas_call(
        near_body,
        grid=(1,),
        out_shape=(shape_of(PROWS, BLK), shape_of(PROWS, BLK)),
        in_specs=[SMEM_SPEC] * 2 + [VMEM_SPEC] * 2 + half_specs(0),
        out_specs=(VMEM_SPEC, VMEM_SPEC),
        scratch_shapes=half_scratch,
        compiler_params=PARAMS,
        cost_estimate=pl.CostEstimate(
            flops=5 * 10**9, transcendentals=5 * 10**6, bytes_accessed=4 * 10**6
        ),
        name="attend_near",
    )(*scalars, keys, values, qs, acc, top)
    core_recv = lax.ppermute(send_near, "seq", core_pairs)
    width = w_out.shape[1]
    projected = pl.pallas_call(
        project_out_body,
        out_shape=shape_of(width, BLK),
        in_specs=[VMEM_SPEC] * 3,
        out_specs=VMEM_SPEC,
        compiler_params=PARAMS,
        name="project_out",
    )(merge_two(keep_near, x_recv), core_recv, w_out)
    tp = lax.axis_size("tp")
    columns = width // tp
    parts = lax.all_to_all(
        projected.reshape(tp, columns, BLK), "tp", split_axis=0, concat_axis=0, tiled=True
    )
    residual = lax.dynamic_slice_in_dim(
        hidden_in, lax.axis_index("tp") * columns, columns, 1
    ).T
    hidden_t = pl.pallas_call(
        final_body,
        out_shape=shape_of(columns, BLK),
        in_specs=[VMEM_SPEC] * 2,
        out_specs=VMEM_SPEC,
        compiler_params=PARAMS,
        name="final_sum",
    )(parts, residual)
    return (hidden_t.T, key_t.T, value_t.T)


def solution(mesh):
    return jax.shard_map(
        per_device,
        mesh=mesh,
        in_specs=(
            P("seq", None),
            P(),
            P(None, "tp"),
            P(None, "tp"),
            P(None, "tp"),
            P("tp", None),
            P("seq", "tp"),
            P("seq", "tp"),
            P(),
            P(),
        ),
        out_specs=(P("seq", "tp"), P("seq", "tp"), P("seq", "tp")),
        check_vma=False,
    )
```

```python
import jax
import jax.numpy as jnp
from jax import lax
from jax.experimental import pallas as pl
from jax.experimental.pallas import tpu as pltpu
from jax.sharding import PartitionSpec as P

HEAD_DIM = 80
GROUPS = 2
REQS = 4
BLK = 256
PRE_LEN = 4096
COLS = 4
ZDIM = 8
HPD = 4
QROWS = HPD * HEAD_DIM
PROWS = QROWS + 16
NEG = -1e30
LIMIT = 1e30
FLOOR = 1e-20
AHEAD = 4
TILES = COLS * HPD
HALF = ZDIM // GROUPS
EARLY = 3
LATE = 6 + 1 - EARLY


def request_ends(lens):
    ends = []
    total = 0
    for i in range(REQS):
        total = total + lens[i]
        ends.append(total)
    return ends


def start_of(p, ends):
    st = jnp.int32(0)
    for i in range(REQS - 1):
        st = jnp.where(p >= ends[i], ends[i], st)
    return st


def token_vectors(z, r, ends, grps):
    tvecs, svecs, gvecs = [], [], []
    for k in range(COLS):
        tok0 = (z * COLS + (r ^ k)) * BLK
        tvec = tok0 + lax.broadcasted_iota(jnp.int32, (1, BLK), 1)
        svec = jnp.zeros((1, BLK), jnp.int32)
        gvec = jnp.zeros((1, BLK), jnp.int32) + grps[0]
        for i in range(REQS - 1):
            svec = jnp.where(tvec >= ends[i], ends[i], svec)
            gvec = jnp.where(tvec >= ends[i], grps[i + 1], gvec)
        tvecs.append(tvec)
        svecs.append(svec)
        gvecs.append(gvec)
    return tvecs, svecs, gvecs


def place(keys, values, n, kscr, vscr):
    kt = jnp.concatenate([keys, jnp.zeros((128 - HEAD_DIM, BLK), jnp.bfloat16)], axis=0)
    kscr[n * BLK : (n + 1) * BLK, :] = kt.T
    vscr[n, 0:HEAD_DIM, :] = values
    vscr[n, HEAD_DIM:96, :] = jnp.ones((96 - HEAD_DIM, BLK), jnp.bfloat16)


def key_rows(kscr, blk):
    return kscr[pl.ds(pl.multiple_of(blk * BLK, BLK), BLK), :]


def add_block(blks, masks, tiles, kscr, vscr, qs, acc, m):
    count = len(tiles)
    scores, weights = {}, {}
    for i in range(count + AHEAD + 1):
        if i < count:
            t = tiles[i]
            scores[i] = jnp.dot(
                key_rows(kscr, blks[t // HPD]), qs[t], preferred_element_type=jnp.float32
            )
        j = i - AHEAD
        if 0 <= j < count:
            t = tiles[j]
            sc = scores.pop(j)
            if masks is not None:
                sc = jnp.where(masks[t // HPD], sc, NEG)
            weights[j] = jnp.exp(sc - m[t]).astype(jnp.bfloat16)
        n = j - 1
        if 0 <= n < count:
            t = tiles[n]
            acc[t] = acc[t] + jnp.dot(
                vscr[blks[t // HPD]], weights.pop(n), preferred_element_type=jnp.float32
            )


def add_block_exact(tile, blk, mask, kscr, vscr, qs, acc, m):
    sc = jnp.dot(key_rows(kscr, blk), qs[tile], preferred_element_type=jnp.float32)
    sc = jnp.where(mask, sc, NEG)
    m_old = m[tile]
    m_new = jnp.maximum(m_old, jnp.max(sc, axis=0, keepdims=True))
    w = jnp.exp(sc - m_new).astype(jnp.bfloat16)
    acc[tile] = acc[tile] * jnp.exp(m_old - m_new) + jnp.dot(
        vscr[blk], w, preferred_element_type=jnp.float32
    )
    m[tile] = m_new


def out_of_range(acc):
    top = acc[0, HEAD_DIM : HEAD_DIM + 1, :]
    least = top
    for t in range(1, acc.shape[0]):
        row = acc[t, HEAD_DIM : HEAD_DIM + 1, :]
        top = jnp.maximum(top, row)
        least = jnp.minimum(least, row)
    return jnp.logical_not((jnp.max(top) < LIMIT) & (jnp.min(least) > FLOOR))


def suffix_low(z, r, ends):
    first = start_of(z * COLS * BLK, ends)
    gap = jnp.maximum(first - (BLK - 1) - r * BLK, 0)
    return jnp.minimum((gap + COLS * BLK - 1) // (COLS * BLK), z)


def suffix_full(jz, z, r, ends):
    last = start_of((z + 1) * COLS * BLK - 1, ends)
    return (jz < z) & (last <= (jz * COLS + r) * BLK)


def suffix_mask(jz, r, tvec, svec):
    kvec = (jz * COLS + r) * BLK + lax.broadcasted_iota(jnp.int32, (BLK, BLK), 0)
    return (kvec <= tvec) & (kvec >= svec)


def groups_seen(lo, hi, ends, grps):
    seen = [jnp.bool_(False) for g in range(GROUPS)]
    begin = jnp.int32(0)
    for i in range(REQS):
        inside = (begin < hi) & (ends[i] > lo)
        for g in range(GROUPS):
            seen[g] = seen[g] | (inside & (grps[i] == g))
        begin = ends[i]
    return seen


def early_body(lens, grps, pre, s_0, s_1, s_2, q_0, q_1, q_2, q_3, qs, acc, m, kscr, vscr):
    s = lax.axis_index("seq")
    z = s // COLS
    r = s % COLS
    ends = request_ends(lens)
    tvecs, svecs, gvecs = token_vectors(z, r, ends, grps)
    low = suffix_low(z, r, ends)
    tiles = list(range(TILES))
    for k, ref in enumerate((q_0, q_1, q_2, q_3)):
        for h in range(HPD):
            lo = h * HEAD_DIM
            qs[k * HPD + h, 0:HEAD_DIM, :] = ref[lo : lo + HEAD_DIM, :]
            qs[k * HPD + h, HEAD_DIM:128, :] = jnp.zeros((128 - HEAD_DIM, BLK), jnp.bfloat16)
    here = groups_seen(z * COLS * BLK, (z + 1) * COLS * BLK, ends, grps)
    for g in range(GROUPS):

        @pl.when(here[g])
        def _():
            for c in range(HALF):
                n = g * HALF + c
                place(pre[n, 0:HEAD_DIM, :], pre[n, HEAD_DIM : 2 * HEAD_DIM, :], n, kscr, vscr)

    for d, ref in enumerate((s_0, s_1, s_2)):
        place(ref[0:HEAD_DIM, :], ref[HEAD_DIM : 2 * HEAD_DIM, :], ZDIM + d, kscr, vscr)
    group, both = [], []
    for k in range(COLS):
        tok0 = (z * COLS + (r ^ k)) * BLK
        seen = groups_seen(tok0, tok0 + BLK, ends, grps)
        group.append(jnp.where(seen[0], 0, 1))
        both.append(seen[0] & seen[1])
    any_both = both[0] | both[1] | both[2] | both[3]

    for t in range(TILES):
        sc = jnp.dot(
            key_rows(kscr, group[t // HPD] * HALF), qs[t], preferred_element_type=jnp.float32
        )
        m[t] = jnp.max(sc, axis=0, keepdims=True)
    acc[...] = jnp.zeros_like(acc)

    @pl.when(jnp.logical_not(any_both))
    def _():
        @pl.loop(0, HALF)
        def _(c):
            add_block([g * HALF + c for g in group], None, tiles, kscr, vscr, qs, acc, m)

    @pl.when(any_both)
    def _():
        @pl.loop(0, HALF)
        def _(c):
            masks = [jnp.broadcast_to(gvecs[k] == group[k], (BLK, BLK)) for k in range(COLS)]
            add_block([g * HALF + c for g in group], masks, tiles, kscr, vscr, qs, acc, m)

    for k in range(COLS):

        @pl.when(both[k])
        def _():
            @pl.loop(0, HALF)
            def _(c):
                masks = [jnp.broadcast_to(gvecs[k] == 1, (BLK, BLK))] * COLS
                part = tiles[k * HPD : (k + 1) * HPD]
                add_block([HALF + c] * COLS, masks, part, kscr, vscr, qs, acc, m)

    early_end = jnp.minimum(z - low + 1, EARLY)

    @pl.loop(0, early_end)
    def _(d):
        jz = z - d
        full = suffix_full(jz, z, r, ends)

        @pl.when(full)
        def _():
            add_block([ZDIM + d] * COLS, None, tiles, kscr, vscr, qs, acc, m)

        @pl.when(jnp.logical_not(full))
        def _():
            masks = [suffix_mask(jz, r, tvecs[k], svecs[k]) for k in range(COLS)]
            add_block([ZDIM + d] * COLS, masks, tiles, kscr, vscr, qs, acc, m)

    @pl.when(out_of_range(acc))
    def _():
        acc[...] = jnp.zeros_like(acc)
        m[...] = jnp.full(m.shape, NEG, jnp.float32)
        for k in range(COLS):
            for g in range(GROUPS):

                @pl.when((group[k] == g) | both[k])
                def _():
                    mask = jnp.broadcast_to(gvecs[k] == g, (BLK, BLK))

                    @pl.loop(0, HALF)
                    def _(c):
                        @pl.loop(0, HPD)
                        def _(h):
                            add_block_exact(
                                k * HPD + h, g * HALF + c, mask, kscr, vscr, qs, acc, m
                            )

            @pl.loop(0, early_end)
            def _(d):
                mask = suffix_mask(z - d, r, tvecs[k], svecs[k])

                @pl.loop(0, HPD)
                def _(h):
                    add_block_exact(k * HPD + h, ZDIM + d, mask, kscr, vscr, qs, acc, m)


def write_partial(dst, acc, m, k):
    rows = lax.broadcasted_iota(jnp.int32, (16, BLK), 0)
    extra = jnp.zeros((16, BLK), jnp.float32)
    for h in range(HPD):
        t = k * HPD + h
        total_w = acc[t, HEAD_DIM : HEAD_DIM + 1, :]
        dst[h * HEAD_DIM : (h + 1) * HEAD_DIM, :] = (
            acc[t, 0:HEAD_DIM, :] * (1.0 / total_w)
        ).astype(jnp.bfloat16)
        lse = m[t] + jnp.log(total_w)
        for j in range(3):
            part = lse.astype(jnp.bfloat16).astype(jnp.float32)
            extra = jnp.where(rows == 3 * h + j, part, extra)
            lse = lse - part
    dst[QROWS:PROWS, :] = extra.astype(jnp.bfloat16)


def suffix_tiles(k0, lens, grps, qs, acc_in, m_in, keep, send, kscr, vscr, acc, m):
    s = lax.axis_index("seq")
    z = s // COLS
    r = s % COLS
    ends = request_ends(lens)
    tvecs, svecs, unused = token_vectors(z, r, ends, grps)
    end = z - suffix_low(z, r, ends) + 1
    tiles = list(range(2 * HPD))
    acc[...] = acc_in[...]
    m[...] = m_in[...]

    def step(d, c):
        jz = z - d
        full = suffix_full(jz, z, r, ends)

        @pl.when(full)
        def _():
            add_block([d - EARLY] * 2, None, tiles, kscr, vscr, qs, acc, m)

        @pl.when(jnp.logical_not(full))
        def _():
            masks = [suffix_mask(jz, r, tvecs[k0 + k], svecs[k0 + k]) for k in range(2)]
            add_block([d - EARLY] * 2, masks, tiles, kscr, vscr, qs, acc, m)

        return c

    lax.fori_loop(EARLY, end, step, 0)

    @pl.when(out_of_range(acc))
    def _():
        acc[...] = acc_in[...]
        m[...] = m_in[...]
        for k in range(2):

            def exact_step(d, c):
                mask = suffix_mask(z - d, r, tvecs[k0 + k], svecs[k0 + k])

                @pl.loop(0, HPD)
                def _(h):
                    add_block_exact(k * HPD + h, d - EARLY, mask, kscr, vscr, qs, acc, m)

                return c

            lax.fori_loop(EARLY, end, exact_step, 0)

    write_partial(keep, acc, m, 0)
    write_partial(send, acc, m, 1)


def far_body(lens, grps, *refs):
    late = refs[:LATE]
    qs, acc_in, m_in, keep, send, kscr, vscr, acc, m = refs[LATE:]
    for n in range(LATE):
        place(late[n][0:HEAD_DIM, :], late[n][HEAD_DIM : 2 * HEAD_DIM, :], n, kscr, vscr)
    suffix_tiles(2, lens, grps, qs, acc_in, m_in, keep, send, kscr, vscr, acc, m)


def near_body(lens, grps, kscr, vscr, qs, acc_in, m_in, keep, send, acc, m):
    suffix_tiles(0, lens, grps, qs, acc_in, m_in, keep, send, kscr, vscr, acc, m)


def spread_body(keys, values, out, sem):
    copies = []
    for n in range(ZDIM):
        copies.append(
            pltpu.make_async_copy(keys, out.at[n, pl.ds(0, HEAD_DIM)], sem.at[0, n])
        )
        copies.append(
            pltpu.make_async_copy(values, out.at[n, pl.ds(HEAD_DIM, HEAD_DIM)], sem.at[1, n])
        )
    for copy in copies:
        copy.start()
    for copy in copies:
        copy.wait()


def project_body(
    lens,
    gain,
    freq,
    hidden_far,
    wk_far,
    wv_far,
    wq_far,
    q_out,
    kv_out,
    k_out,
    v_out,
    hidden,
    wk,
    wv,
    wq,
    sem,
):
    moves = (
        (hidden_far, hidden),
        (wk_far, wk),
        (wv_far, wv),
        (wq_far, wq),
    )
    fetches = [
        pltpu.make_async_copy(src, dst, sem.at[n]) for n, (src, dst) in enumerate(moves)
    ]
    for fetch in fetches:
        fetch.start()
    ends = request_ends(lens)
    tvec = lax.axis_index("seq") * BLK + lax.broadcasted_iota(jnp.int32, (1, BLK), 1)
    svec = jnp.zeros((1, BLK), jnp.int32)
    for i in range(REQS - 1):
        svec = jnp.where(tvec >= ends[i], ends[i], svec)
    positions = (PRE_LEN + tvec - svec).astype(jnp.float32)
    angles = freq[...] * positions
    c = jnp.cos(angles)
    sn = jnp.sin(angles)
    fetches[0].wait()
    wide = hidden[...].astype(jnp.float32)
    mean_square = jnp.mean(wide * wide, axis=-1, keepdims=True)
    normed = (
        wide * lax.rsqrt(mean_square + 1e-05) * gain[...].reshape(1, wide.shape[1])
    ).astype(jnp.bfloat16)

    def proj(w):
        return lax.dot_general(
            w[...], normed, (((1,), (1,)), ((), ())), preferred_element_type=jnp.float32
        )

    hf = HEAD_DIM // 2

    def rotate(a, b):
        return a * c - b * sn, b * c + a * sn

    fetches[1].wait()
    kf = proj(wk)
    ka, kb = rotate(kf[0:hf], kf[hf:HEAD_DIM])
    kt = jnp.concatenate([ka, kb], axis=0).astype(jnp.bfloat16)
    fetches[2].wait()
    vt = proj(wv).astype(jnp.bfloat16)
    k_out[...] = kt
    v_out[...] = vt
    kv_out[0:HEAD_DIM, :] = kt
    kv_out[HEAD_DIM : 2 * HEAD_DIM, :] = vt
    fetches[3].wait()
    qf = proj(wq)
    for h in range(HPD):
        lo = h * HEAD_DIM
        qa, qb = rotate(qf[lo : lo + hf], qf[lo + hf : lo + HEAD_DIM])
        q_out[lo : lo + HEAD_DIM, :] = (
            jnp.concatenate([qa, qb], axis=0) * HEAD_DIM ** (-0.5)
        ).astype(jnp.bfloat16)


def merged(*parts):
    tails = [p[QROWS:PROWS, :].astype(jnp.float32) for p in parts]
    outs, lses = [], []
    for h in range(HPD):
        ls = [
            t[3 * h : 3 * h + 1] + t[3 * h + 1 : 3 * h + 2] + t[3 * h + 2 : 3 * h + 3]
            for t in tails
        ]
        top = ls[0]
        for x in ls[1:]:
            top = jnp.maximum(top, x)
        ws = [jnp.exp(x - top) for x in ls]
        tot = ws[0]
        for x in ws[1:]:
            tot = tot + x
        rows = slice(h * HEAD_DIM, (h + 1) * HEAD_DIM)
        out = parts[0][rows, :].astype(jnp.float32) * (ws[0] / tot)
        for p, w in zip(parts[1:], ws[1:]):
            out = out + p[rows, :].astype(jnp.float32) * (w / tot)
        outs.append(out.astype(jnp.bfloat16))
        lses.append(top + jnp.log(tot))
    return outs, lses


def merge_far_body(keep, recv, dst):
    outs, lses = merged(keep[...], recv[...])
    extra = jnp.zeros((16, BLK), jnp.float32)
    rows = lax.broadcasted_iota(jnp.int32, (16, BLK), 0)
    for h in range(HPD):
        lse = lses[h]
        for j in range(3):
            part = lse.astype(jnp.bfloat16).astype(jnp.float32)
            extra = jnp.where(rows == 3 * h + j, part, extra)
            lse = lse - part
    dst[...] = jnp.concatenate(outs + [extra.astype(jnp.bfloat16)], axis=0)


def project_out_body(own, near, w, out):
    outs, unused = merged(own[...], near[...])
    attended = jnp.concatenate(outs, axis=0)
    out[...] = lax.dot_general(
        w[...], attended, (((0,), (0,)), ((), ())), preferred_element_type=jnp.float32
    ).astype(jnp.bfloat16)


def final_body(parts, residual, out):
    total = residual[...].astype(jnp.float32)
    acc = parts[0].astype(jnp.float32)
    for i in range(1, parts.shape[0]):
        acc = acc + parts[i].astype(jnp.float32)
    out[...] = (acc + total).astype(jnp.bfloat16)


def shape_of(*dims):
    return jax.ShapeDtypeStruct(dims, jnp.bfloat16)


VMEM_SPEC = pl.BlockSpec(memory_space=pltpu.VMEM)
HBM_SPEC = pl.BlockSpec(memory_space=pltpu.HBM)
SMEM_SPEC = pl.BlockSpec(memory_space=pltpu.SMEM)
PARAMS = pltpu.CompilerParams(vmem_limit_bytes=20 * 1024 * 1024)


def in_hbm(x):
    return pltpu.with_memory_space_constraint(x, pltpu.HBM)


def per_device(
    hidden_in,
    norm_gain,
    w_query,
    w_key,
    w_value,
    w_out,
    prefix_keys,
    prefix_values,
    lengths,
    groups,
):
    columns_of_z = [list(range(c, ZDIM * COLS, COLS)) for c in range(COLS)]

    def along_z(x):
        return lax.all_to_all(
            x, "seq", split_axis=0, concat_axis=0, tiled=True, axis_index_groups=columns_of_z
        )

    pre = along_z(
        pl.pallas_call(
            spread_body,
            out_shape=shape_of(ZDIM, 2 * HEAD_DIM, BLK),
            in_specs=[HBM_SPEC] * 2,
            out_specs=HBM_SPEC,
            scratch_shapes=[pltpu.SemaphoreType.DMA((2, ZDIM))],
            compiler_params=PARAMS,
            name="spread_prefix",
        )(in_hbm(prefix_keys.T), in_hbm(prefix_values.T))
    )

    half_dim = HEAD_DIM // 2
    frequency = jnp.power(
        jnp.float32(1000000.0), -jnp.arange(half_dim, dtype=jnp.float32) / half_dim
    )
    q_t, suf_own, key_t, value_t = pl.pallas_call(
        project_body,
        out_shape=(
            shape_of(QROWS, BLK),
            shape_of(2 * HEAD_DIM, BLK),
            shape_of(HEAD_DIM, BLK),
            shape_of(HEAD_DIM, BLK),
        ),
        in_specs=[SMEM_SPEC] + [VMEM_SPEC] * 2 + [HBM_SPEC] * 4,
        out_specs=(VMEM_SPEC,) * 4,
        scratch_shapes=[
            pltpu.VMEM(hidden_in.shape, jnp.bfloat16),
            pltpu.VMEM((HEAD_DIM, w_query.shape[0]), jnp.bfloat16),
            pltpu.VMEM((HEAD_DIM, w_query.shape[0]), jnp.bfloat16),
            pltpu.VMEM((QROWS, w_query.shape[0]), jnp.bfloat16),
            pltpu.SemaphoreType.DMA((4,)),
        ],
        compiler_params=PARAMS,
        name="project_in",
    )(
        lengths,
        norm_gain,
        frequency[:, None],
        *[in_hbm(x) for x in (hidden_in, w_key.T, w_value.T, w_query.T)],
    )
    q_all = [q_t] + [
        lax.ppermute(q_t, "seq", [(i, i ^ k) for i in range(32)]) for k in range(1, COLS)
    ]


    def later(x, d):
        return lax.ppermute(
            x, "seq", [(i, i + COLS * d) for i in range(COLS * (ZDIM - d))]
        )

    suf_late, q_all[1] = lax.optimization_barrier((suf_own, q_all[1]))
    suf = [suf_own] + [
        later(suf_own if d < EARLY else suf_late, d) for d in range(1, ZDIM - 1)
    ]
    scalars = (lengths, groups)
    qs, acc, top = pl.pallas_call(
        early_body,
        out_shape=(
            shape_of(TILES, 128, BLK),
            jax.ShapeDtypeStruct((TILES, 96, BLK), jnp.float32),
            jax.ShapeDtypeStruct((TILES, 1, BLK), jnp.float32),
        ),
        in_specs=[SMEM_SPEC] * 2 + [VMEM_SPEC] * (1 + EARLY + COLS),
        out_specs=(VMEM_SPEC,) * 3,
        scratch_shapes=[
            pltpu.VMEM(((ZDIM + EARLY) * BLK, 128), jnp.bfloat16),
            pltpu.VMEM((ZDIM + EARLY, 96, BLK), jnp.bfloat16),
        ],
        compiler_params=PARAMS,
        cost_estimate=pl.CostEstimate(
            flops=8 * 10**9, transcendentals=8 * 10**6, bytes_accessed=4 * 10**6
        ),
        name="attend_early",
    )(*scalars, pre, *suf[:EARLY], *q_all)
    halves = TILES // 2
    half_scratch = [
        pltpu.VMEM((halves, 96, BLK), jnp.float32),
        pltpu.VMEM((halves, 1, BLK), jnp.float32),
    ]

    def half_specs(at):
        return [
            pl.BlockSpec((halves, 128, BLK), lambda i: (at, 0, 0)),
            pl.BlockSpec((halves, 96, BLK), lambda i: (at, 0, 0)),
            pl.BlockSpec((halves, 1, BLK), lambda i: (at, 0, 0)),
        ]

    core_pairs = [(i, i ^ 1) for i in range(32)]
    keep_far, send_far, keys, values = pl.pallas_call(
        far_body,
        grid=(1,),
        out_shape=(
            shape_of(PROWS, BLK),
            shape_of(PROWS, BLK),
            shape_of(LATE * BLK, 128),
            shape_of(LATE, 96, BLK),
        ),
        in_specs=[SMEM_SPEC] * 2 + [VMEM_SPEC] * LATE + half_specs(1),
        out_specs=(VMEM_SPEC,) * 4,
        scratch_shapes=half_scratch,
        compiler_params=PARAMS,
        cost_estimate=pl.CostEstimate(
            flops=5 * 10**9, transcendentals=5 * 10**6, bytes_accessed=4 * 10**6
        ),
        name="attend_far",
    )(*scalars, *suf[EARLY:], qs, acc, top)

    def merge_two(one, two):
        return pl.pallas_call(
            merge_far_body,
            out_shape=shape_of(PROWS, BLK),
            in_specs=[VMEM_SPEC] * 2,
            out_specs=VMEM_SPEC,
            compiler_params=PARAMS,
            name="merge_two",
        )(one, two)

    far = merge_two(keep_far, lax.ppermute(send_far, "seq", core_pairs))
    far, values = lax.optimization_barrier((far, values))
    x_recv = lax.ppermute(far, "seq", [(i, i ^ 2) for i in range(32)])
    keep_near, send_near = pl.pallas_call(
        near_body,
        grid=(1,),
        out_shape=(shape_of(PROWS, BLK), shape_of(PROWS, BLK)),
        in_specs=[SMEM_SPEC] * 2 + [VMEM_SPEC] * 2 + half_specs(0),
        out_specs=(VMEM_SPEC, VMEM_SPEC),
        scratch_shapes=half_scratch,
        compiler_params=PARAMS,
        cost_estimate=pl.CostEstimate(
            flops=5 * 10**9, transcendentals=5 * 10**6, bytes_accessed=4 * 10**6
        ),
        name="attend_near",
    )(*scalars, keys, values, qs, acc, top)
    core_recv = lax.ppermute(send_near, "seq", core_pairs)
    width = w_out.shape[1]
    projected = pl.pallas_call(
        project_out_body,
        out_shape=shape_of(width, BLK),
        in_specs=[VMEM_SPEC] * 3,
        out_specs=VMEM_SPEC,
        compiler_params=PARAMS,
        name="project_out",
    )(merge_two(keep_near, x_recv), core_recv, w_out)
    tp = lax.axis_size("tp")
    columns = width // tp
    parts = lax.all_to_all(
        projected.reshape(tp, columns, BLK), "tp", split_axis=0, concat_axis=0, tiled=True
    )
    residual = lax.dynamic_slice_in_dim(
        hidden_in, lax.axis_index("tp") * columns, columns, 1
    ).T
    hidden_t = pl.pallas_call(
        final_body,
        out_shape=shape_of(columns, BLK),
        in_specs=[VMEM_SPEC] * 2,
        out_specs=VMEM_SPEC,
        compiler_params=PARAMS,
        name="final_sum",
    )(parts, residual)
    return (hidden_t.T, key_t.T, value_t.T)


def solution(mesh):
    return jax.shard_map(
        per_device,
        mesh=mesh,
        in_specs=(
            P("seq", None),
            P(),
            P(None, "tp"),
            P(None, "tp"),
            P(None, "tp"),
            P("tp", None),
            P("seq", "tp"),
            P("seq", "tp"),
            P(),
            P(),
        ),
        out_specs=(P("seq", "tp"), P("seq", "tp"), P("seq", "tp")),
        check_vma=False,
    )
```

```python
import jax
import jax.numpy as jnp
from jax import lax
from jax.experimental import pallas as pl
from jax.experimental.pallas import tpu as pltpu
from jax.sharding import PartitionSpec as P

HEAD_DIM = 80
GROUPS = 2
REQS = 4
BLK = 256
PRE_LEN = 4096
COLS = 4
ZDIM = 8
HPD = 4
QROWS = HPD * HEAD_DIM
PROWS = QROWS + 16
NEG = -1e30
LIMIT = 1e30
FLOOR = 1e-20
AHEAD = 4
TILES = COLS * HPD
HALF = ZDIM // GROUPS
SOON = 4
SPAN = 6 + 1


def request_ends(lens):
    ends = []
    total = 0
    for i in range(REQS):
        total = total + lens[i]
        ends.append(total)
    return ends


def start_of(p, ends):
    st = jnp.int32(0)
    for i in range(REQS - 1):
        st = jnp.where(p >= ends[i], ends[i], st)
    return st


def token_vectors(z, r, ends, grps):
    tvecs, svecs, gvecs = [], [], []
    for k in range(COLS):
        tok0 = (z * COLS + (r ^ k)) * BLK
        tvec = tok0 + lax.broadcasted_iota(jnp.int32, (1, BLK), 1)
        svec = jnp.zeros((1, BLK), jnp.int32)
        gvec = jnp.zeros((1, BLK), jnp.int32) + grps[0]
        for i in range(REQS - 1):
            svec = jnp.where(tvec >= ends[i], ends[i], svec)
            gvec = jnp.where(tvec >= ends[i], grps[i + 1], gvec)
        tvecs.append(tvec)
        svecs.append(svec)
        gvecs.append(gvec)
    return tvecs, svecs, gvecs


def place(keys, values, n, kscr, vscr):
    kt = jnp.concatenate([keys, jnp.zeros((128 - HEAD_DIM, BLK), jnp.bfloat16)], axis=0)
    kscr[n * BLK : (n + 1) * BLK, :] = kt.T
    vscr[n, 0:HEAD_DIM, :] = values
    vscr[n, HEAD_DIM:96, :] = jnp.ones((96 - HEAD_DIM, BLK), jnp.bfloat16)


def key_rows(kscr, blk):
    return kscr[pl.ds(pl.multiple_of(blk * BLK, BLK), BLK), :]


def add_block(blks, masks, tiles, kscr, vscr, qs, acc, m):
    count = len(tiles)
    scores, weights = {}, {}
    for i in range(count + AHEAD + 1):
        if i < count:
            t = tiles[i]
            scores[i] = jnp.dot(
                key_rows(kscr, blks[t // HPD]), qs[t], preferred_element_type=jnp.float32
            )
        j = i - AHEAD
        if 0 <= j < count:
            t = tiles[j]
            sc = scores.pop(j)
            if masks is not None:
                sc = jnp.where(masks[t // HPD], sc, NEG)
            weights[j] = jnp.exp(sc - m[t]).astype(jnp.bfloat16)
        n = j - 1
        if 0 <= n < count:
            t = tiles[n]
            acc[t] = acc[t] + jnp.dot(
                vscr[blks[t // HPD]], weights.pop(n), preferred_element_type=jnp.float32
            )


def add_block_exact(tile, blk, mask, kscr, vscr, qs, acc, m):
    sc = jnp.dot(key_rows(kscr, blk), qs[tile], preferred_element_type=jnp.float32)
    sc = jnp.where(mask, sc, NEG)
    m_old = m[tile]
    m_new = jnp.maximum(m_old, jnp.max(sc, axis=0, keepdims=True))
    w = jnp.exp(sc - m_new).astype(jnp.bfloat16)
    acc[tile] = acc[tile] * jnp.exp(m_old - m_new) + jnp.dot(
        vscr[blk], w, preferred_element_type=jnp.float32
    )
    m[tile] = m_new


def out_of_range(acc):
    top = acc[0, HEAD_DIM : HEAD_DIM + 1, :]
    least = top
    for t in range(1, acc.shape[0]):
        row = acc[t, HEAD_DIM : HEAD_DIM + 1, :]
        top = jnp.maximum(top, row)
        least = jnp.minimum(least, row)
    return jnp.logical_not((jnp.max(top) < LIMIT) & (jnp.min(least) > FLOOR))


def suffix_low(z, r, ends):
    first = start_of(z * COLS * BLK, ends)
    gap = jnp.maximum(first - (BLK - 1) - r * BLK, 0)
    return jnp.minimum((gap + COLS * BLK - 1) // (COLS * BLK), z)


def suffix_full(jz, z, r, ends):
    last = start_of((z + 1) * COLS * BLK - 1, ends)
    return (jz < z) & (last <= (jz * COLS + r) * BLK)


def suffix_mask(jz, r, tvec, svec):
    kvec = (jz * COLS + r) * BLK + lax.broadcasted_iota(jnp.int32, (BLK, BLK), 0)
    return (kvec <= tvec) & (kvec >= svec)


def groups_seen(lo, hi, ends, grps):
    seen = [jnp.bool_(False) for g in range(GROUPS)]
    begin = jnp.int32(0)
    for i in range(REQS):
        inside = (begin < hi) & (ends[i] > lo)
        for g in range(GROUPS):
            seen[g] = seen[g] | (inside & (grps[i] == g))
        begin = ends[i]
    return seen


def prefix_body(lens, grps, pre, q_0, q_1, q_2, q_3, qs, acc, m, kscr, vscr):
    s = lax.axis_index("seq")
    z = s // COLS
    r = s % COLS
    ends = request_ends(lens)
    gvecs = token_vectors(z, r, ends, grps)[2]
    tiles = list(range(TILES))
    for k, ref in enumerate((q_0, q_1, q_2, q_3)):
        for h in range(HPD):
            lo = h * HEAD_DIM
            qs[k * HPD + h, 0:HEAD_DIM, :] = ref[lo : lo + HEAD_DIM, :]
            qs[k * HPD + h, HEAD_DIM:128, :] = jnp.zeros((128 - HEAD_DIM, BLK), jnp.bfloat16)
    here = groups_seen(z * COLS * BLK, (z + 1) * COLS * BLK, ends, grps)
    for g in range(GROUPS):

        @pl.when(here[g])
        def _():
            for c in range(HALF):
                n = g * HALF + c
                place(pre[n, 0:HEAD_DIM, :], pre[n, HEAD_DIM : 2 * HEAD_DIM, :], n, kscr, vscr)

    group, both = [], []
    for k in range(COLS):
        tok0 = (z * COLS + (r ^ k)) * BLK
        seen = groups_seen(tok0, tok0 + BLK, ends, grps)
        group.append(jnp.where(seen[0], 0, 1))
        both.append(seen[0] & seen[1])
    any_both = both[0] | both[1] | both[2] | both[3]

    for t in range(TILES):
        sc = jnp.dot(
            key_rows(kscr, group[t // HPD] * HALF), qs[t], preferred_element_type=jnp.float32
        )
        m[t] = jnp.max(sc, axis=0, keepdims=True)
    acc[...] = jnp.zeros_like(acc)

    @pl.when(jnp.logical_not(any_both))
    def _():
        @pl.loop(0, HALF)
        def _(c):
            add_block([g * HALF + c for g in group], None, tiles, kscr, vscr, qs, acc, m)

    @pl.when(any_both)
    def _():
        @pl.loop(0, HALF)
        def _(c):
            masks = [jnp.broadcast_to(gvecs[k] == group[k], (BLK, BLK)) for k in range(COLS)]
            add_block([g * HALF + c for g in group], masks, tiles, kscr, vscr, qs, acc, m)

    for k in range(COLS):

        @pl.when(both[k])
        def _():
            @pl.loop(0, HALF)
            def _(c):
                masks = [jnp.broadcast_to(gvecs[k] == 1, (BLK, BLK))] * COLS
                part = tiles[k * HPD : (k + 1) * HPD]
                add_block([HALF + c] * COLS, masks, part, kscr, vscr, qs, acc, m)

    @pl.when(out_of_range(acc))
    def _():
        acc[...] = jnp.zeros_like(acc)
        m[...] = jnp.full(m.shape, NEG, jnp.float32)
        for k in range(COLS):
            for g in range(GROUPS):

                @pl.when((group[k] == g) | both[k])
                def _():
                    mask = jnp.broadcast_to(gvecs[k] == g, (BLK, BLK))

                    @pl.loop(0, HALF)
                    def _(c):
                        @pl.loop(0, HPD)
                        def _(h):
                            add_block_exact(
                                k * HPD + h, g * HALF + c, mask, kscr, vscr, qs, acc, m
                            )


def write_partial(dst, acc, m, k):
    rows = lax.broadcasted_iota(jnp.int32, (16, BLK), 0)
    extra = jnp.zeros((16, BLK), jnp.float32)
    for h in range(HPD):
        t = k * HPD + h
        total_w = acc[t, HEAD_DIM : HEAD_DIM + 1, :]
        dst[h * HEAD_DIM : (h + 1) * HEAD_DIM, :] = (
            acc[t, 0:HEAD_DIM, :] * (1.0 / total_w)
        ).astype(jnp.bfloat16)
        lse = m[t] + jnp.log(total_w)
        for j in range(3):
            part = lse.astype(jnp.bfloat16).astype(jnp.float32)
            extra = jnp.where(rows == 3 * h + j, part, extra)
            lse = lse - part
    dst[QROWS:PROWS, :] = extra.astype(jnp.bfloat16)


def suffix_tiles(k0, lens, grps, qs, acc_in, m_in, keep, send, kscr, vscr, acc, m):
    s = lax.axis_index("seq")
    z = s // COLS
    r = s % COLS
    ends = request_ends(lens)
    tvecs, svecs, unused = token_vectors(z, r, ends, grps)
    end = z - suffix_low(z, r, ends) + 1
    tiles = list(range(2 * HPD))
    acc[...] = acc_in[...]
    m[...] = m_in[...]

    def step(d, c):
        jz = z - d
        full = suffix_full(jz, z, r, ends)

        @pl.when(full)
        def _():
            add_block([d] * 2, None, tiles, kscr, vscr, qs, acc, m)

        @pl.when(jnp.logical_not(full))
        def _():
            masks = [suffix_mask(jz, r, tvecs[k0 + k], svecs[k0 + k]) for k in range(2)]
            add_block([d] * 2, masks, tiles, kscr, vscr, qs, acc, m)

        return c

    lax.fori_loop(0, end, step, 0)

    @pl.when(out_of_range(acc))
    def _():
        acc[...] = acc_in[...]
        m[...] = m_in[...]
        for k in range(2):

            def exact_step(d, c):
                mask = suffix_mask(z - d, r, tvecs[k0 + k], svecs[k0 + k])

                @pl.loop(0, HPD)
                def _(h):
                    add_block_exact(k * HPD + h, d, mask, kscr, vscr, qs, acc, m)

                return c

            lax.fori_loop(0, end, exact_step, 0)

    write_partial(keep, acc, m, 0)
    write_partial(send, acc, m, 1)


def far_body(lens, grps, *refs):
    suf = refs[:SPAN]
    qs, acc_in, m_in, keep, send, kscr, vscr, acc, m = refs[SPAN:]
    for n in range(SPAN):
        place(suf[n][0:HEAD_DIM, :], suf[n][HEAD_DIM : 2 * HEAD_DIM, :], n, kscr, vscr)
    suffix_tiles(2, lens, grps, qs, acc_in, m_in, keep, send, kscr, vscr, acc, m)


def near_body(lens, grps, kscr, vscr, qs, acc_in, m_in, keep, send, acc, m):
    suffix_tiles(0, lens, grps, qs, acc_in, m_in, keep, send, kscr, vscr, acc, m)


def spread_body(keys, values, out, stage, sem, slot_sem):
    loads = [
        pltpu.make_async_copy(keys, stage.at[pl.ds(0, HEAD_DIM)], sem.at[0]),
        pltpu.make_async_copy(values, stage.at[pl.ds(HEAD_DIM, HEAD_DIM)], sem.at[1]),
    ]
    slots = [pltpu.make_async_copy(stage, out.at[n], slot_sem.at[n]) for n in range(ZDIM)]
    for copy in loads:
        copy.start()
    for copy in loads:
        copy.wait()
    for copy in slots:
        copy.start()
    for copy in slots:
        copy.wait()


def project_body(
    lens,
    gain,
    freq,
    hidden_far,
    wk_far,
    wv_far,
    wq_far,
    q_out,
    kv_out,
    k_out,
    v_out,
    hidden,
    wk,
    wv,
    wq,
    sem,
):
    moves = (
        (hidden_far, hidden),
        (wk_far, wk),
        (wv_far, wv),
        (wq_far, wq),
    )
    fetches = [
        pltpu.make_async_copy(src, dst, sem.at[n]) for n, (src, dst) in enumerate(moves)
    ]
    for fetch in fetches:
        fetch.start()
    ends = request_ends(lens)
    tvec = lax.axis_index("seq") * BLK + lax.broadcasted_iota(jnp.int32, (1, BLK), 1)
    svec = jnp.zeros((1, BLK), jnp.int32)
    for i in range(REQS - 1):
        svec = jnp.where(tvec >= ends[i], ends[i], svec)
    positions = (PRE_LEN + tvec - svec).astype(jnp.float32)
    angles = freq[...] * positions
    c = jnp.cos(angles)
    sn = jnp.sin(angles)
    fetches[0].wait()
    wide = hidden[...].astype(jnp.float32)
    mean_square = jnp.mean(wide * wide, axis=-1, keepdims=True)
    normed = (
        wide * lax.rsqrt(mean_square + 1e-05) * gain[...].reshape(1, wide.shape[1])
    ).astype(jnp.bfloat16)

    def proj(w):
        return lax.dot_general(
            w[...], normed, (((1,), (1,)), ((), ())), preferred_element_type=jnp.float32
        )

    hf = HEAD_DIM // 2

    def rotate(a, b):
        return a * c - b * sn, b * c + a * sn

    fetches[1].wait()
    kf = proj(wk)
    ka, kb = rotate(kf[0:hf], kf[hf:HEAD_DIM])
    kt = jnp.concatenate([ka, kb], axis=0).astype(jnp.bfloat16)
    fetches[2].wait()
    vt = proj(wv).astype(jnp.bfloat16)
    k_out[...] = kt
    v_out[...] = vt
    kv_out[0:HEAD_DIM, :] = kt
    kv_out[HEAD_DIM : 2 * HEAD_DIM, :] = vt
    fetches[3].wait()
    qf = proj(wq)
    for h in range(HPD):
        lo = h * HEAD_DIM
        qa, qb = rotate(qf[lo : lo + hf], qf[lo + hf : lo + HEAD_DIM])
        q_out[lo : lo + HEAD_DIM, :] = (
            jnp.concatenate([qa, qb], axis=0) * HEAD_DIM ** (-0.5)
        ).astype(jnp.bfloat16)


def merged(*parts):
    tails = [p[QROWS:PROWS, :].astype(jnp.float32) for p in parts]
    outs, lses = [], []
    for h in range(HPD):
        ls = [
            t[3 * h : 3 * h + 1] + t[3 * h + 1 : 3 * h + 2] + t[3 * h + 2 : 3 * h + 3]
            for t in tails
        ]
        top = ls[0]
        for x in ls[1:]:
            top = jnp.maximum(top, x)
        ws = [jnp.exp(x - top) for x in ls]
        tot = ws[0]
        for x in ws[1:]:
            tot = tot + x
        rows = slice(h * HEAD_DIM, (h + 1) * HEAD_DIM)
        out = parts[0][rows, :].astype(jnp.float32) * (ws[0] / tot)
        for p, w in zip(parts[1:], ws[1:]):
            out = out + p[rows, :].astype(jnp.float32) * (w / tot)
        outs.append(out.astype(jnp.bfloat16))
        lses.append(top + jnp.log(tot))
    return outs, lses


def merge_far_body(keep, recv, dst):
    outs, lses = merged(keep[...], recv[...])
    extra = jnp.zeros((16, BLK), jnp.float32)
    rows = lax.broadcasted_iota(jnp.int32, (16, BLK), 0)
    for h in range(HPD):
        lse = lses[h]
        for j in range(3):
            part = lse.astype(jnp.bfloat16).astype(jnp.float32)
            extra = jnp.where(rows == 3 * h + j, part, extra)
            lse = lse - part
    dst[...] = jnp.concatenate(outs + [extra.astype(jnp.bfloat16)], axis=0)


def project_out_body(own, near, w, out):
    outs, unused = merged(own[...], near[...])
    attended = jnp.concatenate(outs, axis=0)
    out[...] = lax.dot_general(
        w[...], attended, (((0,), (0,)), ((), ())), preferred_element_type=jnp.float32
    ).astype(jnp.bfloat16)


def final_body(parts, residual, out):
    total = residual[...].astype(jnp.float32)
    acc = parts[0].astype(jnp.float32)
    for i in range(1, parts.shape[0]):
        acc = acc + parts[i].astype(jnp.float32)
    out[...] = (acc + total).astype(jnp.bfloat16)


def shape_of(*dims):
    return jax.ShapeDtypeStruct(dims, jnp.bfloat16)


VMEM_SPEC = pl.BlockSpec(memory_space=pltpu.VMEM)
HBM_SPEC = pl.BlockSpec(memory_space=pltpu.HBM)
SMEM_SPEC = pl.BlockSpec(memory_space=pltpu.SMEM)
PARAMS = pltpu.CompilerParams(vmem_limit_bytes=20 * 1024 * 1024)


def in_hbm(x):
    return pltpu.with_memory_space_constraint(x, pltpu.HBM)


def per_device(
    hidden_in,
    norm_gain,
    w_query,
    w_key,
    w_value,
    w_out,
    prefix_keys,
    prefix_values,
    lengths,
    groups,
):
    columns_of_z = [list(range(c, ZDIM * COLS, COLS)) for c in range(COLS)]

    def along_z(x):
        return lax.all_to_all(
            x, "seq", split_axis=0, concat_axis=0, tiled=True, axis_index_groups=columns_of_z
        )

    pre = along_z(
        pl.pallas_call(
            spread_body,
            out_shape=shape_of(ZDIM, 2 * HEAD_DIM, BLK),
            in_specs=[HBM_SPEC] * 2,
            out_specs=HBM_SPEC,
            scratch_shapes=[
                pltpu.VMEM((2 * HEAD_DIM, BLK), jnp.bfloat16),
                pltpu.SemaphoreType.DMA((2,)),
                pltpu.SemaphoreType.DMA((ZDIM,)),
            ],
            compiler_params=PARAMS,
            name="spread_prefix",
        )(in_hbm(prefix_keys.T), in_hbm(prefix_values.T))
    )

    half_dim = HEAD_DIM // 2
    frequency = jnp.power(
        jnp.float32(1000000.0), -jnp.arange(half_dim, dtype=jnp.float32) / half_dim
    )
    q_t, suf_own, key_t, value_t = pl.pallas_call(
        project_body,
        out_shape=(
            shape_of(QROWS, BLK),
            shape_of(2 * HEAD_DIM, BLK),
            shape_of(HEAD_DIM, BLK),
            shape_of(HEAD_DIM, BLK),
        ),
        in_specs=[SMEM_SPEC] + [VMEM_SPEC] * 2 + [HBM_SPEC] * 4,
        out_specs=(VMEM_SPEC,) * 4,
        scratch_shapes=[
            pltpu.VMEM(hidden_in.shape, jnp.bfloat16),
            pltpu.VMEM((HEAD_DIM, w_query.shape[0]), jnp.bfloat16),
            pltpu.VMEM((HEAD_DIM, w_query.shape[0]), jnp.bfloat16),
            pltpu.VMEM((QROWS, w_query.shape[0]), jnp.bfloat16),
            pltpu.SemaphoreType.DMA((4,)),
        ],
        compiler_params=PARAMS,
        name="project_in",
    )(
        lengths,
        norm_gain,
        frequency[:, None],
        *[in_hbm(x) for x in (hidden_in, w_key.T, w_value.T, w_query.T)],
    )
    q_all = [q_t] + [
        lax.ppermute(q_t, "seq", [(i, i ^ k) for i in range(32)]) for k in range(1, COLS)
    ]


    def later(x, d):
        return lax.ppermute(
            x, "seq", [(i, i + COLS * d) for i in range(COLS * (ZDIM - d))]
        )

    scalars = (lengths, groups)
    qs, acc, top = pl.pallas_call(
        prefix_body,
        out_shape=(
            shape_of(TILES, 128, BLK),
            jax.ShapeDtypeStruct((TILES, 96, BLK), jnp.float32),
            jax.ShapeDtypeStruct((TILES, 1, BLK), jnp.float32),
        ),
        in_specs=[SMEM_SPEC] * 2 + [VMEM_SPEC] * (1 + COLS),
        out_specs=(VMEM_SPEC,) * 3,
        scratch_shapes=[
            pltpu.VMEM((ZDIM * BLK, 128), jnp.bfloat16),
            pltpu.VMEM((ZDIM, 96, BLK), jnp.bfloat16),
        ],
        compiler_params=PARAMS,
        cost_estimate=pl.CostEstimate(
            flops=8 * 10**9, transcendentals=8 * 10**6, bytes_accessed=4 * 10**6
        ),
        name="attend_prefix",
    )(*scalars, pre, *q_all)
    suf_late, top = lax.optimization_barrier((suf_own, top))
    suf = [suf_own] + [
        later(suf_own if d < SOON else suf_late, d) for d in range(1, SPAN)
    ]
    halves = TILES // 2
    half_scratch = [
        pltpu.VMEM((halves, 96, BLK), jnp.float32),
        pltpu.VMEM((halves, 1, BLK), jnp.float32),
    ]

    def half_specs(at):
        return [
            pl.BlockSpec((halves, 128, BLK), lambda i: (at, 0, 0)),
            pl.BlockSpec((halves, 96, BLK), lambda i: (at, 0, 0)),
            pl.BlockSpec((halves, 1, BLK), lambda i: (at, 0, 0)),
        ]

    core_pairs = [(i, i ^ 1) for i in range(32)]
    keep_far, send_far, keys, values = pl.pallas_call(
        far_body,
        grid=(1,),
        out_shape=(
            shape_of(PROWS, BLK),
            shape_of(PROWS, BLK),
            shape_of(SPAN * BLK, 128),
            shape_of(SPAN, 96, BLK),
        ),
        in_specs=[SMEM_SPEC] * 2 + [VMEM_SPEC] * SPAN + half_specs(1),
        out_specs=(VMEM_SPEC,) * 4,
        scratch_shapes=half_scratch,
        compiler_params=PARAMS,
        cost_estimate=pl.CostEstimate(
            flops=5 * 10**9, transcendentals=5 * 10**6, bytes_accessed=4 * 10**6
        ),
        name="attend_far",
    )(*scalars, *suf, qs, acc, top)

    def merge_two(one, two):
        return pl.pallas_call(
            merge_far_body,
            out_shape=shape_of(PROWS, BLK),
            in_specs=[VMEM_SPEC] * 2,
            out_specs=VMEM_SPEC,
            compiler_params=PARAMS,
            name="merge_two",
        )(one, two)

    far = merge_two(keep_far, lax.ppermute(send_far, "seq", core_pairs))
    far, values = lax.optimization_barrier((far, values))
    x_recv = lax.ppermute(far, "seq", [(i, i ^ 2) for i in range(32)])
    keep_near, send_near = pl.pallas_call(
        near_body,
        grid=(1,),
        out_shape=(shape_of(PROWS, BLK), shape_of(PROWS, BLK)),
        in_specs=[SMEM_SPEC] * 2 + [VMEM_SPEC] * 2 + half_specs(0),
        out_specs=(VMEM_SPEC, VMEM_SPEC),
        scratch_shapes=half_scratch,
        compiler_params=PARAMS,
        cost_estimate=pl.CostEstimate(
            flops=5 * 10**9, transcendentals=5 * 10**6, bytes_accessed=4 * 10**6
        ),
        name="attend_near",
    )(*scalars, keys, values, qs, acc, top)
    core_recv = lax.ppermute(send_near, "seq", core_pairs)
    width = w_out.shape[1]
    projected = pl.pallas_call(
        project_out_body,
        out_shape=shape_of(width, BLK),
        in_specs=[VMEM_SPEC] * 3,
        out_specs=VMEM_SPEC,
        compiler_params=PARAMS,
        name="project_out",
    )(merge_two(keep_near, x_recv), core_recv, w_out)
    tp = lax.axis_size("tp")
    columns = width // tp
    parts = lax.all_to_all(
        projected.reshape(tp, columns, BLK), "tp", split_axis=0, concat_axis=0, tiled=True
    )
    residual = lax.dynamic_slice_in_dim(
        hidden_in, lax.axis_index("tp") * columns, columns, 1
    ).T
    hidden_t = pl.pallas_call(
        final_body,
        out_shape=shape_of(columns, BLK),
        in_specs=[VMEM_SPEC] * 2,
        out_specs=VMEM_SPEC,
        compiler_params=PARAMS,
        name="final_sum",
    )(parts, residual)
    return (hidden_t.T, key_t.T, value_t.T)


def solution(mesh):
    return jax.shard_map(
        per_device,
        mesh=mesh,
        in_specs=(
            P("seq", None),
            P(),
            P(None, "tp"),
            P(None, "tp"),
            P(None, "tp"),
            P("tp", None),
            P("seq", "tp"),
            P("seq", "tp"),
            P(),
            P(),
        ),
        out_specs=(P("seq", "tp"), P("seq", "tp"), P("seq", "tp")),
        check_vma=False,
    )
```

```python
import jax
import jax.numpy as jnp
from jax import lax
from jax.experimental import pallas as pl
from jax.experimental.pallas import tpu as pltpu
from jax.sharding import PartitionSpec as P

HEAD_DIM = 80
GROUPS = 2
REQS = 4
BLK = 256
PRE_LEN = 4096
COLS = 4
ZDIM = 8
HPD = 4
QROWS = HPD * HEAD_DIM
PROWS = QROWS + 16
NEG = -1e30
LIMIT = 1e30
FLOOR = 1e-20
AHEAD = 4
TILES = COLS * HPD
HALF = ZDIM // GROUPS
SPAN = 6 + 1


def request_ends(lens):
    ends = []
    total = 0
    for i in range(REQS):
        total = total + lens[i]
        ends.append(total)
    return ends


def start_of(p, ends):
    st = jnp.int32(0)
    for i in range(REQS - 1):
        st = jnp.where(p >= ends[i], ends[i], st)
    return st


def token_vectors(z, r, ends, grps):
    tvecs, svecs, gvecs = [], [], []
    for k in range(COLS):
        tok0 = (z * COLS + (r ^ k)) * BLK
        tvec = tok0 + lax.broadcasted_iota(jnp.int32, (1, BLK), 1)
        svec = jnp.zeros((1, BLK), jnp.int32)
        gvec = jnp.zeros((1, BLK), jnp.int32) + grps[0]
        for i in range(REQS - 1):
            svec = jnp.where(tvec >= ends[i], ends[i], svec)
            gvec = jnp.where(tvec >= ends[i], grps[i + 1], gvec)
        tvecs.append(tvec)
        svecs.append(svec)
        gvecs.append(gvec)
    return tvecs, svecs, gvecs


def place(keys, values, n, kscr, vscr):
    kt = jnp.concatenate([keys, jnp.zeros((128 - HEAD_DIM, BLK), jnp.bfloat16)], axis=0)
    kscr[n * BLK : (n + 1) * BLK, :] = kt.T
    vscr[n, 0:HEAD_DIM, :] = values
    vscr[n, HEAD_DIM:96, :] = jnp.ones((96 - HEAD_DIM, BLK), jnp.bfloat16)


def key_rows(kscr, blk):
    return kscr[pl.ds(pl.multiple_of(blk * BLK, BLK), BLK), :]


def add_block(blks, masks, tiles, kscr, vscr, qs, acc, m):
    count = len(tiles)
    scores, weights = {}, {}
    for i in range(count + AHEAD + 1):
        if i < count:
            t = tiles[i]
            scores[i] = jnp.dot(
                key_rows(kscr, blks[t // HPD]), qs[t], preferred_element_type=jnp.float32
            )
        j = i - AHEAD
        if 0 <= j < count:
            t = tiles[j]
            sc = scores.pop(j)
            if masks is not None:
                sc = jnp.where(masks[t // HPD], sc, NEG)
            weights[j] = jnp.exp(sc - m[t]).astype(jnp.bfloat16)
        n = j - 1
        if 0 <= n < count:
            t = tiles[n]
            acc[t] = acc[t] + jnp.dot(
                vscr[blks[t // HPD]], weights.pop(n), preferred_element_type=jnp.float32
            )


def add_block_exact(tile, blk, mask, kscr, vscr, qs, acc, m):
    sc = jnp.dot(key_rows(kscr, blk), qs[tile], preferred_element_type=jnp.float32)
    sc = jnp.where(mask, sc, NEG)
    m_old = m[tile]
    m_new = jnp.maximum(m_old, jnp.max(sc, axis=0, keepdims=True))
    w = jnp.exp(sc - m_new).astype(jnp.bfloat16)
    acc[tile] = acc[tile] * jnp.exp(m_old - m_new) + jnp.dot(
        vscr[blk], w, preferred_element_type=jnp.float32
    )
    m[tile] = m_new


def out_of_range(acc):
    top = acc[0, HEAD_DIM : HEAD_DIM + 1, :]
    least = top
    for t in range(1, acc.shape[0]):
        row = acc[t, HEAD_DIM : HEAD_DIM + 1, :]
        top = jnp.maximum(top, row)
        least = jnp.minimum(least, row)
    return jnp.logical_not((jnp.max(top) < LIMIT) & (jnp.min(least) > FLOOR))


def suffix_low(z, r, ends):
    first = start_of(z * COLS * BLK, ends)
    gap = jnp.maximum(first - (BLK - 1) - r * BLK, 0)
    return jnp.minimum((gap + COLS * BLK - 1) // (COLS * BLK), z)


def suffix_full(jz, z, r, ends):
    last = start_of((z + 1) * COLS * BLK - 1, ends)
    return (jz < z) & (last <= (jz * COLS + r) * BLK)


def suffix_mask(jz, r, tvec, svec):
    kvec = (jz * COLS + r) * BLK + lax.broadcasted_iota(jnp.int32, (BLK, BLK), 0)
    return (kvec <= tvec) & (kvec >= svec)


def groups_seen(lo, hi, ends, grps):
    seen = [jnp.bool_(False) for g in range(GROUPS)]
    begin = jnp.int32(0)
    for i in range(REQS):
        inside = (begin < hi) & (ends[i] > lo)
        for g in range(GROUPS):
            seen[g] = seen[g] | (inside & (grps[i] == g))
        begin = ends[i]
    return seen


def prefix_body(lens, grps, pre, q_0, q_1, q_2, q_3, qs, acc, m, kscr, vscr):
    s = lax.axis_index("seq")
    z = s // COLS
    r = s % COLS
    ends = request_ends(lens)
    gvecs = token_vectors(z, r, ends, grps)[2]
    tiles = list(range(TILES))
    for k, ref in enumerate((q_0, q_1, q_2, q_3)):
        for h in range(HPD):
            lo = h * HEAD_DIM
            qs[k * HPD + h, 0:HEAD_DIM, :] = ref[lo : lo + HEAD_DIM, :]
            qs[k * HPD + h, HEAD_DIM:128, :] = jnp.zeros((128 - HEAD_DIM, BLK), jnp.bfloat16)
    here = groups_seen(z * COLS * BLK, (z + 1) * COLS * BLK, ends, grps)
    for g in range(GROUPS):

        @pl.when(here[g])
        def _():
            for c in range(HALF):
                n = g * HALF + c
                place(pre[n, 0:HEAD_DIM, :], pre[n, HEAD_DIM : 2 * HEAD_DIM, :], n, kscr, vscr)

    group, both = [], []
    for k in range(COLS):
        tok0 = (z * COLS + (r ^ k)) * BLK
        seen = groups_seen(tok0, tok0 + BLK, ends, grps)
        group.append(jnp.where(seen[0], 0, 1))
        both.append(seen[0] & seen[1])
    any_both = both[0] | both[1] | both[2] | both[3]

    for t in range(TILES):
        sc = jnp.dot(
            key_rows(kscr, group[t // HPD] * HALF), qs[t], preferred_element_type=jnp.float32
        )
        m[t] = jnp.max(sc, axis=0, keepdims=True)
    acc[...] = jnp.zeros_like(acc)

    @pl.when(jnp.logical_not(any_both))
    def _():
        @pl.loop(0, HALF)
        def _(c):
            add_block([g * HALF + c for g in group], None, tiles, kscr, vscr, qs, acc, m)

    @pl.when(any_both)
    def _():
        @pl.loop(0, HALF)
        def _(c):
            masks = [jnp.broadcast_to(gvecs[k] == group[k], (BLK, BLK)) for k in range(COLS)]
            add_block([g * HALF + c for g in group], masks, tiles, kscr, vscr, qs, acc, m)

    for k in range(COLS):

        @pl.when(both[k])
        def _():
            @pl.loop(0, HALF)
            def _(c):
                masks = [jnp.broadcast_to(gvecs[k] == 1, (BLK, BLK))] * COLS
                part = tiles[k * HPD : (k + 1) * HPD]
                add_block([HALF + c] * COLS, masks, part, kscr, vscr, qs, acc, m)

    @pl.when(out_of_range(acc))
    def _():
        acc[...] = jnp.zeros_like(acc)
        m[...] = jnp.full(m.shape, NEG, jnp.float32)
        for k in range(COLS):
            for g in range(GROUPS):

                @pl.when((group[k] == g) | both[k])
                def _():
                    mask = jnp.broadcast_to(gvecs[k] == g, (BLK, BLK))

                    @pl.loop(0, HALF)
                    def _(c):
                        @pl.loop(0, HPD)
                        def _(h):
                            add_block_exact(
                                k * HPD + h, g * HALF + c, mask, kscr, vscr, qs, acc, m
                            )


def write_partial(dst, acc, m, k):
    rows = lax.broadcasted_iota(jnp.int32, (16, BLK), 0)
    extra = jnp.zeros((16, BLK), jnp.float32)
    for h in range(HPD):
        t = k * HPD + h
        total_w = acc[t, HEAD_DIM : HEAD_DIM + 1, :]
        dst[h * HEAD_DIM : (h + 1) * HEAD_DIM, :] = (
            acc[t, 0:HEAD_DIM, :] * (1.0 / total_w)
        ).astype(jnp.bfloat16)
        lse = m[t] + jnp.log(total_w)
        for j in range(3):
            part = lse.astype(jnp.bfloat16).astype(jnp.float32)
            extra = jnp.where(rows == 3 * h + j, part, extra)
            lse = lse - part
    dst[QROWS:PROWS, :] = extra.astype(jnp.bfloat16)


def suffix_tiles(k0, lens, grps, qs, acc_in, m_in, keep, send, kscr, vscr, acc, m):
    s = lax.axis_index("seq")
    z = s // COLS
    r = s % COLS
    ends = request_ends(lens)
    tvecs, svecs, unused = token_vectors(z, r, ends, grps)
    end = z - suffix_low(z, r, ends) + 1
    tiles = list(range(2 * HPD))
    acc[...] = acc_in[...]
    m[...] = m_in[...]

    def step(d, c):
        jz = z - d
        full = suffix_full(jz, z, r, ends)

        @pl.when(full)
        def _():
            add_block([d] * 2, None, tiles, kscr, vscr, qs, acc, m)

        @pl.when(jnp.logical_not(full))
        def _():
            masks = [suffix_mask(jz, r, tvecs[k0 + k], svecs[k0 + k]) for k in range(2)]
            add_block([d] * 2, masks, tiles, kscr, vscr, qs, acc, m)

        return c

    lax.fori_loop(0, end, step, 0)

    @pl.when(out_of_range(acc))
    def _():
        acc[...] = acc_in[...]
        m[...] = m_in[...]
        for k in range(2):

            def exact_step(d, c):
                mask = suffix_mask(z - d, r, tvecs[k0 + k], svecs[k0 + k])

                @pl.loop(0, HPD)
                def _(h):
                    add_block_exact(k * HPD + h, d, mask, kscr, vscr, qs, acc, m)

                return c

            lax.fori_loop(0, end, exact_step, 0)

    write_partial(keep, acc, m, 0)
    write_partial(send, acc, m, 1)


def far_body(lens, grps, *refs):
    suf = refs[:SPAN]
    qs, acc_in, m_in, keep, send, kscr, vscr, acc, m = refs[SPAN:]
    for n in range(SPAN):
        place(suf[n][0:HEAD_DIM, :], suf[n][HEAD_DIM : 2 * HEAD_DIM, :], n, kscr, vscr)
    suffix_tiles(2, lens, grps, qs, acc_in, m_in, keep, send, kscr, vscr, acc, m)


def near_body(lens, grps, kscr, vscr, qs, acc_in, m_in, keep, send, acc, m):
    suffix_tiles(0, lens, grps, qs, acc_in, m_in, keep, send, kscr, vscr, acc, m)


def spread_body(keys, values, out, stage, sem, slot_sem):
    loads = [
        pltpu.make_async_copy(keys, stage.at[pl.ds(0, HEAD_DIM)], sem.at[0]),
        pltpu.make_async_copy(values, stage.at[pl.ds(HEAD_DIM, HEAD_DIM)], sem.at[1]),
    ]
    slots = [pltpu.make_async_copy(stage, out.at[n], slot_sem.at[n]) for n in range(ZDIM)]
    for copy in loads:
        copy.start()
    for copy in loads:
        copy.wait()
    for copy in slots:
        copy.start()
    for copy in slots:
        copy.wait()


def project_body(
    lens,
    gain,
    freq,
    hidden_far,
    wk_far,
    wv_far,
    wq_far,
    q_out,
    kv_out,
    k_out,
    v_out,
    hidden,
    wk,
    wv,
    wq,
    sem,
):
    moves = (
        (hidden_far, hidden),
        (wk_far, wk),
        (wv_far, wv),
        (wq_far, wq),
    )
    fetches = [
        pltpu.make_async_copy(src, dst, sem.at[n]) for n, (src, dst) in enumerate(moves)
    ]
    for fetch in fetches:
        fetch.start()
    ends = request_ends(lens)
    tvec = lax.axis_index("seq") * BLK + lax.broadcasted_iota(jnp.int32, (1, BLK), 1)
    svec = jnp.zeros((1, BLK), jnp.int32)
    for i in range(REQS - 1):
        svec = jnp.where(tvec >= ends[i], ends[i], svec)
    positions = (PRE_LEN + tvec - svec).astype(jnp.float32)
    angles = freq[...] * positions
    c = jnp.cos(angles)
    sn = jnp.sin(angles)
    fetches[0].wait()
    wide = hidden[...].astype(jnp.float32)
    mean_square = jnp.mean(wide * wide, axis=-1, keepdims=True)
    normed = (
        wide * lax.rsqrt(mean_square + 1e-05) * gain[...].reshape(1, wide.shape[1])
    ).astype(jnp.bfloat16)

    def proj(w):
        return lax.dot_general(
            w[...], normed, (((1,), (1,)), ((), ())), preferred_element_type=jnp.float32
        )

    hf = HEAD_DIM // 2

    def rotate(a, b):
        return a * c - b * sn, b * c + a * sn

    fetches[1].wait()
    kf = proj(wk)
    ka, kb = rotate(kf[0:hf], kf[hf:HEAD_DIM])
    kt = jnp.concatenate([ka, kb], axis=0).astype(jnp.bfloat16)
    fetches[2].wait()
    vt = proj(wv).astype(jnp.bfloat16)
    k_out[...] = kt
    v_out[...] = vt
    kv_out[0:HEAD_DIM, :] = kt
    kv_out[HEAD_DIM : 2 * HEAD_DIM, :] = vt
    fetches[3].wait()
    qf = proj(wq)
    for h in range(HPD):
        lo = h * HEAD_DIM
        qa, qb = rotate(qf[lo : lo + hf], qf[lo + hf : lo + HEAD_DIM])
        q_out[lo : lo + HEAD_DIM, :] = (
            jnp.concatenate([qa, qb], axis=0) * HEAD_DIM ** (-0.5)
        ).astype(jnp.bfloat16)


def merged(*parts):
    tails = [p[QROWS:PROWS, :].astype(jnp.float32) for p in parts]
    outs, lses = [], []
    for h in range(HPD):
        ls = [
            t[3 * h : 3 * h + 1] + t[3 * h + 1 : 3 * h + 2] + t[3 * h + 2 : 3 * h + 3]
            for t in tails
        ]
        top = ls[0]
        for x in ls[1:]:
            top = jnp.maximum(top, x)
        ws = [jnp.exp(x - top) for x in ls]
        tot = ws[0]
        for x in ws[1:]:
            tot = tot + x
        rows = slice(h * HEAD_DIM, (h + 1) * HEAD_DIM)
        out = parts[0][rows, :].astype(jnp.float32) * (ws[0] / tot)
        for p, w in zip(parts[1:], ws[1:]):
            out = out + p[rows, :].astype(jnp.float32) * (w / tot)
        outs.append(out.astype(jnp.bfloat16))
        lses.append(top + jnp.log(tot))
    return outs, lses


def merge_far_body(keep, recv, dst):
    outs, lses = merged(keep[...], recv[...])
    extra = jnp.zeros((16, BLK), jnp.float32)
    rows = lax.broadcasted_iota(jnp.int32, (16, BLK), 0)
    for h in range(HPD):
        lse = lses[h]
        for j in range(3):
            part = lse.astype(jnp.bfloat16).astype(jnp.float32)
            extra = jnp.where(rows == 3 * h + j, part, extra)
            lse = lse - part
    dst[...] = jnp.concatenate(outs + [extra.astype(jnp.bfloat16)], axis=0)


def project_out_body(own, near, w, out):
    outs, unused = merged(own[...], near[...])
    attended = jnp.concatenate(outs, axis=0)
    out[...] = lax.dot_general(
        w[...], attended, (((0,), (0,)), ((), ())), preferred_element_type=jnp.float32
    ).astype(jnp.bfloat16)


def final_body(parts, residual, out):
    total = residual[...].astype(jnp.float32)
    acc = parts[0].astype(jnp.float32)
    for i in range(1, parts.shape[0]):
        acc = acc + parts[i].astype(jnp.float32)
    out[...] = (acc + total).astype(jnp.bfloat16)


def shape_of(*dims):
    return jax.ShapeDtypeStruct(dims, jnp.bfloat16)


VMEM_SPEC = pl.BlockSpec(memory_space=pltpu.VMEM)
HBM_SPEC = pl.BlockSpec(memory_space=pltpu.HBM)
SMEM_SPEC = pl.BlockSpec(memory_space=pltpu.SMEM)
PARAMS = pltpu.CompilerParams(vmem_limit_bytes=20 * 1024 * 1024)


def in_hbm(x):
    return pltpu.with_memory_space_constraint(x, pltpu.HBM)


def per_device(
    hidden_in,
    norm_gain,
    w_query,
    w_key,
    w_value,
    w_out,
    prefix_keys,
    prefix_values,
    lengths,
    groups,
):
    columns_of_z = [list(range(c, ZDIM * COLS, COLS)) for c in range(COLS)]

    def along_z(x):
        return lax.all_to_all(
            x, "seq", split_axis=0, concat_axis=0, tiled=True, axis_index_groups=columns_of_z
        )

    pre = along_z(
        pl.pallas_call(
            spread_body,
            out_shape=shape_of(ZDIM, 2 * HEAD_DIM, BLK),
            in_specs=[HBM_SPEC] * 2,
            out_specs=HBM_SPEC,
            scratch_shapes=[
                pltpu.VMEM((2 * HEAD_DIM, BLK), jnp.bfloat16),
                pltpu.SemaphoreType.DMA((2,)),
                pltpu.SemaphoreType.DMA((ZDIM,)),
            ],
            compiler_params=PARAMS,
            name="spread_prefix",
        )(in_hbm(prefix_keys.T), in_hbm(prefix_values.T))
    )

    half_dim = HEAD_DIM // 2
    frequency = jnp.power(
        jnp.float32(1000000.0), -jnp.arange(half_dim, dtype=jnp.float32) / half_dim
    )
    q_t, suf_own, key_t, value_t = pl.pallas_call(
        project_body,
        out_shape=(
            shape_of(QROWS, BLK),
            shape_of(2 * HEAD_DIM, BLK),
            shape_of(HEAD_DIM, BLK),
            shape_of(HEAD_DIM, BLK),
        ),
        in_specs=[SMEM_SPEC] + [VMEM_SPEC] * 2 + [HBM_SPEC] * 4,
        out_specs=(VMEM_SPEC,) * 4,
        scratch_shapes=[
            pltpu.VMEM(hidden_in.shape, jnp.bfloat16),
            pltpu.VMEM((HEAD_DIM, w_query.shape[0]), jnp.bfloat16),
            pltpu.VMEM((HEAD_DIM, w_query.shape[0]), jnp.bfloat16),
            pltpu.VMEM((QROWS, w_query.shape[0]), jnp.bfloat16),
            pltpu.SemaphoreType.DMA((4,)),
        ],
        compiler_params=PARAMS,
        name="project_in",
    )(
        lengths,
        norm_gain,
        frequency[:, None],
        *[in_hbm(x) for x in (hidden_in, w_key.T, w_value.T, w_query.T)],
    )
    q_all = [q_t] + [
        lax.ppermute(q_t, "seq", [(i, i ^ k) for i in range(32)]) for k in range(1, COLS)
    ]


    def later(x, d, first=0):
        return lax.ppermute(
            x, "seq", [(i, i + COLS * d) for i in range(COLS * first, COLS * (ZDIM - d))]
        )

    scalars = (lengths, groups)
    qs, acc, top = pl.pallas_call(
        prefix_body,
        out_shape=(
            shape_of(TILES, 128, BLK),
            jax.ShapeDtypeStruct((TILES, 96, BLK), jnp.float32),
            jax.ShapeDtypeStruct((TILES, 1, BLK), jnp.float32),
        ),
        in_specs=[SMEM_SPEC] * 2 + [VMEM_SPEC] * (1 + COLS),
        out_specs=(VMEM_SPEC,) * 3,
        scratch_shapes=[
            pltpu.VMEM((ZDIM * BLK, 128), jnp.bfloat16),
            pltpu.VMEM((ZDIM, 96, BLK), jnp.bfloat16),
        ],
        compiler_params=PARAMS,
        cost_estimate=pl.CostEstimate(
            flops=8 * 10**9, transcendentals=8 * 10**6, bytes_accessed=4 * 10**6
        ),
        name="attend_prefix",
    )(*scalars, pre, *q_all)
    suf = [suf_own] + [later(suf_own, d) for d in (1, 2, 3)]
    suf_6 = later(suf_own, 6)
    two_back, three_back, top = lax.optimization_barrier((suf[2], suf[3], top))
    suf += [later(two_back, 2, 2), later(three_back, 2, 3), suf_6]
    halves = TILES // 2
    half_scratch = [
        pltpu.VMEM((halves, 96, BLK), jnp.float32),
        pltpu.VMEM((halves, 1, BLK), jnp.float32),
    ]

    def half_specs(at):
        return [
            pl.BlockSpec((halves, 128, BLK), lambda i: (at, 0, 0)),
            pl.BlockSpec((halves, 96, BLK), lambda i: (at, 0, 0)),
            pl.BlockSpec((halves, 1, BLK), lambda i: (at, 0, 0)),
        ]

    core_pairs = [(i, i ^ 1) for i in range(32)]
    keep_far, send_far, keys, values = pl.pallas_call(
        far_body,
        grid=(1,),
        out_shape=(
            shape_of(PROWS, BLK),
            shape_of(PROWS, BLK),
            shape_of(SPAN * BLK, 128),
            shape_of(SPAN, 96, BLK),
        ),
        in_specs=[SMEM_SPEC] * 2 + [VMEM_SPEC] * SPAN + half_specs(1),
        out_specs=(VMEM_SPEC,) * 4,
        scratch_shapes=half_scratch,
        compiler_params=PARAMS,
        cost_estimate=pl.CostEstimate(
            flops=5 * 10**9, transcendentals=5 * 10**6, bytes_accessed=4 * 10**6
        ),
        name="attend_far",
    )(*scalars, *suf, qs, acc, top)

    def merge_two(one, two):
        return pl.pallas_call(
            merge_far_body,
            out_shape=shape_of(PROWS, BLK),
            in_specs=[VMEM_SPEC] * 2,
            out_specs=VMEM_SPEC,
            compiler_params=PARAMS,
            name="merge_two",
        )(one, two)

    far = merge_two(keep_far, lax.ppermute(send_far, "seq", core_pairs))
    far, values = lax.optimization_barrier((far, values))
    x_recv = lax.ppermute(far, "seq", [(i, i ^ 2) for i in range(32)])
    keep_near, send_near = pl.pallas_call(
        near_body,
        grid=(1,),
        out_shape=(shape_of(PROWS, BLK), shape_of(PROWS, BLK)),
        in_specs=[SMEM_SPEC] * 2 + [VMEM_SPEC] * 2 + half_specs(0),
        out_specs=(VMEM_SPEC, VMEM_SPEC),
        scratch_shapes=half_scratch,
        compiler_params=PARAMS,
        cost_estimate=pl.CostEstimate(
            flops=5 * 10**9, transcendentals=5 * 10**6, bytes_accessed=4 * 10**6
        ),
        name="attend_near",
    )(*scalars, keys, values, qs, acc, top)
    core_recv = lax.ppermute(send_near, "seq", core_pairs)
    width = w_out.shape[1]
    projected = pl.pallas_call(
        project_out_body,
        out_shape=shape_of(width, BLK),
        in_specs=[VMEM_SPEC] * 3,
        out_specs=VMEM_SPEC,
        compiler_params=PARAMS,
        name="project_out",
    )(merge_two(keep_near, x_recv), core_recv, w_out)
    tp = lax.axis_size("tp")
    columns = width // tp
    parts = lax.all_to_all(
        projected.reshape(tp, columns, BLK), "tp", split_axis=0, concat_axis=0, tiled=True
    )
    residual = lax.dynamic_slice_in_dim(
        hidden_in, lax.axis_index("tp") * columns, columns, 1
    ).T
    hidden_t = pl.pallas_call(
        final_body,
        out_shape=shape_of(columns, BLK),
        in_specs=[VMEM_SPEC] * 2,
        out_specs=VMEM_SPEC,
        compiler_params=PARAMS,
        name="final_sum",
    )(parts, residual)
    return (hidden_t.T, key_t.T, value_t.T)


def solution(mesh):
    return jax.shard_map(
        per_device,
        mesh=mesh,
        in_specs=(
            P("seq", None),
            P(),
            P(None, "tp"),
            P(None, "tp"),
            P(None, "tp"),
            P("tp", None),
            P("seq", "tp"),
            P("seq", "tp"),
            P(),
            P(),
        ),
        out_specs=(P("seq", "tp"), P("seq", "tp"), P("seq", "tp")),
        check_vma=False,
    )
```

```python
import jax
import jax.numpy as jnp
from jax import lax
from jax.experimental import pallas as pl
from jax.experimental.pallas import tpu as pltpu
from jax.sharding import PartitionSpec as P

HEAD_DIM = 80
GROUPS = 2
REQS = 4
BLK = 256
PRE_LEN = 4096
COLS = 4
ZDIM = 8
HPD = 4
QROWS = HPD * HEAD_DIM
PROWS = QROWS + 16
NEG = -1e30
LIMIT = 1e30
FLOOR = 1e-20
AHEAD = 4
TILES = COLS * HPD
HALF = ZDIM // GROUPS
SPAN = 6 + 1
SOON = 4


def request_ends(lens):
    ends = []
    total = 0
    for i in range(REQS):
        total = total + lens[i]
        ends.append(total)
    return ends


def start_of(p, ends):
    st = jnp.int32(0)
    for i in range(REQS - 1):
        st = jnp.where(p >= ends[i], ends[i], st)
    return st


def token_vectors(z, r, ends, grps):
    tvecs, svecs, gvecs = [], [], []
    for k in range(COLS):
        tok0 = (z * COLS + (r ^ k)) * BLK
        tvec = tok0 + lax.broadcasted_iota(jnp.int32, (1, BLK), 1)
        svec = jnp.zeros((1, BLK), jnp.int32)
        gvec = jnp.zeros((1, BLK), jnp.int32) + grps[0]
        for i in range(REQS - 1):
            svec = jnp.where(tvec >= ends[i], ends[i], svec)
            gvec = jnp.where(tvec >= ends[i], grps[i + 1], gvec)
        tvecs.append(tvec)
        svecs.append(svec)
        gvecs.append(gvec)
    return tvecs, svecs, gvecs


def place(keys, values, n, kscr, vscr):
    kt = jnp.concatenate([keys, jnp.zeros((128 - HEAD_DIM, BLK), jnp.bfloat16)], axis=0)
    kscr[n * BLK : (n + 1) * BLK, :] = kt.T
    vscr[n, 0:HEAD_DIM, :] = values
    vscr[n, HEAD_DIM:96, :] = jnp.ones((96 - HEAD_DIM, BLK), jnp.bfloat16)


def key_rows(kscr, blk):
    return kscr[pl.ds(pl.multiple_of(blk * BLK, BLK), BLK), :]


def add_block(blks, masks, tiles, kscr, vscr, qs, acc, m):
    count = len(tiles)
    scores, weights = {}, {}
    for i in range(count + AHEAD + 1):
        if i < count:
            t = tiles[i]
            scores[i] = jnp.dot(
                key_rows(kscr, blks[t // HPD]), qs[t], preferred_element_type=jnp.float32
            )
        j = i - AHEAD
        if 0 <= j < count:
            t = tiles[j]
            sc = scores.pop(j)
            if masks is not None:
                sc = jnp.where(masks[t // HPD], sc, NEG)
            weights[j] = jnp.exp(sc - m[t]).astype(jnp.bfloat16)
        n = j - 1
        if 0 <= n < count:
            t = tiles[n]
            acc[t] = acc[t] + jnp.dot(
                vscr[blks[t // HPD]], weights.pop(n), preferred_element_type=jnp.float32
            )


def add_block_exact(tile, blk, mask, kscr, vscr, qs, acc, m):
    sc = jnp.dot(key_rows(kscr, blk), qs[tile], preferred_element_type=jnp.float32)
    sc = jnp.where(mask, sc, NEG)
    m_old = m[tile]
    m_new = jnp.maximum(m_old, jnp.max(sc, axis=0, keepdims=True))
    w = jnp.exp(sc - m_new).astype(jnp.bfloat16)
    acc[tile] = acc[tile] * jnp.exp(m_old - m_new) + jnp.dot(
        vscr[blk], w, preferred_element_type=jnp.float32
    )
    m[tile] = m_new


def out_of_range(acc):
    top = acc[0, HEAD_DIM : HEAD_DIM + 1, :]
    least = top
    for t in range(1, acc.shape[0]):
        row = acc[t, HEAD_DIM : HEAD_DIM + 1, :]
        top = jnp.maximum(top, row)
        least = jnp.minimum(least, row)
    return jnp.logical_not((jnp.max(top) < LIMIT) & (jnp.min(least) > FLOOR))


def suffix_low(z, r, ends):
    first = start_of(z * COLS * BLK, ends)
    gap = jnp.maximum(first - (BLK - 1) - r * BLK, 0)
    return jnp.minimum((gap + COLS * BLK - 1) // (COLS * BLK), z)


def suffix_full(jz, z, r, ends):
    last = start_of((z + 1) * COLS * BLK - 1, ends)
    return (jz < z) & (last <= (jz * COLS + r) * BLK)


def suffix_mask(jz, r, tvec, svec):
    kvec = (jz * COLS + r) * BLK + lax.broadcasted_iota(jnp.int32, (BLK, BLK), 0)
    return (kvec <= tvec) & (kvec >= svec)


def groups_seen(lo, hi, ends, grps):
    seen = [jnp.bool_(False) for g in range(GROUPS)]
    begin = jnp.int32(0)
    for i in range(REQS):
        inside = (begin < hi) & (ends[i] > lo)
        for g in range(GROUPS):
            seen[g] = seen[g] | (inside & (grps[i] == g))
        begin = ends[i]
    return seen


def prefix_body(lens, grps, pre, q_0, q_1, q_2, q_3, qs, acc, m, kscr, vscr):
    s = lax.axis_index("seq")
    z = s // COLS
    r = s % COLS
    ends = request_ends(lens)
    gvecs = token_vectors(z, r, ends, grps)[2]
    tiles = list(range(TILES))
    for k, ref in enumerate((q_0, q_1, q_2, q_3)):
        for h in range(HPD):
            lo = h * HEAD_DIM
            qs[k * HPD + h, 0:HEAD_DIM, :] = ref[lo : lo + HEAD_DIM, :]
            qs[k * HPD + h, HEAD_DIM:128, :] = jnp.zeros((128 - HEAD_DIM, BLK), jnp.bfloat16)
    here = groups_seen(z * COLS * BLK, (z + 1) * COLS * BLK, ends, grps)
    for g in range(GROUPS):

        @pl.when(here[g])
        def _():
            for c in range(HALF):
                n = g * HALF + c
                place(pre[n, 0:HEAD_DIM, :], pre[n, HEAD_DIM : 2 * HEAD_DIM, :], n, kscr, vscr)

    group, both = [], []
    for k in range(COLS):
        tok0 = (z * COLS + (r ^ k)) * BLK
        seen = groups_seen(tok0, tok0 + BLK, ends, grps)
        group.append(jnp.where(seen[0], 0, 1))
        both.append(seen[0] & seen[1])
    any_both = both[0] | both[1] | both[2] | both[3]

    for t in range(TILES):
        sc = jnp.dot(
            key_rows(kscr, group[t // HPD] * HALF), qs[t], preferred_element_type=jnp.float32
        )
        m[t] = jnp.max(sc, axis=0, keepdims=True)
    acc[...] = jnp.zeros_like(acc)

    @pl.when(jnp.logical_not(any_both))
    def _():
        @pl.loop(0, HALF)
        def _(c):
            add_block([g * HALF + c for g in group], None, tiles, kscr, vscr, qs, acc, m)

    @pl.when(any_both)
    def _():
        @pl.loop(0, HALF)
        def _(c):
            masks = [jnp.broadcast_to(gvecs[k] == group[k], (BLK, BLK)) for k in range(COLS)]
            add_block([g * HALF + c for g in group], masks, tiles, kscr, vscr, qs, acc, m)

    for k in range(COLS):

        @pl.when(both[k])
        def _():
            @pl.loop(0, HALF)
            def _(c):
                masks = [jnp.broadcast_to(gvecs[k] == 1, (BLK, BLK))] * COLS
                part = tiles[k * HPD : (k + 1) * HPD]
                add_block([HALF + c] * COLS, masks, part, kscr, vscr, qs, acc, m)

    @pl.when(out_of_range(acc))
    def _():
        acc[...] = jnp.zeros_like(acc)
        m[...] = jnp.full(m.shape, NEG, jnp.float32)
        for k in range(COLS):
            for g in range(GROUPS):

                @pl.when((group[k] == g) | both[k])
                def _():
                    mask = jnp.broadcast_to(gvecs[k] == g, (BLK, BLK))

                    @pl.loop(0, HALF)
                    def _(c):
                        @pl.loop(0, HPD)
                        def _(h):
                            add_block_exact(
                                k * HPD + h, g * HALF + c, mask, kscr, vscr, qs, acc, m
                            )


def write_partial(dst, acc, m, k):
    rows = lax.broadcasted_iota(jnp.int32, (16, BLK), 0)
    extra = jnp.zeros((16, BLK), jnp.float32)
    for h in range(HPD):
        t = k * HPD + h
        total_w = acc[t, HEAD_DIM : HEAD_DIM + 1, :]
        dst[h * HEAD_DIM : (h + 1) * HEAD_DIM, :] = (
            acc[t, 0:HEAD_DIM, :] * (1.0 / total_w)
        ).astype(jnp.bfloat16)
        lse = m[t] + jnp.log(total_w)
        for j in range(3):
            part = lse.astype(jnp.bfloat16).astype(jnp.float32)
            extra = jnp.where(rows == 3 * h + j, part, extra)
            lse = lse - part
    dst[QROWS:PROWS, :] = extra.astype(jnp.bfloat16)


def add_suffix(k0, d0, d1, lens, grps, qs, acc_in, m_in, kscr, vscr, acc, m):
    s = lax.axis_index("seq")
    z = s // COLS
    r = s % COLS
    ends = request_ends(lens)
    tvecs, svecs, unused = token_vectors(z, r, ends, grps)
    end = jnp.minimum(z - suffix_low(z, r, ends) + 1, d1)
    count = acc.shape[0] // HPD
    tiles = list(range(count * HPD))
    acc[...] = acc_in[...]
    m[...] = m_in[...]

    def step(d, c):
        jz = z - d
        full = suffix_full(jz, z, r, ends)

        @pl.when(full)
        def _():
            add_block([d - d0] * count, None, tiles, kscr, vscr, qs, acc, m)

        @pl.when(jnp.logical_not(full))
        def _():
            masks = [suffix_mask(jz, r, tvecs[k0 + k], svecs[k0 + k]) for k in range(count)]
            add_block([d - d0] * count, masks, tiles, kscr, vscr, qs, acc, m)

        return c

    lax.fori_loop(d0, end, step, 0)

    @pl.when(out_of_range(acc))
    def _():
        acc[...] = acc_in[...]
        m[...] = m_in[...]
        for k in range(count):

            def exact_step(d, c):
                mask = suffix_mask(z - d, r, tvecs[k0 + k], svecs[k0 + k])

                @pl.loop(0, HPD)
                def _(h):
                    add_block_exact(k * HPD + h, d - d0, mask, kscr, vscr, qs, acc, m)

                return c

            lax.fori_loop(d0, end, exact_step, 0)


def soon_body(lens, grps, *refs):
    suf = refs[:SOON]
    qs, acc_in, m_in, acc, m, kscr, vscr = refs[SOON:]
    for n in range(SOON):
        place(suf[n][0:HEAD_DIM, :], suf[n][HEAD_DIM : 2 * HEAD_DIM, :], n, kscr, vscr)
    add_suffix(0, 0, SOON, lens, grps, qs, acc_in, m_in, kscr, vscr, acc, m)


def far_body(lens, grps, *refs):
    late = refs[: SPAN - SOON]
    qs, acc_in, m_in, keep, send, kscr, vscr, acc, m = refs[SPAN - SOON :]
    for n in range(SPAN - SOON):
        place(late[n][0:HEAD_DIM, :], late[n][HEAD_DIM : 2 * HEAD_DIM, :], n, kscr, vscr)
    add_suffix(2, SOON, SPAN, lens, grps, qs, acc_in, m_in, kscr, vscr, acc, m)
    write_partial(keep, acc, m, 0)
    write_partial(send, acc, m, 1)


def near_body(lens, grps, kscr, vscr, qs, acc_in, m_in, keep, send, acc, m):
    add_suffix(0, SOON, SPAN, lens, grps, qs, acc_in, m_in, kscr, vscr, acc, m)
    write_partial(keep, acc, m, 0)
    write_partial(send, acc, m, 1)


def spread_body(keys, values, out, stage, sem, slot_sem):
    loads = [
        pltpu.make_async_copy(keys, stage.at[pl.ds(0, HEAD_DIM)], sem.at[0]),
        pltpu.make_async_copy(values, stage.at[pl.ds(HEAD_DIM, HEAD_DIM)], sem.at[1]),
    ]
    slots = [pltpu.make_async_copy(stage, out.at[n], slot_sem.at[n]) for n in range(ZDIM)]
    for copy in loads:
        copy.start()
    for copy in loads:
        copy.wait()
    for copy in slots:
        copy.start()
    for copy in slots:
        copy.wait()


def project_body(
    lens,
    gain,
    freq,
    hidden_far,
    wk_far,
    wv_far,
    wq_far,
    q_out,
    kv_out,
    k_out,
    v_out,
    hidden,
    wk,
    wv,
    wq,
    sem,
):
    moves = (
        (hidden_far, hidden),
        (wk_far, wk),
        (wv_far, wv),
        (wq_far, wq),
    )
    fetches = [
        pltpu.make_async_copy(src, dst, sem.at[n]) for n, (src, dst) in enumerate(moves)
    ]
    for fetch in fetches:
        fetch.start()
    ends = request_ends(lens)
    tvec = lax.axis_index("seq") * BLK + lax.broadcasted_iota(jnp.int32, (1, BLK), 1)
    svec = jnp.zeros((1, BLK), jnp.int32)
    for i in range(REQS - 1):
        svec = jnp.where(tvec >= ends[i], ends[i], svec)
    positions = (PRE_LEN + tvec - svec).astype(jnp.float32)
    angles = freq[...] * positions
    c = jnp.cos(angles)
    sn = jnp.sin(angles)
    fetches[0].wait()
    wide = hidden[...].astype(jnp.float32)
    mean_square = jnp.mean(wide * wide, axis=-1, keepdims=True)
    normed = (
        wide * lax.rsqrt(mean_square + 1e-05) * gain[...].reshape(1, wide.shape[1])
    ).astype(jnp.bfloat16)

    def proj(w):
        return lax.dot_general(
            w[...], normed, (((1,), (1,)), ((), ())), preferred_element_type=jnp.float32
        )

    hf = HEAD_DIM // 2

    def rotate(a, b):
        return a * c - b * sn, b * c + a * sn

    fetches[1].wait()
    kf = proj(wk)
    ka, kb = rotate(kf[0:hf], kf[hf:HEAD_DIM])
    kt = jnp.concatenate([ka, kb], axis=0).astype(jnp.bfloat16)
    fetches[2].wait()
    vt = proj(wv).astype(jnp.bfloat16)
    k_out[...] = kt
    v_out[...] = vt
    kv_out[0:HEAD_DIM, :] = kt
    kv_out[HEAD_DIM : 2 * HEAD_DIM, :] = vt
    fetches[3].wait()
    qf = proj(wq)
    for h in range(HPD):
        lo = h * HEAD_DIM
        qa, qb = rotate(qf[lo : lo + hf], qf[lo + hf : lo + HEAD_DIM])
        q_out[lo : lo + HEAD_DIM, :] = (
            jnp.concatenate([qa, qb], axis=0) * HEAD_DIM ** (-0.5)
        ).astype(jnp.bfloat16)


def merged(*parts):
    tails = [p[QROWS:PROWS, :].astype(jnp.float32) for p in parts]
    outs, lses = [], []
    for h in range(HPD):
        ls = [
            t[3 * h : 3 * h + 1] + t[3 * h + 1 : 3 * h + 2] + t[3 * h + 2 : 3 * h + 3]
            for t in tails
        ]
        top = ls[0]
        for x in ls[1:]:
            top = jnp.maximum(top, x)
        ws = [jnp.exp(x - top) for x in ls]
        tot = ws[0]
        for x in ws[1:]:
            tot = tot + x
        rows = slice(h * HEAD_DIM, (h + 1) * HEAD_DIM)
        out = parts[0][rows, :].astype(jnp.float32) * (ws[0] / tot)
        for p, w in zip(parts[1:], ws[1:]):
            out = out + p[rows, :].astype(jnp.float32) * (w / tot)
        outs.append(out.astype(jnp.bfloat16))
        lses.append(top + jnp.log(tot))
    return outs, lses


def merge_far_body(keep, recv, dst):
    outs, lses = merged(keep[...], recv[...])
    extra = jnp.zeros((16, BLK), jnp.float32)
    rows = lax.broadcasted_iota(jnp.int32, (16, BLK), 0)
    for h in range(HPD):
        lse = lses[h]
        for j in range(3):
            part = lse.astype(jnp.bfloat16).astype(jnp.float32)
            extra = jnp.where(rows == 3 * h + j, part, extra)
            lse = lse - part
    dst[...] = jnp.concatenate(outs + [extra.astype(jnp.bfloat16)], axis=0)


def project_out_body(own, near, w, out):
    outs, unused = merged(own[...], near[...])
    attended = jnp.concatenate(outs, axis=0)
    out[...] = lax.dot_general(
        w[...], attended, (((0,), (0,)), ((), ())), preferred_element_type=jnp.float32
    ).astype(jnp.bfloat16)


def final_body(parts, residual, out):
    total = residual[...].astype(jnp.float32)
    acc = parts[0].astype(jnp.float32)
    for i in range(1, parts.shape[0]):
        acc = acc + parts[i].astype(jnp.float32)
    out[...] = (acc + total).astype(jnp.bfloat16)


def shape_of(*dims):
    return jax.ShapeDtypeStruct(dims, jnp.bfloat16)


VMEM_SPEC = pl.BlockSpec(memory_space=pltpu.VMEM)
HBM_SPEC = pl.BlockSpec(memory_space=pltpu.HBM)
SMEM_SPEC = pl.BlockSpec(memory_space=pltpu.SMEM)
PARAMS = pltpu.CompilerParams(vmem_limit_bytes=20 * 1024 * 1024)


def in_hbm(x):
    return pltpu.with_memory_space_constraint(x, pltpu.HBM)


def per_device(
    hidden_in,
    norm_gain,
    w_query,
    w_key,
    w_value,
    w_out,
    prefix_keys,
    prefix_values,
    lengths,
    groups,
):
    columns_of_z = [list(range(c, ZDIM * COLS, COLS)) for c in range(COLS)]

    def along_z(x):
        return lax.all_to_all(
            x, "seq", split_axis=0, concat_axis=0, tiled=True, axis_index_groups=columns_of_z
        )

    pre = along_z(
        pl.pallas_call(
            spread_body,
            out_shape=shape_of(ZDIM, 2 * HEAD_DIM, BLK),
            in_specs=[HBM_SPEC] * 2,
            out_specs=HBM_SPEC,
            scratch_shapes=[
                pltpu.VMEM((2 * HEAD_DIM, BLK), jnp.bfloat16),
                pltpu.SemaphoreType.DMA((2,)),
                pltpu.SemaphoreType.DMA((ZDIM,)),
            ],
            compiler_params=PARAMS,
            name="spread_prefix",
        )(in_hbm(prefix_keys.T), in_hbm(prefix_values.T))
    )

    half_dim = HEAD_DIM // 2
    frequency = jnp.power(
        jnp.float32(1000000.0), -jnp.arange(half_dim, dtype=jnp.float32) / half_dim
    )
    q_t, suf_own, key_t, value_t = pl.pallas_call(
        project_body,
        out_shape=(
            shape_of(QROWS, BLK),
            shape_of(2 * HEAD_DIM, BLK),
            shape_of(HEAD_DIM, BLK),
            shape_of(HEAD_DIM, BLK),
        ),
        in_specs=[SMEM_SPEC] + [VMEM_SPEC] * 2 + [HBM_SPEC] * 4,
        out_specs=(VMEM_SPEC,) * 4,
        scratch_shapes=[
            pltpu.VMEM(hidden_in.shape, jnp.bfloat16),
            pltpu.VMEM((HEAD_DIM, w_query.shape[0]), jnp.bfloat16),
            pltpu.VMEM((HEAD_DIM, w_query.shape[0]), jnp.bfloat16),
            pltpu.VMEM((QROWS, w_query.shape[0]), jnp.bfloat16),
            pltpu.SemaphoreType.DMA((4,)),
        ],
        compiler_params=PARAMS,
        name="project_in",
    )(
        lengths,
        norm_gain,
        frequency[:, None],
        *[in_hbm(x) for x in (hidden_in, w_key.T, w_value.T, w_query.T)],
    )
    q_all = [q_t] + [
        lax.ppermute(q_t, "seq", [(i, i ^ k) for i in range(32)]) for k in range(1, COLS)
    ]


    def later(x, d, first=0):
        return lax.ppermute(
            x, "seq", [(i, i + COLS * d) for i in range(COLS * first, COLS * (ZDIM - d))]
        )

    scalars = (lengths, groups)
    qs, acc, top = pl.pallas_call(
        prefix_body,
        out_shape=(
            shape_of(TILES, 128, BLK),
            jax.ShapeDtypeStruct((TILES, 96, BLK), jnp.float32),
            jax.ShapeDtypeStruct((TILES, 1, BLK), jnp.float32),
        ),
        in_specs=[SMEM_SPEC] * 2 + [VMEM_SPEC] * (1 + COLS),
        out_specs=(VMEM_SPEC,) * 3,
        scratch_shapes=[
            pltpu.VMEM((ZDIM * BLK, 128), jnp.bfloat16),
            pltpu.VMEM((ZDIM, 96, BLK), jnp.bfloat16),
        ],
        compiler_params=PARAMS,
        cost_estimate=pl.CostEstimate(
            flops=8 * 10**9, transcendentals=8 * 10**6, bytes_accessed=4 * 10**6
        ),
        name="attend_prefix",
    )(*scalars, pre, *q_all)
    suf = [suf_own] + [later(suf_own, d) for d in (1, 2, 3)]
    suf_6 = later(suf_own, 6)
    two_back, three_back, top = lax.optimization_barrier((suf[2], suf[3], top))
    suf += [later(two_back, 2, 2), later(three_back, 2, 3), suf_6]
    acc, top = pl.pallas_call(
        soon_body,
        out_shape=(
            jax.ShapeDtypeStruct((TILES, 96, BLK), jnp.float32),
            jax.ShapeDtypeStruct((TILES, 1, BLK), jnp.float32),
        ),
        in_specs=[SMEM_SPEC] * 2 + [VMEM_SPEC] * (SOON + 3),
        out_specs=(VMEM_SPEC, VMEM_SPEC),
        scratch_shapes=[
            pltpu.VMEM((SOON * BLK, 128), jnp.bfloat16),
            pltpu.VMEM((SOON, 96, BLK), jnp.bfloat16),
        ],
        compiler_params=PARAMS,
        cost_estimate=pl.CostEstimate(
            flops=5 * 10**9, transcendentals=5 * 10**6, bytes_accessed=4 * 10**6
        ),
        name="attend_soon",
    )(*scalars, *suf[:SOON], qs, acc, top)
    halves = TILES // 2
    half_scratch = [
        pltpu.VMEM((halves, 96, BLK), jnp.float32),
        pltpu.VMEM((halves, 1, BLK), jnp.float32),
    ]

    def half_specs(at):
        return [
            pl.BlockSpec((halves, 128, BLK), lambda i: (at, 0, 0)),
            pl.BlockSpec((halves, 96, BLK), lambda i: (at, 0, 0)),
            pl.BlockSpec((halves, 1, BLK), lambda i: (at, 0, 0)),
        ]

    core_pairs = [(i, i ^ 1) for i in range(32)]
    keep_far, send_far, keys, values = pl.pallas_call(
        far_body,
        grid=(1,),
        out_shape=(
            shape_of(PROWS, BLK),
            shape_of(PROWS, BLK),
            shape_of((SPAN - SOON) * BLK, 128),
            shape_of(SPAN - SOON, 96, BLK),
        ),
        in_specs=[SMEM_SPEC] * 2 + [VMEM_SPEC] * (SPAN - SOON) + half_specs(1),
        out_specs=(VMEM_SPEC,) * 4,
        scratch_shapes=half_scratch,
        compiler_params=PARAMS,
        cost_estimate=pl.CostEstimate(
            flops=5 * 10**9, transcendentals=5 * 10**6, bytes_accessed=4 * 10**6
        ),
        name="attend_far",
    )(*scalars, *suf[SOON:], qs, acc, top)

    def merge_two(one, two):
        return pl.pallas_call(
            merge_far_body,
            out_shape=shape_of(PROWS, BLK),
            in_specs=[VMEM_SPEC] * 2,
            out_specs=VMEM_SPEC,
            compiler_params=PARAMS,
            name="merge_two",
        )(one, two)

    far = merge_two(keep_far, lax.ppermute(send_far, "seq", core_pairs))
    far, values = lax.optimization_barrier((far, values))
    x_recv = lax.ppermute(far, "seq", [(i, i ^ 2) for i in range(32)])
    keep_near, send_near = pl.pallas_call(
        near_body,
        grid=(1,),
        out_shape=(shape_of(PROWS, BLK), shape_of(PROWS, BLK)),
        in_specs=[SMEM_SPEC] * 2 + [VMEM_SPEC] * 2 + half_specs(0),
        out_specs=(VMEM_SPEC, VMEM_SPEC),
        scratch_shapes=half_scratch,
        compiler_params=PARAMS,
        cost_estimate=pl.CostEstimate(
            flops=5 * 10**9, transcendentals=5 * 10**6, bytes_accessed=4 * 10**6
        ),
        name="attend_near",
    )(*scalars, keys, values, qs, acc, top)
    core_recv = lax.ppermute(send_near, "seq", core_pairs)
    width = w_out.shape[1]
    projected = pl.pallas_call(
        project_out_body,
        out_shape=shape_of(width, BLK),
        in_specs=[VMEM_SPEC] * 3,
        out_specs=VMEM_SPEC,
        compiler_params=PARAMS,
        name="project_out",
    )(merge_two(keep_near, x_recv), core_recv, w_out)
    tp = lax.axis_size("tp")
    columns = width // tp
    parts = lax.all_to_all(
        projected.reshape(tp, columns, BLK), "tp", split_axis=0, concat_axis=0, tiled=True
    )
    residual = lax.dynamic_slice_in_dim(
        hidden_in, lax.axis_index("tp") * columns, columns, 1
    ).T
    hidden_t = pl.pallas_call(
        final_body,
        out_shape=shape_of(columns, BLK),
        in_specs=[VMEM_SPEC] * 2,
        out_specs=VMEM_SPEC,
        compiler_params=PARAMS,
        name="final_sum",
    )(parts, residual)
    return (hidden_t.T, key_t.T, value_t.T)


def solution(mesh):
    return jax.shard_map(
        per_device,
        mesh=mesh,
        in_specs=(
            P("seq", None),
            P(),
            P(None, "tp"),
            P(None, "tp"),
            P(None, "tp"),
            P("tp", None),
            P("seq", "tp"),
            P("seq", "tp"),
            P(),
            P(),
        ),
        out_specs=(P("seq", "tp"), P("seq", "tp"), P("seq", "tp")),
        check_vma=False,
    )
```

```python
import jax
import jax.numpy as jnp
from jax import lax
from jax.experimental import pallas as pl
from jax.experimental.pallas import tpu as pltpu
from jax.sharding import PartitionSpec as P

HEAD_DIM = 80
GROUPS = 2
REQS = 4
BLK = 256
PRE_LEN = 4096
COLS = 4
ZDIM = 8
HPD = 4
QROWS = HPD * HEAD_DIM
PROWS = QROWS + 16
NEG = -1e30
LIMIT = 1e30
FLOOR = 1e-20
AHEAD = 4
TILES = COLS * HPD
HALF = ZDIM // GROUPS
SPAN = 6 + 1
SOON = 4


def request_ends(lens):
    ends = []
    total = 0
    for i in range(REQS):
        total = total + lens[i]
        ends.append(total)
    return ends


def start_of(p, ends):
    st = jnp.int32(0)
    for i in range(REQS - 1):
        st = jnp.where(p >= ends[i], ends[i], st)
    return st


def token_vectors(z, r, ends, grps):
    tvecs, svecs, gvecs = [], [], []
    for k in range(COLS):
        tok0 = (z * COLS + (r ^ k)) * BLK
        tvec = tok0 + lax.broadcasted_iota(jnp.int32, (1, BLK), 1)
        svec = jnp.zeros((1, BLK), jnp.int32)
        gvec = jnp.zeros((1, BLK), jnp.int32) + grps[0]
        for i in range(REQS - 1):
            svec = jnp.where(tvec >= ends[i], ends[i], svec)
            gvec = jnp.where(tvec >= ends[i], grps[i + 1], gvec)
        tvecs.append(tvec)
        svecs.append(svec)
        gvecs.append(gvec)
    return tvecs, svecs, gvecs


def place(keys, values, n, kscr, vscr):
    kt = jnp.concatenate([keys, jnp.zeros((128 - HEAD_DIM, BLK), jnp.bfloat16)], axis=0)
    kscr[n * BLK : (n + 1) * BLK, :] = kt.T
    vscr[n, 0:HEAD_DIM, :] = values
    vscr[n, HEAD_DIM:96, :] = jnp.ones((96 - HEAD_DIM, BLK), jnp.bfloat16)


def key_rows(kscr, blk):
    return kscr[pl.ds(pl.multiple_of(blk * BLK, BLK), BLK), :]


def add_block(blks, masks, tiles, kscr, vscr, qs, acc, m):
    count = len(tiles)
    scores, weights = {}, {}
    for i in range(count + AHEAD + 1):
        if i < count:
            t = tiles[i]
            scores[i] = jnp.dot(
                key_rows(kscr, blks[t // HPD]), qs[t], preferred_element_type=jnp.float32
            )
        j = i - AHEAD
        if 0 <= j < count:
            t = tiles[j]
            sc = scores.pop(j)
            if masks is not None:
                sc = jnp.where(masks[t // HPD], sc, NEG)
            weights[j] = jnp.exp(sc - m[t]).astype(jnp.bfloat16)
        n = j - 1
        if 0 <= n < count:
            t = tiles[n]
            acc[t] = acc[t] + jnp.dot(
                vscr[blks[t // HPD]], weights.pop(n), preferred_element_type=jnp.float32
            )


def add_block_exact(tile, blk, mask, kscr, vscr, qs, acc, m):
    sc = jnp.dot(key_rows(kscr, blk), qs[tile], preferred_element_type=jnp.float32)
    sc = jnp.where(mask, sc, NEG)
    m_old = m[tile]
    m_new = jnp.maximum(m_old, jnp.max(sc, axis=0, keepdims=True))
    w = jnp.exp(sc - m_new).astype(jnp.bfloat16)
    acc[tile] = acc[tile] * jnp.exp(m_old - m_new) + jnp.dot(
        vscr[blk], w, preferred_element_type=jnp.float32
    )
    m[tile] = m_new


def out_of_range(acc):
    top = acc[0, HEAD_DIM : HEAD_DIM + 1, :]
    least = top
    for t in range(1, acc.shape[0]):
        row = acc[t, HEAD_DIM : HEAD_DIM + 1, :]
        top = jnp.maximum(top, row)
        least = jnp.minimum(least, row)
    return jnp.logical_not((jnp.max(top) < LIMIT) & (jnp.min(least) > FLOOR))


def suffix_low(z, r, ends):
    first = start_of(z * COLS * BLK, ends)
    gap = jnp.maximum(first - (BLK - 1) - r * BLK, 0)
    return jnp.minimum((gap + COLS * BLK - 1) // (COLS * BLK), z)


def suffix_full(jz, z, r, ends):
    last = start_of((z + 1) * COLS * BLK - 1, ends)
    return (jz < z) & (last <= (jz * COLS + r) * BLK)


def suffix_mask(jz, r, tvec, svec):
    kvec = (jz * COLS + r) * BLK + lax.broadcasted_iota(jnp.int32, (BLK, BLK), 0)
    return (kvec <= tvec) & (kvec >= svec)


def groups_seen(lo, hi, ends, grps):
    seen = [jnp.bool_(False) for g in range(GROUPS)]
    begin = jnp.int32(0)
    for i in range(REQS):
        inside = (begin < hi) & (ends[i] > lo)
        for g in range(GROUPS):
            seen[g] = seen[g] | (inside & (grps[i] == g))
        begin = ends[i]
    return seen


def prefix_body(lens, grps, pre, q_0, q_1, q_2, q_3, qs, acc, m, kscr, vscr):
    s = lax.axis_index("seq")
    z = s // COLS
    r = s % COLS
    ends = request_ends(lens)
    gvecs = token_vectors(z, r, ends, grps)[2]
    tiles = list(range(TILES))
    for k, ref in enumerate((q_0, q_1, q_2, q_3)):
        for h in range(HPD):
            lo = h * HEAD_DIM
            qs[k * HPD + h, 0:HEAD_DIM, :] = ref[lo : lo + HEAD_DIM, :]
            qs[k * HPD + h, HEAD_DIM:128, :] = jnp.zeros((128 - HEAD_DIM, BLK), jnp.bfloat16)
    here = groups_seen(z * COLS * BLK, (z + 1) * COLS * BLK, ends, grps)
    for g in range(GROUPS):

        @pl.when(here[g])
        def _():
            for c in range(HALF):
                n = g * HALF + c
                place(pre[n, 0:HEAD_DIM, :], pre[n, HEAD_DIM : 2 * HEAD_DIM, :], n, kscr, vscr)

    group, both = [], []
    for k in range(COLS):
        tok0 = (z * COLS + (r ^ k)) * BLK
        seen = groups_seen(tok0, tok0 + BLK, ends, grps)
        group.append(jnp.where(seen[0], 0, 1))
        both.append(seen[0] & seen[1])
    any_both = both[0] | both[1] | both[2] | both[3]

    for t in range(TILES):
        sc = jnp.dot(
            key_rows(kscr, group[t // HPD] * HALF), qs[t], preferred_element_type=jnp.float32
        )
        m[t] = jnp.max(sc, axis=0, keepdims=True)
    acc[...] = jnp.zeros_like(acc)

    @pl.when(jnp.logical_not(any_both))
    def _():
        @pl.loop(0, HALF)
        def _(c):
            add_block([g * HALF + c for g in group], None, tiles, kscr, vscr, qs, acc, m)

    @pl.when(any_both)
    def _():
        @pl.loop(0, HALF)
        def _(c):
            masks = [jnp.broadcast_to(gvecs[k] == group[k], (BLK, BLK)) for k in range(COLS)]
            add_block([g * HALF + c for g in group], masks, tiles, kscr, vscr, qs, acc, m)

    for k in range(COLS):

        @pl.when(both[k])
        def _():
            @pl.loop(0, HALF)
            def _(c):
                masks = [jnp.broadcast_to(gvecs[k] == 1, (BLK, BLK))] * COLS
                part = tiles[k * HPD : (k + 1) * HPD]
                add_block([HALF + c] * COLS, masks, part, kscr, vscr, qs, acc, m)

    @pl.when(out_of_range(acc))
    def _():
        acc[...] = jnp.zeros_like(acc)
        m[...] = jnp.full(m.shape, NEG, jnp.float32)
        for k in range(COLS):
            for g in range(GROUPS):

                @pl.when((group[k] == g) | both[k])
                def _():
                    mask = jnp.broadcast_to(gvecs[k] == g, (BLK, BLK))

                    @pl.loop(0, HALF)
                    def _(c):
                        @pl.loop(0, HPD)
                        def _(h):
                            add_block_exact(
                                k * HPD + h, g * HALF + c, mask, kscr, vscr, qs, acc, m
                            )


def write_partial(dst, acc, m, k):
    rows = lax.broadcasted_iota(jnp.int32, (16, BLK), 0)
    extra = jnp.zeros((16, BLK), jnp.float32)
    for h in range(HPD):
        t = k * HPD + h
        total_w = acc[t, HEAD_DIM : HEAD_DIM + 1, :]
        dst[h * HEAD_DIM : (h + 1) * HEAD_DIM, :] = (
            acc[t, 0:HEAD_DIM, :] * (1.0 / total_w)
        ).astype(jnp.bfloat16)
        lse = m[t] + jnp.log(total_w)
        for j in range(3):
            part = lse.astype(jnp.bfloat16).astype(jnp.float32)
            extra = jnp.where(rows == 3 * h + j, part, extra)
            lse = lse - part
    dst[QROWS:PROWS, :] = extra.astype(jnp.bfloat16)


def add_suffix(k0, d0, d1, lens, grps, qs, acc_in, m_in, kscr, vscr, acc, m):
    s = lax.axis_index("seq")
    z = s // COLS
    r = s % COLS
    ends = request_ends(lens)
    tvecs, svecs, unused = token_vectors(z, r, ends, grps)
    end = jnp.minimum(z - suffix_low(z, r, ends) + 1, d1)
    count = acc.shape[0] // HPD
    tiles = list(range(count * HPD))
    acc[...] = acc_in[...]
    m[...] = m_in[...]

    def step(d, c):
        jz = z - d
        full = suffix_full(jz, z, r, ends)

        @pl.when(full)
        def _():
            add_block([d - d0] * count, None, tiles, kscr, vscr, qs, acc, m)

        @pl.when(jnp.logical_not(full))
        def _():
            masks = [suffix_mask(jz, r, tvecs[k0 + k], svecs[k0 + k]) for k in range(count)]
            add_block([d - d0] * count, masks, tiles, kscr, vscr, qs, acc, m)

        return c

    lax.fori_loop(d0, end, step, 0)

    @pl.when(out_of_range(acc))
    def _():
        acc[...] = acc_in[...]
        m[...] = m_in[...]
        for k in range(count):

            def exact_step(d, c):
                mask = suffix_mask(z - d, r, tvecs[k0 + k], svecs[k0 + k])

                @pl.loop(0, HPD)
                def _(h):
                    add_block_exact(k * HPD + h, d - d0, mask, kscr, vscr, qs, acc, m)

                return c

            lax.fori_loop(d0, end, exact_step, 0)


def soon_body(lens, grps, *refs):
    suf = refs[:SOON]
    qs, acc_in, m_in, acc, m, kscr, vscr = refs[SOON:]
    for n in range(SOON):
        place(suf[n][0:HEAD_DIM, :], suf[n][HEAD_DIM : 2 * HEAD_DIM, :], n, kscr, vscr)
    add_suffix(0, 0, SOON, lens, grps, qs, acc_in, m_in, kscr, vscr, acc, m)


def far_body(lens, grps, *refs):
    late = refs[: SPAN - SOON]
    qs, acc_in, m_in, keep, send, kscr, vscr, acc, m = refs[SPAN - SOON :]
    for n in range(SPAN - SOON):
        place(late[n][0:HEAD_DIM, :], late[n][HEAD_DIM : 2 * HEAD_DIM, :], n, kscr, vscr)
    add_suffix(2, SOON, SPAN, lens, grps, qs, acc_in, m_in, kscr, vscr, acc, m)
    write_partial(keep, acc, m, 0)
    write_partial(send, acc, m, 1)


def near_body(lens, grps, kscr, vscr, qs, acc_in, m_in, keep, send, acc, m):
    add_suffix(0, SOON, SPAN, lens, grps, qs, acc_in, m_in, kscr, vscr, acc, m)
    write_partial(keep, acc, m, 0)
    write_partial(send, acc, m, 1)


def spread_body(keys, values, out, stage, sem, slot_sem):
    loads = [
        pltpu.make_async_copy(keys, stage.at[pl.ds(0, HEAD_DIM)], sem.at[0]),
        pltpu.make_async_copy(values, stage.at[pl.ds(HEAD_DIM, HEAD_DIM)], sem.at[1]),
    ]
    slots = [pltpu.make_async_copy(stage, out.at[n], slot_sem.at[n]) for n in range(ZDIM)]
    for copy in loads:
        copy.start()
    for copy in loads:
        copy.wait()
    for copy in slots:
        copy.start()
    for copy in slots:
        copy.wait()


def project_body(
    lens,
    gain,
    freq,
    hidden_far,
    wk_far,
    wv_far,
    wq_far,
    q_out,
    kv_out,
    k_out,
    v_out,
    hidden,
    w_all,
    sem,
):
    moves = (
        (hidden_far, hidden),
        (wk_far, w_all.at[pl.ds(0, HEAD_DIM)]),
        (wv_far, w_all.at[pl.ds(HEAD_DIM, HEAD_DIM)]),
        (wq_far, w_all.at[pl.ds(2 * HEAD_DIM, QROWS)]),
    )
    fetches = [
        pltpu.make_async_copy(src, dst, sem.at[n]) for n, (src, dst) in enumerate(moves)
    ]
    for fetch in fetches:
        fetch.start()
    ends = request_ends(lens)
    tvec = lax.axis_index("seq") * BLK + lax.broadcasted_iota(jnp.int32, (1, BLK), 1)
    svec = jnp.zeros((1, BLK), jnp.int32)
    for i in range(REQS - 1):
        svec = jnp.where(tvec >= ends[i], ends[i], svec)
    positions = (PRE_LEN + tvec - svec).astype(jnp.float32)
    angles = freq[...] * positions
    c = jnp.cos(angles)
    sn = jnp.sin(angles)
    fetches[0].wait()
    wide = hidden[...].astype(jnp.float32)
    mean_square = jnp.mean(wide * wide, axis=-1, keepdims=True)
    normed = (
        wide * lax.rsqrt(mean_square + 1e-05) * gain[...].reshape(1, wide.shape[1])
    ).astype(jnp.bfloat16)

    for fetch in fetches[1:]:
        fetch.wait()
    rows = lax.dot_general(
        w_all[...], normed, (((1,), (1,)), ((), ())), preferred_element_type=jnp.float32
    )
    hf = HEAD_DIM // 2

    def rotate(a, b):
        return a * c - b * sn, b * c + a * sn

    kf = rows[0:HEAD_DIM]
    ka, kb = rotate(kf[0:hf], kf[hf:HEAD_DIM])
    kt = jnp.concatenate([ka, kb], axis=0).astype(jnp.bfloat16)
    vt = rows[HEAD_DIM : 2 * HEAD_DIM].astype(jnp.bfloat16)
    k_out[...] = kt
    v_out[...] = vt
    kv_out[0:HEAD_DIM, :] = kt
    kv_out[HEAD_DIM : 2 * HEAD_DIM, :] = vt
    qf = rows[2 * HEAD_DIM :]
    for h in range(HPD):
        lo = h * HEAD_DIM
        qa, qb = rotate(qf[lo : lo + hf], qf[lo + hf : lo + HEAD_DIM])
        q_out[lo : lo + HEAD_DIM, :] = (
            jnp.concatenate([qa, qb], axis=0) * HEAD_DIM ** (-0.5)
        ).astype(jnp.bfloat16)


def merged(*parts):
    tails = [p[QROWS:PROWS, :].astype(jnp.float32) for p in parts]
    outs, lses = [], []
    for h in range(HPD):
        ls = [
            t[3 * h : 3 * h + 1] + t[3 * h + 1 : 3 * h + 2] + t[3 * h + 2 : 3 * h + 3]
            for t in tails
        ]
        top = ls[0]
        for x in ls[1:]:
            top = jnp.maximum(top, x)
        ws = [jnp.exp(x - top) for x in ls]
        tot = ws[0]
        for x in ws[1:]:
            tot = tot + x
        rows = slice(h * HEAD_DIM, (h + 1) * HEAD_DIM)
        out = parts[0][rows, :].astype(jnp.float32) * (ws[0] / tot)
        for p, w in zip(parts[1:], ws[1:]):
            out = out + p[rows, :].astype(jnp.float32) * (w / tot)
        outs.append(out.astype(jnp.bfloat16))
        lses.append(top + jnp.log(tot))
    return outs, lses


def merge_far_body(keep, recv, dst):
    outs, lses = merged(keep[...], recv[...])
    extra = jnp.zeros((16, BLK), jnp.float32)
    rows = lax.broadcasted_iota(jnp.int32, (16, BLK), 0)
    for h in range(HPD):
        lse = lses[h]
        for j in range(3):
            part = lse.astype(jnp.bfloat16).astype(jnp.float32)
            extra = jnp.where(rows == 3 * h + j, part, extra)
            lse = lse - part
    dst[...] = jnp.concatenate(outs + [extra.astype(jnp.bfloat16)], axis=0)


def project_out_body(own, near, w, out, stage, sem):
    outs, unused = merged(own[...], near[...])
    attended = jnp.concatenate(outs, axis=0)
    copies = []
    for n in range(w.shape[1] // BLK):
        rows = pl.ds(n * BLK, BLK)
        stage[rows, :] = lax.dot_general(
            w[:, rows], attended, (((0,), (0,)), ((), ())), preferred_element_type=jnp.float32
        ).astype(jnp.bfloat16)
        copies.append(pltpu.make_async_copy(stage.at[rows], out.at[rows], sem.at[n]))
        copies[-1].start()
    for copy in copies:
        copy.wait()


def final_body(parts, residual, out):
    total = residual[...].astype(jnp.float32)
    acc = parts[0].astype(jnp.float32)
    for i in range(1, parts.shape[0]):
        acc = acc + parts[i].astype(jnp.float32)
    out[...] = (acc + total).astype(jnp.bfloat16)


def shape_of(*dims):
    return jax.ShapeDtypeStruct(dims, jnp.bfloat16)


VMEM_SPEC = pl.BlockSpec(memory_space=pltpu.VMEM)
HBM_SPEC = pl.BlockSpec(memory_space=pltpu.HBM)
SMEM_SPEC = pl.BlockSpec(memory_space=pltpu.SMEM)
PARAMS = pltpu.CompilerParams(vmem_limit_bytes=20 * 1024 * 1024)


def in_hbm(x):
    return pltpu.with_memory_space_constraint(x, pltpu.HBM)


def per_device(
    hidden_in,
    norm_gain,
    w_query,
    w_key,
    w_value,
    w_out,
    prefix_keys,
    prefix_values,
    lengths,
    groups,
):
    columns_of_z = [list(range(c, ZDIM * COLS, COLS)) for c in range(COLS)]

    def along_z(x):
        return lax.all_to_all(
            x, "seq", split_axis=0, concat_axis=0, tiled=True, axis_index_groups=columns_of_z
        )

    pre = along_z(
        pl.pallas_call(
            spread_body,
            out_shape=shape_of(ZDIM, 2 * HEAD_DIM, BLK),
            in_specs=[HBM_SPEC] * 2,
            out_specs=HBM_SPEC,
            scratch_shapes=[
                pltpu.VMEM((2 * HEAD_DIM, BLK), jnp.bfloat16),
                pltpu.SemaphoreType.DMA((2,)),
                pltpu.SemaphoreType.DMA((ZDIM,)),
            ],
            compiler_params=PARAMS,
            name="spread_prefix",
        )(in_hbm(prefix_keys.T), in_hbm(prefix_values.T))
    )

    half_dim = HEAD_DIM // 2
    frequency = jnp.power(
        jnp.float32(1000000.0), -jnp.arange(half_dim, dtype=jnp.float32) / half_dim
    )
    q_t, suf_own, key_t, value_t = pl.pallas_call(
        project_body,
        out_shape=(
            shape_of(QROWS, BLK),
            shape_of(2 * HEAD_DIM, BLK),
            shape_of(HEAD_DIM, BLK),
            shape_of(HEAD_DIM, BLK),
        ),
        in_specs=[SMEM_SPEC] + [VMEM_SPEC] * 2 + [HBM_SPEC] * 4,
        out_specs=(VMEM_SPEC,) * 4,
        scratch_shapes=[
            pltpu.VMEM(hidden_in.shape, jnp.bfloat16),
            pltpu.VMEM((2 * HEAD_DIM + QROWS, w_query.shape[0]), jnp.bfloat16),
            pltpu.SemaphoreType.DMA((4,)),
        ],
        compiler_params=PARAMS,
        name="project_in",
    )(
        lengths,
        norm_gain,
        frequency[:, None],
        *[in_hbm(x) for x in (hidden_in, w_key.T, w_value.T, w_query.T)],
    )
    q_all = [q_t] + [
        lax.ppermute(q_t, "seq", [(i, i ^ k) for i in range(32)]) for k in range(1, COLS)
    ]


    def later(x, d, first=0):
        return lax.ppermute(
            x, "seq", [(i, i + COLS * d) for i in range(COLS * first, COLS * (ZDIM - d))]
        )

    scalars = (lengths, groups)
    qs, acc, top = pl.pallas_call(
        prefix_body,
        out_shape=(
            shape_of(TILES, 128, BLK),
            jax.ShapeDtypeStruct((TILES, 96, BLK), jnp.float32),
            jax.ShapeDtypeStruct((TILES, 1, BLK), jnp.float32),
        ),
        in_specs=[SMEM_SPEC] * 2 + [VMEM_SPEC] * (1 + COLS),
        out_specs=(VMEM_SPEC,) * 3,
        scratch_shapes=[
            pltpu.VMEM((ZDIM * BLK, 128), jnp.bfloat16),
            pltpu.VMEM((ZDIM, 96, BLK), jnp.bfloat16),
        ],
        compiler_params=PARAMS,
        cost_estimate=pl.CostEstimate(
            flops=8 * 10**9, transcendentals=8 * 10**6, bytes_accessed=4 * 10**6
        ),
        name="attend_prefix",
    )(*scalars, pre, *q_all)
    suf = [suf_own] + [later(suf_own, d) for d in (1, 2, 3)]
    suf_6 = later(suf_own, 6)
    two_back, three_back, top = lax.optimization_barrier((suf[2], suf[3], top))
    suf += [later(two_back, 2, 2), later(three_back, 2, 3), suf_6]
    acc, top = pl.pallas_call(
        soon_body,
        out_shape=(
            jax.ShapeDtypeStruct((TILES, 96, BLK), jnp.float32),
            jax.ShapeDtypeStruct((TILES, 1, BLK), jnp.float32),
        ),
        in_specs=[SMEM_SPEC] * 2 + [VMEM_SPEC] * (SOON + 3),
        out_specs=(VMEM_SPEC, VMEM_SPEC),
        scratch_shapes=[
            pltpu.VMEM((SOON * BLK, 128), jnp.bfloat16),
            pltpu.VMEM((SOON, 96, BLK), jnp.bfloat16),
        ],
        compiler_params=PARAMS,
        cost_estimate=pl.CostEstimate(
            flops=5 * 10**9, transcendentals=5 * 10**6, bytes_accessed=4 * 10**6
        ),
        name="attend_soon",
    )(*scalars, *suf[:SOON], qs, acc, top)
    halves = TILES // 2
    half_scratch = [
        pltpu.VMEM((halves, 96, BLK), jnp.float32),
        pltpu.VMEM((halves, 1, BLK), jnp.float32),
    ]

    def half_specs(at):
        return [
            pl.BlockSpec((halves, 128, BLK), lambda i: (at, 0, 0)),
            pl.BlockSpec((halves, 96, BLK), lambda i: (at, 0, 0)),
            pl.BlockSpec((halves, 1, BLK), lambda i: (at, 0, 0)),
        ]

    core_pairs = [(i, i ^ 1) for i in range(32)]
    keep_far, send_far, keys, values = pl.pallas_call(
        far_body,
        grid=(1,),
        out_shape=(
            shape_of(PROWS, BLK),
            shape_of(PROWS, BLK),
            shape_of((SPAN - SOON) * BLK, 128),
            shape_of(SPAN - SOON, 96, BLK),
        ),
        in_specs=[SMEM_SPEC] * 2 + [VMEM_SPEC] * (SPAN - SOON) + half_specs(1),
        out_specs=(VMEM_SPEC,) * 4,
        scratch_shapes=half_scratch,
        compiler_params=PARAMS,
        cost_estimate=pl.CostEstimate(
            flops=5 * 10**9, transcendentals=5 * 10**6, bytes_accessed=4 * 10**6
        ),
        name="attend_far",
    )(*scalars, *suf[SOON:], qs, acc, top)

    def merge_two(one, two):
        return pl.pallas_call(
            merge_far_body,
            out_shape=shape_of(PROWS, BLK),
            in_specs=[VMEM_SPEC] * 2,
            out_specs=VMEM_SPEC,
            compiler_params=PARAMS,
            name="merge_two",
        )(one, two)

    far = merge_two(keep_far, lax.ppermute(send_far, "seq", core_pairs))
    far, values = lax.optimization_barrier((far, values))
    x_recv = lax.ppermute(far, "seq", [(i, i ^ 2) for i in range(32)])
    keep_near, send_near = pl.pallas_call(
        near_body,
        grid=(1,),
        out_shape=(shape_of(PROWS, BLK), shape_of(PROWS, BLK)),
        in_specs=[SMEM_SPEC] * 2 + [VMEM_SPEC] * 2 + half_specs(0),
        out_specs=(VMEM_SPEC, VMEM_SPEC),
        scratch_shapes=half_scratch,
        compiler_params=PARAMS,
        cost_estimate=pl.CostEstimate(
            flops=5 * 10**9, transcendentals=5 * 10**6, bytes_accessed=4 * 10**6
        ),
        name="attend_near",
    )(*scalars, keys, values, qs, acc, top)
    core_recv = lax.ppermute(send_near, "seq", core_pairs)
    width = w_out.shape[1]
    projected = pl.pallas_call(
        project_out_body,
        out_shape=shape_of(width, BLK),
        in_specs=[VMEM_SPEC] * 3,
        out_specs=HBM_SPEC,
        scratch_shapes=[
            pltpu.VMEM((width, BLK), jnp.bfloat16),
            pltpu.SemaphoreType.DMA((width // BLK,)),
        ],
        compiler_params=PARAMS,
        name="project_out",
    )(merge_two(keep_near, x_recv), core_recv, w_out)
    tp = lax.axis_size("tp")
    columns = width // tp
    parts = lax.all_to_all(
        projected.reshape(tp, columns, BLK), "tp", split_axis=0, concat_axis=0, tiled=True
    )
    residual = lax.dynamic_slice_in_dim(
        hidden_in, lax.axis_index("tp") * columns, columns, 1
    ).T
    hidden_t = pl.pallas_call(
        final_body,
        out_shape=shape_of(columns, BLK),
        in_specs=[VMEM_SPEC] * 2,
        out_specs=VMEM_SPEC,
        compiler_params=PARAMS,
        name="final_sum",
    )(parts, residual)
    return (hidden_t.T, key_t.T, value_t.T)


def solution(mesh):
    return jax.shard_map(
        per_device,
        mesh=mesh,
        in_specs=(
            P("seq", None),
            P(),
            P(None, "tp"),
            P(None, "tp"),
            P(None, "tp"),
            P("tp", None),
            P("seq", "tp"),
            P("seq", "tp"),
            P(),
            P(),
        ),
        out_specs=(P("seq", "tp"), P("seq", "tp"), P("seq", "tp")),
        check_vma=False,
    )
```
